32 devices in a mesh: seq: 8 (over z, y), head: 4 (over x, core).
Axes of the slice: x: 2, y: 2, z: 4, core: 2. Of those that a mesh axis runs over, the one named last changes fastest.
Arguments:
- layer_input: bfloat16 [8192, 2048], P('seq'), may hold values from -6 to 6
- output_grad: bfloat16 [8192, 2048], P('seq'), may hold values from -6 to 6
- loss_mask: int32 [8192], P('seq'), may hold values 0 or 1
- proj_weight: bfloat16 [2048, 3, 2048], P(None, None, 'head'), may hold values from -0.125 to 0.125
- out_weight: bfloat16 [2048, 2048], P('head'), may hold values from -0.125 to 0.125
- norm_gain: bfloat16 [2048], P('head'), may hold values from 0.099609375 to 1.8984375
Outputs:
- input_grad: bfloat16 [8192, 2048], P(('seq', 'head'))
- proj_weight_grad: float32 [2048, 3, 2048], P('seq', None, 'head')
- out_weight_grad: float32 [2048, 2048], P('head', 'seq')
The draws below stay inside these ranges and needn't reach their ends.
All inputs are finite; a program needn't handle non-finite values. No bound on the sum of `loss_mask` on one device may be relied on, other than what follows from the above.
Results may differ from the reference program's by a relative error of at most 0.018.
Values may be sent and summed in bfloat16 or wider, within the bound.
No kernel may reach another device: no remote copies, remote signals or barrier semaphores. Data moves between devices by JAX's collectives and lax.ppermute only.
A program may use at most 128 MiB of HBM per device.

```python
import jax
import jax.numpy as jnp
from jax import lax

D = 2048
HEADS = 16
HD = 128
BLOCK = 1024
TOK_DEV = 1024
INNER = 2048
TOKENS = 8192


def with_ends(drawn, stream_key, low, largest):
    longest = drawn.shape.index(max(drawn.shape))
    spots = []
    for shift in (0, 1):
        where = [jax.random.randint(jax.random.fold_in(stream_key, axis), (), 0, length) for axis, length in enumerate(drawn.shape)]
        where[longest] = (where[longest] + shift) % drawn.shape[longest]
        spots.append(tuple(where))
    return drawn.at[spots[0]].set(low).at[spots[1]].set(largest)


def strengthened(values, key, source, target, blocks, factor):
    def block_of(position):
        return (jnp.arange(values.shape[position]) // (values.shape[position] // blocks)).reshape((-1,) + (1,) * (values.ndim - 1 - position))

    near = jax.random.permutation(key, blocks)[block_of(target)]
    other_side = (block_of(target) + blocks // 2) % blocks
    return jnp.where((block_of(source) == near) | (block_of(source) == other_side), factor * values, values)


def block_scale(rng, dims, cuts, smallest, high):
    def one(axis_at, parts):
        steps = jax.random.uniform(jax.random.fold_in(jax.random.fold_in(rng, 6), axis_at), (parts,), jnp.float32, smallest / len(cuts), high / len(cuts))
        return jnp.repeat(jnp.exp(steps), dims[axis_at] // parts).reshape((-1,) + (1,) * (len(dims) - axis_at - 1))

    factor_of = one(*cuts[0])
    for cut in cuts[1:]:
        factor_of = factor_of * one(*cut)
    return factor_of


def normal_values(rng, extent, deviation, limit, pieces=(), kind=jnp.bfloat16):
    level = block_scale(rng, extent, pieces, -0.22, 0.18) if pieces else 1.0
    values = jax.random.normal(rng, extent, jnp.float32) * deviation * level
    return jnp.minimum(jnp.maximum(values, -limit), limit).astype(kind)


def bell_draw_with(rng, extent, deviation, bound, pieces, heavy, kind=jnp.bfloat16):
    array = deviation * jax.random.normal(rng, extent, jnp.float32)
    if pieces:
        array = array * block_scale(rng, extent, pieces, -0.22, 0.18)
    return jnp.clip(strengthened(array, jax.random.fold_in(rng, 3), *heavy), -bound, bound).astype(kind)


def setup_inputs(seed: int = 0) -> dict:
    splits = jax.random.split(jax.random.key(seed), 7)
    layer_input = bell_draw_with(splits[0], (TOKENS, D), 1.0, 6.0, ((0, 8),), (0, 1, 8, 2.0))
    output_grad = normal_values(splits[1], (TOKENS, D), 1.0, 6.0, ((0, 8),))
    loss_mask = with_ends((jax.random.randint(splits[2], (TOKENS,), 0, 2) < 1).astype(jnp.int32), jax.random.fold_in(splits[2], 1), 0, 1)
    proj_weight = normal_values(splits[3], (D, 3, INNER), D ** -0.5, 0.125, ((2, 4),))
    out_weight = normal_values(splits[4], (INNER, D), INNER ** -0.5, 0.125, ((0, 4),))
    norm_gain = jnp.clip(1.0 + 0.18 * jax.random.normal(splits[5], (INNER,), jnp.float32), 0.099609375, 1.8984375).astype(jnp.bfloat16)
    return {"layer_input": layer_input, "output_grad": output_grad, "loss_mask": loss_mask, "proj_weight": proj_weight, "out_weight": out_weight, "norm_gain": norm_gain}


epsilon = 1e-06

def group_sum(left, right, width):
    groups = left.shape[0] // TOK_DEV

    def step(total, index):
        start = (index * TOK_DEV).astype(jnp.int32)
        left_rows = lax.dynamic_slice_in_dim(left, start, TOK_DEV, 0)
        right_rows = lax.dynamic_slice_in_dim(right, start, TOK_DEV, 0)
        part = jnp.dot(left_rows.T, right_rows, preferred_element_type=jnp.float32)
        part = lax.optimization_barrier(part.astype(jnp.bfloat16))
        return (total + part.astype(jnp.float32), None)
    init = jnp.zeros((left.shape[1], width), jnp.float32)
    total, unused = lax.scan(step, init, jnp.arange(groups, dtype=jnp.int32))
    return total

def reference(layer_input, output_grad, loss_mask, proj_weight, out_weight, norm_gain):
    count = layer_input.shape[0]
    blocks = count // BLOCK
    flat_weight = proj_weight.reshape(D, 3 * INNER)
    projected = jnp.dot(layer_input, flat_weight, preferred_element_type=jnp.float32).astype(jnp.bfloat16)
    projected = projected.reshape(count, 3, INNER)

    def heads(arr):
        return arr.reshape(blocks, BLOCK, HEADS, HD).astype(jnp.float32)
    query_rows = heads(projected[:, 0])
    key_rows = heads(projected[:, 1])
    value_rows = heads(projected[:, 2])
    block_state = jnp.einsum('nbhi,nbhj->nhij', key_rows, value_rows)
    state = lax.optimization_barrier(jnp.cumsum(block_state, 0).astype(jnp.bfloat16)).astype(jnp.float32)
    attended = jnp.einsum('nbhi,nhij->nbhj', query_rows, state)
    scale = lax.rsqrt(lax.optimization_barrier(jnp.mean(attended * attended, -1, keepdims=True)) + epsilon)
    gain = norm_gain.astype(jnp.float32).reshape(HEADS, HD)
    normed = (attended * scale * gain).astype(jnp.bfloat16).reshape(count, INNER)
    masked_grad = output_grad * loss_mask[:, None].astype(jnp.bfloat16)
    out_weight_grad = group_sum(normed, masked_grad, D)
    normed_grad = lax.dot_general(masked_grad, out_weight, (((1,), (1,)), ((), ())), preferred_element_type=jnp.float32)
    scaled = normed_grad.reshape(blocks, BLOCK, HEADS, HD) * gain
    inner_mean = lax.optimization_barrier(jnp.mean(scaled * attended, -1, keepdims=True))
    attended_grad = (scale * scaled - attended * scale ** 3 * inner_mean).astype(jnp.bfloat16)
    attended_grad = lax.optimization_barrier(attended_grad).astype(jnp.float32)
    block_grad = jnp.einsum('nbhi,nbhj->nhij', query_rows, attended_grad)
    suffix = jnp.flip(jnp.cumsum(jnp.flip(block_grad, 0), 0), 0)
    state_grad = lax.optimization_barrier(suffix.astype(jnp.bfloat16)).astype(jnp.float32)
    query_grad = jnp.einsum('nbhj,nhij->nbhi', attended_grad, state)
    key_grad = jnp.einsum('nbhj,nhij->nbhi', value_rows, state_grad)
    value_grad = jnp.einsum('nbhi,nhij->nbhj', key_rows, state_grad)
    projected_grad = jnp.stack([query_grad.reshape(count, INNER), key_grad.reshape(count, INNER), value_grad.reshape(count, INNER)], 1).astype(jnp.bfloat16)
    flat_grad = projected_grad.reshape(count, 3 * INNER)
    input_grad = lax.dot_general(flat_grad, flat_weight, (((1,), (1,)), ((), ())), preferred_element_type=jnp.float32).astype(jnp.bfloat16)
    proj_weight_grad = group_sum(layer_input, flat_grad, 3 * INNER).reshape(D, 3, INNER)
    return (input_grad, proj_weight_grad, out_weight_grad)
```

```python
import functools

import jax
import jax.numpy as jnp
from jax import lax
from jax.experimental import pallas as pl
from jax.experimental.pallas import tpu as pltpu
from jax.sharding import PartitionSpec as P

D = 2048
HD = 128
BLOCK = 1024
epsilon = 1e-06
f32 = jnp.float32
bf16 = jnp.bfloat16
VMEM_LIMIT = 48 * 1024 * 1024


def params():
    return pltpu.CompilerParams(vmem_limit_bytes=VMEM_LIMIT)


def dot(a, b):
    return lax.dot_general(a, b, (((1,), (0,)), ((), ())), preferred_element_type=f32)


def dot_t(a, b):
    return lax.dot_general(a, b, (((1,), (1,)), ((), ())), preferred_element_type=f32)


def exchange(arr, axis, bit):
    count = lax.axis_size(axis)
    return lax.ppermute(arr, axis, [(i, i ^ (1 << bit)) for i in range(count)])


def slot_order(stage_bits):
    order = [0]
    for bit in reversed(stage_bits):
        order = order + [slot | (1 << bit) for slot in order]
    return order


def state_kernel(key_ref, value_ref, state_ref, key_t_ref, value_t_ref):
    key_t = key_ref[...].T
    key_t_ref[...] = key_t
    value_t_ref[...] = value_ref[...].T
    state_ref[0] = dot(key_t, value_ref[...])


def block_states(keys, values):
    count, width = keys.shape
    heads = width // HD
    column = pl.BlockSpec((count, HD), lambda h: (0, h))
    row = pl.BlockSpec((HD, count), lambda h: (h, 0))
    return pl.pallas_call(
        state_kernel,
        grid=(heads,),
        in_specs=[column, column],
        out_specs=[pl.BlockSpec((1, HD, HD), lambda h: (h, 0, 0)), row, row],
        out_shape=[
            jax.ShapeDtypeStruct((heads, HD, HD), f32),
            jax.ShapeDtypeStruct((width, count), bf16),
            jax.ShapeDtypeStruct((width, count), bf16),
        ],
        compiler_params=params(),
        cost_estimate=pl.CostEstimate(
            flops=2 * count * width * HD, bytes_accessed=8 * count * width, transcendentals=0
        ),
        name="block_states",
    )(keys, values)


def terms_kernel(count_left, block_ref, *refs):
    left, right, out = refs[:count_left], refs[count_left], refs[count_left + 1]
    rows = left[0].shape[0]
    for index, ref in enumerate(left):
        out[0, index * rows : (index + 1) * rows, :] = dot(ref[...], right[...]).astype(bf16)


def gradient_terms(lefts, right, position, slots):
    rows, count = lefts[0].shape
    width = right.shape[1] // lax.axis_size("seq")
    total = rows * len(lefts)
    blocks = position ^ jnp.array(slots, jnp.int32)
    if width % 128:
        picked = jnp.take(right.reshape(count, -1, width), blocks, axis=1)
        left = jnp.concatenate(lefts, 0)
        return jnp.einsum("at,tnb->nab", left, picked, preferred_element_type=f32).astype(bf16)
    return pl.pallas_call(
        functools.partial(terms_kernel, len(lefts)),
        grid_spec=pltpu.PrefetchScalarGridSpec(
            num_scalar_prefetch=1,
            grid=(len(slots),),
            in_specs=[pl.BlockSpec((rows, count), lambda i, b: (0, 0)) for _ in lefts]
            + [pl.BlockSpec((count, width), lambda i, b: (0, b[i]))],
            out_specs=pl.BlockSpec((1, total, width), lambda i, b: (i, 0, 0)),
        ),
        out_shape=jax.ShapeDtypeStruct((len(slots), total, width), bf16),
        compiler_params=params(),
        cost_estimate=pl.CostEstimate(
            flops=2 * count * total * width * len(slots),
            bytes_accessed=2 * len(slots) * width * (count + total) + 2 * total * count,
            transcendentals=0,
        ),
        name="gradient_terms",
    )(blocks, *lefts, right)


def middle_kernel(query_ref, grad_ref, mask_ref, gain_ref, state_ref, normed_t_ref, query_grad_ref, query_grad_t_ref, block_grad_ref):
    query = query_ref[...]
    state = state_ref[0]
    mask = mask_ref[...]
    gain = gain_ref[...].astype(f32)
    attended = dot(query, state)
    scale = lax.rsqrt(jnp.mean(attended * attended, -1, keepdims=True) + epsilon)
    unit = attended * scale
    normed_t_ref[...] = (unit * gain * mask).astype(bf16).T
    scaled = grad_ref[...] * mask * gain
    inner = jnp.mean(scaled * attended, -1, keepdims=True)
    attended_grad = (scale * scaled - attended * (scale * scale * scale) * inner).astype(bf16)
    attended_grad_t = attended_grad.T
    block_grad_ref[0] = dot(attended_grad_t, query)
    query_grad_ref[...] = dot_t(attended_grad, state).astype(bf16)
    query_grad_t_ref[...] = dot(state, attended_grad_t).astype(bf16)


def middle(queries, normed_grad, mask, gain, state):
    count, width = queries.shape
    heads = width // HD
    column = pl.BlockSpec((count, HD), lambda h: (0, h))
    row = pl.BlockSpec((HD, count), lambda h: (h, 0))
    square = pl.BlockSpec((1, HD, HD), lambda h: (h, 0, 0))
    return pl.pallas_call(
        middle_kernel,
        grid=(heads,),
        in_specs=[
            column,
            column,
            pl.BlockSpec((count, 1), lambda h: (0, 0)),
            pl.BlockSpec((1, HD), lambda h: (0, h)),
            square,
        ],
        out_specs=[row, column, row, square],
        out_shape=[
            jax.ShapeDtypeStruct((width, count), bf16),
            jax.ShapeDtypeStruct((count, width), bf16),
            jax.ShapeDtypeStruct((width, count), bf16),
            jax.ShapeDtypeStruct((heads, HD, HD), f32),
        ],
        compiler_params=params(),
        cost_estimate=pl.CostEstimate(
            flops=8 * count * width * HD, bytes_accessed=12 * count * width, transcendentals=count
        ),
        name="norm_backward",
    )(queries, normed_grad, mask, gain, state)


def late_kernel(heads, mine_ref, other_ref, own_keep_ref, own_send_ref, got_keep_ref, got_send_ref, keep_ref, send_ref):
    width = heads * HD
    for own, got, out in ((own_keep_ref, got_keep_ref, keep_ref), (own_send_ref, got_send_ref, send_ref)):
        for h in range(heads):
            lo, hi = h * HD, (h + 1) * HD
            key = lax.dot_general(mine_ref[h], own[0, lo:hi, :], (((0,), (0,)), ((), ())), preferred_element_type=f32)
            key += lax.dot_general(other_ref[h], got[0, lo:hi, :], (((0,), (0,)), ((), ())), preferred_element_type=f32)
            out[0, lo:hi, :] = key.astype(bf16)
            value = dot(mine_ref[h], own[0, width + lo : width + hi, :])
            value += dot(other_ref[h], got[0, width + lo : width + hi, :])
            out[0, width + lo : width + hi, :] = value.astype(bf16)


def late_terms(mine, other, own, got):
    slots, total, width = own.shape
    heads = mine.shape[0]
    half = slots // 2
    square = pl.BlockSpec((heads, HD, HD), lambda i: (0, 0, 0))
    low = pl.BlockSpec((1, total, width), lambda i: (i, 0, 0))
    high = pl.BlockSpec((1, total, width), lambda i: (i + half, 0, 0))
    out = jax.ShapeDtypeStruct((half, total, width), bf16)
    return pl.pallas_call(
        functools.partial(late_kernel, heads),
        grid=(half,),
        in_specs=[square, square, low, high, low, high],
        out_specs=[low, low],
        out_shape=[out, out],
        compiler_params=params(),
        cost_estimate=pl.CostEstimate(
            flops=4 * slots * total * width * HD, bytes_accessed=6 * slots * total * width, transcendentals=0
        ),
        name="late_terms",
    )(mine, other, own, own, got, got)


def key_value_kernel(key_ref, value_ref, grad_ref, key_grad_ref, value_grad_ref):
    key_grad_ref[...] = dot(value_ref[...], grad_ref[0]).astype(bf16)
    value_grad_ref[...] = dot_t(key_ref[...], grad_ref[0]).astype(bf16)


def key_value_grads(keys, values, state_grad_t):
    count, width = keys.shape
    column = pl.BlockSpec((count, HD), lambda h: (0, h))
    out = jax.ShapeDtypeStruct((count, width), bf16)
    return pl.pallas_call(
        key_value_kernel,
        grid=(width // HD,),
        in_specs=[column, column, pl.BlockSpec((1, HD, HD), lambda h: (h, 0, 0))],
        out_specs=[column, column],
        out_shape=[out, out],
        compiler_params=params(),
        cost_estimate=pl.CostEstimate(
            flops=4 * count * width * HD, bytes_accessed=8 * count * width, transcendentals=0
        ),
        name="key_value_grads",
    )(keys, values, state_grad_t)


def halving(keep, send, axis, stage_bits):
    for bit in stage_bits:
        got = exchange(send, axis, bit)
        total = keep.astype(f32) + got.astype(f32)
        half = total.shape[0] // 2
        if half:
            keep, send = total[:half].astype(bf16), total[half:].astype(bf16)
    return total[0]


def per_device(layer_input, output_grad, loss_mask, proj_weight, out_weight, norm_gain):
    count = layer_input.shape[0]
    width_dev = proj_weight.shape[2]
    heads_dev = width_dev // HD
    position = lax.axis_index("seq")
    seq_bits = lax.axis_size("seq").bit_length() - 1
    head_bits = lax.axis_size("head").bit_length() - 1
    stages = list(range(seq_bits))
    swapped = [1, 0] + stages[2:] if seq_bits > 1 else stages
    order = slot_order(stages)
    half = len(order) // 2
    w_query, w_key, w_value = (proj_weight[:, i, :] for i in range(3))

    def project(weight):
        return jnp.dot(layer_input, weight, preferred_element_type=f32).astype(bf16)

    keys, values = project(w_key), project(w_value)
    own_state, keys_t, values_t = block_states(keys, values)

    before, total = jnp.zeros_like(own_state), own_state
    for bit in stages:
        got = exchange(total.astype(bf16), "seq", bit).astype(f32)
        before = before + jnp.where((position >> bit) & 1, got, 0.0)
        total = total + got
    state = (before + own_state).astype(bf16)

    early_send = gradient_terms([values_t, keys_t], layer_input, position, order[half:])
    early_got = exchange(early_send, "seq", stages[0])
    early_keep = gradient_terms([values_t, keys_t], layer_input, position, order[:half])

    queries = project(w_query)
    normed_grad = dot_t(output_grad, out_weight)
    mask = loss_mask.astype(f32)[:, None]
    normed_t, query_grad, query_grad_t, own_grad = middle(
        queries, normed_grad, mask, norm_gain[None, :], state
    )

    after, total, partner = jnp.zeros_like(own_grad), own_grad, None
    for bit in stages:
        got = exchange(total.astype(bf16), "seq", bit).astype(f32)
        if partner is None:
            partner = got
        else:
            after = after + jnp.where((position >> bit) & 1, 0.0, got)
        total = total + got
    upper = (position & 1) == 1
    pair = own_grad + partner
    state_grad = (after + jnp.where(upper, own_grad, pair)).astype(bf16)
    partner_state_grad = (after + jnp.where(upper, pair, partner)).astype(bf16)

    out_send = gradient_terms([normed_t], output_grad, position, order[half:])
    out_keep = gradient_terms([normed_t], output_grad, position, order[:half])
    out_weight_grad = halving(out_keep, out_send, "seq", stages)

    query_order = slot_order(swapped)
    query_send = gradient_terms([query_grad_t], layer_input, position, query_order[half:])
    query_keep = gradient_terms([query_grad_t], layer_input, position, query_order[:half])
    query_part = halving(query_keep, query_send, "seq", swapped)

    late_keep, late_send = late_terms(state_grad, partner_state_grad, early_keep, early_got)
    late_part = halving(late_keep, late_send, "seq", stages[1:])

    key_grad, value_grad = key_value_grads(keys, values, state_grad)
    place = lax.axis_index("head")
    token_order = slot_order(list(range(head_bits)))
    rows = count // len(token_order)

    def pick(grad):
        return [lax.dynamic_slice_in_dim(grad, (place ^ slot) * rows, rows, 0) for slot in token_order]

    half_tokens = len(token_order) // 2
    picked = [pick(grad) for grad in (query_grad, key_grad, value_grad)]

    def input_terms(lo, hi):
        part = 0.0
        for grad, weight in zip(picked, (w_query, w_key, w_value)):
            part = part + dot_t(jnp.concatenate(grad[lo:hi], 0), weight)
        return part.astype(bf16).reshape(hi - lo, rows, D)

    input_send = input_terms(half_tokens, 2 * half_tokens)
    input_keep = input_terms(0, half_tokens)
    input_grad = halving(input_keep, input_send, "head", list(range(head_bits))).astype(bf16)

    proj_weight_grad = jnp.stack(
        [query_part.T, late_part[:width_dev].T, late_part[width_dev:].T], 1
    )
    return (input_grad, proj_weight_grad, out_weight_grad)


def solution(mesh):
    in_specs = (
        P("seq", None),
        P("seq", None),
        P("seq"),
        P(None, None, "head"),
        P("head", None),
        P("head"),
    )
    out_specs = (P(("seq", "head"), None), P("seq", None, "head"), P("head", "seq"))
    return jax.shard_map(
        per_device, mesh=mesh, in_specs=in_specs, out_specs=out_specs, check_vma=False
    )
```

```python
import functools

import jax
import jax.numpy as jnp
from jax import lax
from jax.experimental import pallas as pl
from jax.experimental.pallas import tpu as pltpu
from jax.sharding import PartitionSpec as P

D = 2048
HD = 128
BLOCK = 1024
epsilon = 1e-06
f32 = jnp.float32
bf16 = jnp.bfloat16
VMEM_LIMIT = 48 * 1024 * 1024


def params():
    return pltpu.CompilerParams(vmem_limit_bytes=VMEM_LIMIT)


def dot(a, b):
    return lax.dot_general(a, b, (((1,), (0,)), ((), ())), preferred_element_type=f32)


def dot_t(a, b):
    return lax.dot_general(a, b, (((1,), (1,)), ((), ())), preferred_element_type=f32)


def exchange(arr, axis, bit):
    count = lax.axis_size(axis)
    return lax.ppermute(arr, axis, [(i, i ^ (1 << bit)) for i in range(count)])


def slot_order(stage_bits):
    order = [0]
    for bit in reversed(stage_bits):
        order = order + [slot | (1 << bit) for slot in order]
    return order


def state_kernel(key_ref, value_ref, state_ref, key_t_ref, value_t_ref):
    key_t = key_ref[...].T
    key_t_ref[...] = key_t
    value_t_ref[...] = value_ref[...].T
    state_ref[0] = dot(key_t, value_ref[...])


def block_states(keys, values):
    count, width = keys.shape
    heads = width // HD
    column = pl.BlockSpec((count, HD), lambda h: (0, h))
    row = pl.BlockSpec((HD, count), lambda h: (h, 0))
    return pl.pallas_call(
        state_kernel,
        grid=(heads,),
        in_specs=[column, column],
        out_specs=[pl.BlockSpec((1, HD, HD), lambda h: (h, 0, 0)), row, row],
        out_shape=[
            jax.ShapeDtypeStruct((heads, HD, HD), f32),
            jax.ShapeDtypeStruct((width, count), bf16),
            jax.ShapeDtypeStruct((width, count), bf16),
        ],
        compiler_params=params(),
        cost_estimate=pl.CostEstimate(
            flops=2 * count * width * HD, bytes_accessed=8 * count * width, transcendentals=0
        ),
        name="block_states",
    )(keys, values)


def terms_kernel(count_left, slots, block_ref, *refs):
    lefts, right = refs[:count_left], refs[count_left]
    out, held, sems = refs[count_left + 1 :]
    width = out.shape[2]
    copies = []
    for index in range(slots):
        start = pl.multiple_of(block_ref[index] * width, width)
        copy = pltpu.make_async_copy(right.at[:, pl.ds(start, width)], held.at[index], sems.at[index])
        copy.start()
        copies.append(copy)
    for index in range(slots):
        copies[index].wait()
        low = 0
        for ref in lefts:
            high = low + ref.shape[0]
            out[index, low:high, :] = dot(ref[...], held[index]).astype(bf16)
            low = high


def gradient_terms(lefts, right, position, slots):
    rows, count = lefts[0].shape
    width = right.shape[1] // lax.axis_size("seq")
    total = rows * len(lefts)
    number = len(slots)
    blocks = position ^ jnp.array(slots, jnp.int32)
    if width % 128:
        picked = jnp.take(right.reshape(count, -1, width), blocks, axis=1)
        left = jnp.concatenate(lefts, 0)
        return jnp.einsum("at,tnb->nab", left, picked, preferred_element_type=f32).astype(bf16)
    vmem = pl.BlockSpec(memory_space=pltpu.VMEM)
    return pl.pallas_call(
        functools.partial(terms_kernel, len(lefts), number),
        in_specs=[pl.BlockSpec(memory_space=pltpu.SMEM)]
        + [vmem] * len(lefts)
        + [pl.BlockSpec(memory_space=pl.ANY)],
        out_specs=vmem,
        out_shape=jax.ShapeDtypeStruct((number, total, width), bf16),
        scratch_shapes=[pltpu.VMEM((number, count, width), bf16), pltpu.SemaphoreType.DMA((number,))],
        compiler_params=params(),
        cost_estimate=pl.CostEstimate(
            flops=2 * count * total * width * number,
            bytes_accessed=2 * number * width * (count + total) + 2 * total * count,
            transcendentals=0,
        ),
        name="gradient_terms",
    )(blocks, *lefts, right)


def middle_kernel(query_ref, grad_ref, mask_ref, gain_ref, state_ref, normed_t_ref, query_grad_ref, query_grad_t_ref, block_grad_ref):
    query = query_ref[...]
    state = state_ref[0]
    mask = mask_ref[...]
    gain = gain_ref[...].astype(f32)
    attended = dot(query, state)
    scale = lax.rsqrt(jnp.mean(attended * attended, -1, keepdims=True) + epsilon)
    unit = attended * scale
    normed_t_ref[...] = (unit * gain * mask).astype(bf16).T
    scaled = grad_ref[...] * mask * gain
    inner = jnp.mean(scaled * attended, -1, keepdims=True)
    attended_grad = (scale * scaled - attended * (scale * scale * scale) * inner).astype(bf16)
    attended_grad_t = attended_grad.T
    block_grad_ref[0] = dot(attended_grad_t, query)
    query_grad_ref[...] = dot_t(attended_grad, state).astype(bf16)
    query_grad_t_ref[...] = dot(state, attended_grad_t).astype(bf16)


def middle(queries, normed_grad, mask, gain, state):
    count, width = queries.shape
    heads = width // HD
    column = pl.BlockSpec((count, HD), lambda h: (0, h))
    row = pl.BlockSpec((HD, count), lambda h: (h, 0))
    square = pl.BlockSpec((1, HD, HD), lambda h: (h, 0, 0))
    return pl.pallas_call(
        middle_kernel,
        grid=(heads,),
        in_specs=[
            column,
            column,
            pl.BlockSpec((count, 1), lambda h: (0, 0)),
            pl.BlockSpec((1, HD), lambda h: (0, h)),
            square,
        ],
        out_specs=[row, column, row, square],
        out_shape=[
            jax.ShapeDtypeStruct((width, count), bf16),
            jax.ShapeDtypeStruct((count, width), bf16),
            jax.ShapeDtypeStruct((width, count), bf16),
            jax.ShapeDtypeStruct((heads, HD, HD), f32),
        ],
        compiler_params=params(),
        cost_estimate=pl.CostEstimate(
            flops=8 * count * width * HD, bytes_accessed=12 * count * width, transcendentals=count
        ),
        name="norm_backward",
    )(queries, normed_grad, mask, gain, state)


def late_kernel(flip, mine_ref, other_ref, own_keep_ref, own_send_ref, got_keep_ref, got_send_ref, keep_ref, send_ref):
    side = 0 if flip else 1

    def times(state, block):
        return lax.dot_general(state, block, (((side,), (0,)), ((), ())), preferred_element_type=f32)

    for own, got, out in ((own_keep_ref, got_keep_ref, keep_ref), (own_send_ref, got_send_ref, send_ref)):
        for h in range(mine_ref.shape[0]):
            rows = slice(h * HD, (h + 1) * HD)
            out[0, rows, :] = (times(mine_ref[h], own[0, rows, :]) + times(other_ref[h], got[0, rows, :])).astype(bf16)


def late_terms(flip, mine, other, own, got):
    slots, total, width = own.shape
    heads = mine.shape[0]
    half = slots // 2
    square = pl.BlockSpec((heads, HD, HD), lambda i: (0, 0, 0))
    low = pl.BlockSpec((1, total, width), lambda i: (i, 0, 0))
    high = pl.BlockSpec((1, total, width), lambda i: (i + half, 0, 0))
    out = jax.ShapeDtypeStruct((half, total, width), bf16)
    return pl.pallas_call(
        functools.partial(late_kernel, flip),
        grid=(half,),
        in_specs=[square, square, low, high, low, high],
        out_specs=[low, low],
        out_shape=[out, out],
        compiler_params=params(),
        cost_estimate=pl.CostEstimate(
            flops=4 * slots * total * width * HD, bytes_accessed=6 * slots * total * width, transcendentals=0
        ),
        name="late_terms",
    )(mine, other, own, own, got, got)


def key_value_kernel(key_ref, value_ref, grad_ref, key_grad_ref, value_grad_ref):
    key_grad_ref[...] = dot(value_ref[...], grad_ref[0]).astype(bf16)
    value_grad_ref[...] = dot_t(key_ref[...], grad_ref[0]).astype(bf16)


def key_value_grads(keys, values, state_grad_t):
    count, width = keys.shape
    column = pl.BlockSpec((count, HD), lambda h: (0, h))
    out = jax.ShapeDtypeStruct((count, width), bf16)
    return pl.pallas_call(
        key_value_kernel,
        grid=(width // HD,),
        in_specs=[column, column, pl.BlockSpec((1, HD, HD), lambda h: (h, 0, 0))],
        out_specs=[column, column],
        out_shape=[out, out],
        compiler_params=params(),
        cost_estimate=pl.CostEstimate(
            flops=4 * count * width * HD, bytes_accessed=8 * count * width, transcendentals=0
        ),
        name="key_value_grads",
    )(keys, values, state_grad_t)


def input_kernel(slots, block_ref, query_ref, key_ref, value_ref, weight_ref, out_ref):
    rows = out_ref.shape[1]
    for index in range(slots):
        start = pl.multiple_of(block_ref[index] * rows, rows)
        total = dot_t(query_ref[pl.ds(start, rows), :], weight_ref[0])
        total += dot_t(key_ref[pl.ds(start, rows), :], weight_ref[1])
        total += dot_t(value_ref[pl.ds(start, rows), :], weight_ref[2])
        out_ref[index] = total.astype(bf16)


def input_terms(grads, weight, place, slots, tile=512):
    count, width = grads[0].shape
    rows = count // lax.axis_size("head")
    number = len(slots)
    full = pl.BlockSpec((count, width), lambda i, b: (0, 0))
    return pl.pallas_call(
        functools.partial(input_kernel, number),
        grid_spec=pltpu.PrefetchScalarGridSpec(
            num_scalar_prefetch=1,
            grid=(D // tile,),
            in_specs=[full, full, full, pl.BlockSpec((3, tile, width), lambda i, b: (0, i, 0))],
            out_specs=pl.BlockSpec((number, rows, tile), lambda i, b: (0, 0, i)),
        ),
        out_shape=jax.ShapeDtypeStruct((number, rows, D), bf16),
        compiler_params=params(),
        cost_estimate=pl.CostEstimate(
            flops=6 * number * rows * width * D,
            bytes_accessed=6 * D * width + 6 * count * width + 2 * number * rows * D,
            transcendentals=0,
        ),
        name="input_terms",
    )(place ^ jnp.array(slots, jnp.int32), *grads, weight)


def finish_kernel(*refs):
    out = refs[-1]
    for index in range(3):
        keep, got = refs[2 * index], refs[2 * index + 1]
        out[index] = (keep[...].astype(f32) + got[...].astype(f32)).T


def finish(pairs):
    rows, width = pairs[0].shape
    return pl.pallas_call(
        finish_kernel,
        out_shape=jax.ShapeDtypeStruct((3, width, rows), f32),
        compiler_params=params(),
        name="finish",
    )(*pairs)


def after(value, *others):
    return lax.optimization_barrier((value,) + others)[0]


def split_sum(keep, got):
    total = keep.astype(f32) + got.astype(f32)
    half = total.shape[0] // 2
    return total[:half].astype(bf16), total[half:].astype(bf16)


def halving(keep, send, axis, stage_bits):
    for bit in stage_bits[:-1]:
        keep, send = split_sum(keep, exchange(send, axis, bit))
    return keep[0], exchange(send, axis, stage_bits[-1])[0]


def per_device(layer_input, output_grad, loss_mask, proj_weight, out_weight, norm_gain):
    count = layer_input.shape[0]
    position = lax.axis_index("seq")
    seq_bits = lax.axis_size("seq").bit_length() - 1
    head_bits = lax.axis_size("head").bit_length() - 1
    stages = list(range(seq_bits))
    swapped = [1, 0] + stages[2:]
    bits = [(position >> bit) & 1 == 1 for bit in stages]
    order, order_swapped = slot_order(stages), slot_order(swapped)
    half = len(order) // 2
    weights = jnp.transpose(proj_weight, (1, 0, 2))

    def project(rows, index):
        return jnp.dot(rows, weights[index], preferred_element_type=f32).astype(bf16)

    def terms(lefts, right, slots):
        return gradient_terms(lefts, right, position, slots)

    keys, values = project(layer_input, 1), project(layer_input, 2)
    own_state, keys_t, values_t = block_states(keys, values)
    mask = loss_mask.astype(f32)[:, None]

    got = exchange(own_state.astype(bf16), "seq", 0)
    value_send = terms([values_t], after(layer_input, own_state), order[half:])
    got = after(got, value_send)
    before = jnp.where(bits[0], got.astype(f32), 0.0)
    total = own_state + got.astype(f32)
    value_got = exchange(after(value_send, total), "seq", 0)

    got = exchange(total.astype(bf16), "seq", 1)
    queries = project(after(layer_input, total), 0)
    got = after(got, queries)
    before = before + jnp.where(bits[1], got.astype(f32), 0.0)
    total = total + got.astype(f32)

    for bit in stages[2:]:
        got = exchange(total.astype(bf16), "seq", bit)
        if bit == 2:
            key_send = terms([keys_t], after(layer_input, total), order_swapped[half:])
            key_got = exchange(key_send, "seq", 1)
            normed_grad = dot_t(after(output_grad, key_send), out_weight)
            got = after(got, normed_grad)
        before = before + jnp.where(bits[bit], got.astype(f32), 0.0)
        total = total + got.astype(f32)
    state = (before + own_state).astype(bf16)

    normed_t, query_grad, query_grad_t, own_grad = middle(
        queries, normed_grad, mask, norm_gain[None, :], state
    )

    got = exchange(own_grad.astype(bf16), "seq", 0)
    out_send = terms([normed_t], after(output_grad, own_grad), order[half:])
    out_keep = terms([normed_t], after(output_grad, out_send), order[:half])
    got = after(got, out_keep).astype(f32)
    total = own_grad + got
    mine, mate = jnp.where(bits[0], own_grad, total), jnp.where(bits[0], total, got)
    out_send = after(out_send, total)
    out_got = exchange(out_send, "seq", 0)

    got = exchange(jnp.stack([total, mine]).astype(bf16), "seq", 1)
    query_send = terms([query_grad_t], after(layer_input, total), order[half:])
    query_keep = terms([query_grad_t], after(layer_input, query_send), order[:half])
    got = after(got, query_keep).astype(f32)
    later = jnp.where(bits[1], 0.0, got[0])
    mine, mate = mine + later, mate + later
    other = got[1] + jnp.where(bits[1], total, 0.0)
    total = total + got[0]
    query_got = exchange(after(query_send, total), "seq", 0)

    for bit in stages[2:]:
        got = exchange(total.astype(bf16), "seq", bit)
        if bit == 2:
            value_keep = terms([values_t], after(layer_input, total), order[:half])
            key_keep = terms([keys_t], after(layer_input, value_keep), order_swapped[:half])
            got = after(got, key_keep)
        got = got.astype(f32)
        later = jnp.where(bits[bit], 0.0, got)
        mine, mate, other = mine + later, mate + later, other + later
        total = total + got
    state_grad, mate_grad, other_grad = mine.astype(bf16), mate.astype(bf16), other.astype(bf16)

    value_half = late_terms(True, state_grad, mate_grad, value_keep, value_got)
    value_pair = halving(*value_half, "seq", stages[1:])
    key_half = late_terms(False, state_grad, other_grad, after(key_keep, value_half[0]), key_got)
    key_pair = halving(*key_half, "seq", swapped[1:])

    key_grad, value_grad = key_value_grads(keys, values, after(state_grad, key_half[0]))
    place = lax.axis_index("head")
    head_stages = list(range(head_bits))
    token_order = slot_order(head_stages)
    middle_slot = len(token_order) // 2
    grads = (query_grad, key_grad, value_grad)
    input_send = input_terms(grads, weights, place, token_order[middle_slot:])
    input_keep = input_terms(grads, after(weights, input_send), place, token_order[:middle_slot])
    keep, got = halving(input_keep, input_send, "head", head_stages)
    input_grad = (keep.astype(f32) + got.astype(f32)).astype(bf16)

    keep, send = split_sum(out_keep, out_got)
    keep, got = halving(keep, send, "seq", stages[1:])
    out_weight_grad = keep.astype(f32) + got.astype(f32)

    keep, send = split_sum(query_keep, query_got)
    query_pair = halving(keep, send, "seq", stages[1:])
    proj_weight_grad = finish(query_pair + value_pair + key_pair)
    return (input_grad, jnp.transpose(proj_weight_grad, (1, 0, 2)), out_weight_grad)


def solution(mesh):
    in_specs = (
        P("seq", None),
        P("seq", None),
        P("seq"),
        P(None, None, "head"),
        P("head", None),
        P("head"),
    )
    out_specs = (P(("seq", "head"), None), P("seq", None, "head"), P("head", "seq"))
    return jax.shard_map(
        per_device, mesh=mesh, in_specs=in_specs, out_specs=out_specs, check_vma=False
    )
```

```python
import functools

import jax
import jax.numpy as jnp
from jax import lax
from jax.experimental import pallas as pl
from jax.experimental.pallas import tpu as pltpu
from jax.sharding import PartitionSpec as P

D = 2048
HD = 128
BLOCK = 1024
epsilon = 1e-06
f32 = jnp.float32
bf16 = jnp.bfloat16
MIB = 1024 * 1024


def params(mib=16):
    return pltpu.CompilerParams(vmem_limit_bytes=mib * MIB)


def dot(a, b):
    return lax.dot_general(a, b, (((1,), (0,)), ((), ())), preferred_element_type=f32)


def dot_t(a, b):
    return lax.dot_general(a, b, (((1,), (1,)), ((), ())), preferred_element_type=f32)


def exchange(arr, axis, bit):
    count = lax.axis_size(axis)
    return lax.ppermute(arr, axis, [(i, i ^ (1 << bit)) for i in range(count)])


def slot_order(stage_bits):
    order = [0]
    for bit in reversed(stage_bits):
        order = order + [slot | (1 << bit) for slot in order]
    return order


def state_kernel(key_ref, value_ref, state_ref, key_t_ref, value_t_ref):
    key_t = key_ref[...].T
    key_t_ref[...] = key_t
    value_t_ref[...] = value_ref[...].T
    state_ref[0] = dot(key_t, value_ref[...])


def block_states(keys, values):
    count, width = keys.shape
    heads = width // HD
    column = pl.BlockSpec((count, HD), lambda h: (0, h))
    row = pl.BlockSpec((HD, count), lambda h: (h, 0))
    return pl.pallas_call(
        state_kernel,
        grid=(heads,),
        in_specs=[column, column],
        out_specs=[pl.BlockSpec((1, HD, HD), lambda h: (h, 0, 0)), row, row],
        out_shape=[
            jax.ShapeDtypeStruct((heads, HD, HD), f32),
            jax.ShapeDtypeStruct((width, count), bf16),
            jax.ShapeDtypeStruct((width, count), bf16),
        ],
        compiler_params=params(),
        cost_estimate=pl.CostEstimate(
            flops=2 * count * width * HD, bytes_accessed=8 * count * width, transcendentals=0
        ),
        name="block_states",
    )(keys, values)


def terms_kernel(number, outputs, position_ref, *refs):
    lefts, right, outs = refs[:number], refs[number], refs[number + 1 :]
    width = outs[0].shape[2]
    jobs = {}
    for out, (left, low, high, slots) in zip(outs, outputs):
        for index, slot in enumerate(slots):
            jobs.setdefault((left, slot), []).append((low, high, out, index))
    for (left, slot), parts in jobs.items():
        start = pl.multiple_of((position_ref[0] ^ slot) * width, width)
        product = dot(lefts[left][...], right[:, pl.ds(start, width)]).astype(bf16)
        for low, high, out, index in parts:
            out[index] = product[low:high]


def gradient_terms(lefts, right, position, outputs):
    count = right.shape[0]
    width = right.shape[1] // lax.axis_size("seq")
    if width % 128:
        blocked = right.reshape(count, -1, width)
        results = []
        for left, low, high, slots in outputs:
            picked = jnp.take(blocked, position ^ jnp.array(slots, jnp.int32), axis=1)
            part = jnp.einsum("at,tnb->nab", lefts[left][low:high], picked, preferred_element_type=f32)
            results.append(part.astype(bf16))
        return results
    shapes = [(len(slots), high - low, width) for _, low, high, slots in outputs]
    size = sum(n * r * w for n, r, w in shapes)
    vmem = pl.BlockSpec(memory_space=pltpu.VMEM)
    return pl.pallas_call(
        functools.partial(terms_kernel, len(lefts), outputs),
        in_specs=[pl.BlockSpec(memory_space=pltpu.SMEM)] + [vmem] * (len(lefts) + 1),
        out_specs=[vmem] * len(outputs),
        out_shape=[jax.ShapeDtypeStruct(shape, bf16) for shape in shapes],
        compiler_params=params(),
        cost_estimate=pl.CostEstimate(
            flops=2 * count * size,
            bytes_accessed=2 * (size + right.size + sum(left.size for left in lefts)),
            transcendentals=0,
        ),
        name="gradient_terms",
    )(position[None], *lefts, right)


def sums_kernel(groups, merge, *refs):
    ins, outs = refs[: 2 * groups], refs[2 * groups :]
    low = 0
    for index in range(groups):
        keep, got = ins[2 * index], ins[2 * index + 1]
        half, rows = keep.shape[0] // 2, keep.shape[1]
        if merge:
            kept, sent = (out.at[:, low : low + rows, :] for out in outs)
            low += rows
        else:
            kept, sent = outs[2 * index], outs[2 * index + 1]
        for slot in range(half):
            kept[slot] = (keep[slot].astype(f32) + got[slot].astype(f32)).astype(bf16)
            other = half + slot
            sent[slot] = (keep[other].astype(f32) + got[other].astype(f32)).astype(bf16)


def sums(pairs, merge=False):
    slots, rows, width = pairs[0][0].shape
    total = sum(keep.shape[1] for keep, _ in pairs) if merge else rows
    shape = jax.ShapeDtypeStruct((slots // 2, total, width), bf16)
    vmem = pl.BlockSpec(memory_space=pltpu.VMEM)
    outs = 2 if merge else 2 * len(pairs)
    size = sum(keep.size for keep, _ in pairs)
    return pl.pallas_call(
        functools.partial(sums_kernel, len(pairs), merge),
        in_specs=[vmem] * (2 * len(pairs)),
        out_specs=[vmem] * outs,
        out_shape=[shape] * outs,
        compiler_params=params(),
        cost_estimate=pl.CostEstimate(flops=size, bytes_accessed=6 * size, transcendentals=0),
        name="sums",
    )(*[array for pair in pairs for array in pair])


def middle_kernel(query_ref, grad_ref, mask_ref, gain_ref, state_ref, normed_t_ref, query_grad_ref, query_grad_t_ref, block_grad_ref):
    query = query_ref[...]
    state = state_ref[0]
    mask = mask_ref[...]
    gain = gain_ref[...].astype(f32)
    attended = dot(query, state)
    scale = lax.rsqrt(jnp.mean(attended * attended, -1, keepdims=True) + epsilon)
    unit = attended * scale
    normed_t_ref[...] = (unit * gain * mask).astype(bf16).T
    scaled = grad_ref[...] * mask * gain
    inner = jnp.mean(scaled * attended, -1, keepdims=True)
    attended_grad = (scale * scaled - attended * (scale * scale * scale) * inner).astype(bf16)
    attended_grad_t = attended_grad.T
    block_grad_ref[0] = dot(attended_grad_t, query)
    query_grad_ref[...] = dot_t(attended_grad, state).astype(bf16)
    query_grad_t_ref[...] = dot(state, attended_grad_t).astype(bf16)


def middle(queries, normed_grad, mask, gain, state):
    count, width = queries.shape
    heads = width // HD
    column = pl.BlockSpec((count, HD), lambda h: (0, h))
    row = pl.BlockSpec((HD, count), lambda h: (h, 0))
    square = pl.BlockSpec((1, HD, HD), lambda h: (h, 0, 0))
    return pl.pallas_call(
        middle_kernel,
        grid=(heads,),
        in_specs=[
            column,
            column,
            pl.BlockSpec((count, 1), lambda h: (0, 0)),
            pl.BlockSpec((1, HD), lambda h: (0, h)),
            square,
        ],
        out_specs=[row, column, row, square],
        out_shape=[
            jax.ShapeDtypeStruct((width, count), bf16),
            jax.ShapeDtypeStruct((count, width), bf16),
            jax.ShapeDtypeStruct((width, count), bf16),
            jax.ShapeDtypeStruct((heads, HD, HD), f32),
        ],
        compiler_params=params(),
        cost_estimate=pl.CostEstimate(
            flops=8 * count * width * HD, bytes_accessed=12 * count * width, transcendentals=count
        ),
        name="norm_backward",
    )(queries, normed_grad, mask, gain, state)


def late_kernel(flip, mine_ref, other_ref, own_keep_ref, own_send_ref, got_keep_ref, got_send_ref, keep_ref, send_ref):
    side = 0 if flip else 1

    def times(state, block):
        return lax.dot_general(state, block, (((side,), (0,)), ((), ())), preferred_element_type=f32)

    for own, got, out in ((own_keep_ref, got_keep_ref, keep_ref), (own_send_ref, got_send_ref, send_ref)):
        for h in range(mine_ref.shape[0]):
            rows = slice(h * HD, (h + 1) * HD)
            out[0, rows, :] = (times(mine_ref[h], own[0, rows, :]) + times(other_ref[h], got[0, rows, :])).astype(bf16)


def late_terms(flip, mine, other, own, got):
    slots, total, width = own.shape
    heads = mine.shape[0]
    half = slots // 2
    square = pl.BlockSpec((heads, HD, HD), lambda i: (0, 0, 0))
    low = pl.BlockSpec((1, total, width), lambda i: (i, 0, 0))
    high = pl.BlockSpec((1, total, width), lambda i: (i + half, 0, 0))
    out = jax.ShapeDtypeStruct((half, total, width), bf16)
    return pl.pallas_call(
        functools.partial(late_kernel, flip),
        grid=(half,),
        in_specs=[square, square, low, high, low, high],
        out_specs=[low, low],
        out_shape=[out, out],
        compiler_params=params(),
        cost_estimate=pl.CostEstimate(
            flops=4 * slots * total * width * HD, bytes_accessed=6 * slots * total * width, transcendentals=0
        ),
        name="late_terms",
    )(mine, other, own, own, got, got)


def key_value_kernel(key_ref, value_ref, grad_ref, key_grad_ref, value_grad_ref):
    key_grad_ref[...] = dot(value_ref[...], grad_ref[0]).astype(bf16)
    value_grad_ref[...] = dot_t(key_ref[...], grad_ref[0]).astype(bf16)


def key_value_grads(keys, values, state_grad_t):
    count, width = keys.shape
    column = pl.BlockSpec((count, HD), lambda h: (0, h))
    out = jax.ShapeDtypeStruct((count, width), bf16)
    return pl.pallas_call(
        key_value_kernel,
        grid=(width // HD,),
        in_specs=[column, column, pl.BlockSpec((1, HD, HD), lambda h: (h, 0, 0))],
        out_specs=[column, column],
        out_shape=[out, out],
        compiler_params=params(),
        cost_estimate=pl.CostEstimate(
            flops=4 * count * width * HD, bytes_accessed=8 * count * width, transcendentals=0
        ),
        name="key_value_grads",
    )(keys, values, state_grad_t)


def input_kernel(order, place_ref, query_ref, key_ref, value_ref, weight_ref, keep_ref, send_ref, held_ref):
    total = dot_t(query_ref[...], weight_ref[0])
    total += dot_t(key_ref[...], weight_ref[1])
    total += dot_t(value_ref[...], weight_ref[2])
    held_ref[...] = total.astype(bf16).reshape(held_ref.shape)
    half = len(order) // 2
    for index in range(half):
        keep_ref[index] = held_ref[place_ref[0] ^ order[index]]
        send_ref[index] = held_ref[place_ref[0] ^ order[half + index]]


def input_terms(grads, weight, place, order, chunk, chunks, tile=512):
    count, width = grads[0].shape
    half = len(order) // 2
    rows = count // len(order)
    columns = D // chunks
    first = chunk * columns // tile
    full = pl.BlockSpec((count, width), lambda i, b: (0, 0))
    out = pl.BlockSpec((half, rows, tile), lambda i, b: (0, 0, i))
    shape = jax.ShapeDtypeStruct((half, rows, columns), bf16)
    return pl.pallas_call(
        functools.partial(input_kernel, order),
        grid_spec=pltpu.PrefetchScalarGridSpec(
            num_scalar_prefetch=1,
            grid=(columns // tile,),
            in_specs=[full, full, full, pl.BlockSpec((3, tile, width), lambda i, b: (0, first + i, 0))],
            out_specs=[out, out],
            scratch_shapes=[pltpu.VMEM((len(order), rows, tile), bf16)],
        ),
        out_shape=[shape, shape],
        compiler_params=params(32),
        cost_estimate=pl.CostEstimate(
            flops=6 * count * width * columns,
            bytes_accessed=6 * columns * width + 6 * count * width + 2 * count * columns,
            transcendentals=0,
        ),
        name="input_terms",
    )(place[None], *grads, weight)


def finish_kernel(*refs):
    out = refs[-1]
    for index in range(3):
        keep, got = refs[2 * index], refs[2 * index + 1]
        out[index] = (keep[...].astype(f32) + got[...].astype(f32)).T


def finish(pairs):
    rows, width = pairs[0].shape
    return pl.pallas_call(
        finish_kernel,
        out_shape=jax.ShapeDtypeStruct((3, width, rows), f32),
        compiler_params=params(),
        name="finish",
    )(*pairs)


def after(value, *others):
    return lax.optimization_barrier((value,) + others)[0]


def per_device(layer_input, output_grad, loss_mask, proj_weight, out_weight, norm_gain):
    width_dev = proj_weight.shape[2]
    side = width_dev // 2
    position = lax.axis_index("seq")
    place = lax.axis_index("head")
    seq_bits = lax.axis_size("seq").bit_length() - 1
    head_bits = lax.axis_size("head").bit_length() - 1
    stages = list(range(seq_bits))
    bits = [(position >> bit) & 1 == 1 for bit in stages]
    order, swapped = slot_order(stages), slot_order([1, 0] + stages[2:])
    half = len(order) // 2
    head_order = slot_order(list(range(head_bits)))
    weights = jnp.transpose(proj_weight, (1, 0, 2))

    def project(rows, index):
        return jnp.dot(rows, weights[index], preferred_element_type=f32).astype(bf16)

    def one_term(left, right, slots):
        return gradient_terms([left], right, position, [(0, 0, left.shape[0], slots)])[0]

    def both_terms(left, right):
        outputs = []
        for low, slots in ((0, order), (side, swapped)):
            outputs += [(0, low, low + side, slots[:half]), (0, low, low + side, slots[half:])]
        return gradient_terms([left], right, position, outputs)

    keys, values = project(layer_input, 1), project(layer_input, 2)
    own_state, keys_t, values_t = block_states(keys, values)
    mask = loss_mask.astype(f32)[:, None]

    got = exchange(own_state.astype(bf16), "seq", 0)
    value_send = one_term(values_t, after(layer_input, own_state), order[half:])
    got = after(got, value_send)
    before = jnp.where(bits[0], got.astype(f32), 0.0)
    total = own_state + got.astype(f32)
    value_got = exchange(after(value_send, total), "seq", 0)

    got = exchange(total.astype(bf16), "seq", 1)
    queries = project(after(layer_input, total), 0)
    got = after(got, queries)
    before = before + jnp.where(bits[1], got.astype(f32), 0.0)
    total = total + got.astype(f32)

    for bit in stages[2:]:
        got = exchange(total.astype(bf16), "seq", bit)
        if bit == 2:
            key_send = one_term(keys_t, after(layer_input, total), swapped[half:])
            key_got = exchange(key_send, "seq", 1)
            normed_grad = dot_t(after(output_grad, key_send), out_weight)
            got = after(got, normed_grad)
        before = before + jnp.where(bits[bit], got.astype(f32), 0.0)
        total = total + got.astype(f32)
    state = (before + own_state).astype(bf16)

    normed_t, query_grad, query_grad_t, own_grad = middle(
        queries, normed_grad, mask, norm_gain[None, :], state
    )

    got = exchange(own_grad.astype(bf16), "seq", 0)
    out_terms = both_terms(normed_t, after(output_grad, own_grad))
    got = after(got, *out_terms).astype(f32)
    total = own_grad + got
    mine, mate = jnp.where(bits[0], own_grad, total), jnp.where(bits[0], total, got)
    out_first_got = exchange(after(out_terms[1], total), "seq", 0)

    got = exchange(jnp.stack([total, mine]).astype(bf16), "seq", 1)
    query_terms = both_terms(query_grad_t, after(layer_input, total))
    got = after(got, *query_terms, value_got).astype(f32)
    later = jnp.where(bits[1], 0.0, got[0])
    mine, mate = mine + later, mate + later
    other = got[1] + jnp.where(bits[1], total, 0.0)
    total = total + got[0]

    for bit in stages[2:]:
        got = exchange(total.astype(bf16), "seq", bit)
        if bit == 2:
            out_second_got = exchange(after(out_terms[3], total), "seq", 1)
            value_keep = one_term(values_t, after(layer_input, total), order[:half])
            key_keep = one_term(keys_t, after(layer_input, value_keep), swapped[:half])
            got = after(got, key_keep, key_got)
        got = got.astype(f32)
        later = jnp.where(bits[bit], 0.0, got)
        mine, mate, other = mine + later, mate + later, other + later
        total = total + got
    state_grad, mate_grad, other_grad = mine.astype(bf16), mate.astype(bf16), other.astype(bf16)

    value_half = late_terms(True, state_grad, mate_grad, value_keep, value_got)
    value_got = exchange(value_half[1], "seq", 1)
    key_half = late_terms(False, state_grad, other_grad, after(key_keep, value_half[0]), key_got)
    key_got = exchange(key_half[1], "seq", 0)

    key_grad, value_grad = key_value_grads(keys, values, after(state_grad, key_half[0]))
    grads = (query_grad, key_grad, value_grad)
    input_keep, input_send, input_got = [None, None], [None, None], [None, None]
    input_keep[0], input_send[0] = input_terms(grads, weights, place, head_order, 0, 2)
    input_got[0] = exchange(input_send[0], "head", 0)

    out_first_got, out_second_got = after((out_first_got, out_second_got), input_keep[0])
    out_terms = sums([(out_terms[0], out_first_got), (out_terms[2], out_second_got)])
    out_first_got = exchange(out_terms[1], "seq", 1)
    out_second_got = exchange(out_terms[3], "seq", 0)

    input_keep[1], input_send[1] = input_terms(
        grads, after(weights, out_terms[0]), place, head_order, 1, 2
    )
    input_got[1] = exchange(input_send[1], "head", 0)

    def rest(keep, send, bits_left):
        for bit in bits_left[:-1]:
            keep, send = sums([(keep, exchange(send, "seq", bit))])
        return keep[0], exchange(send, "seq", bits_left[-1])[0]

    key_got = after(key_got, input_keep[1])
    key_half = sums([(key_half[0], key_got)])
    key_pair = rest(*key_half, stages[2:])
    query_first_got = exchange(after(query_terms[1], key_half[0]), "seq", 0)
    query_second_got = exchange(after(query_terms[3], key_half[0]), "seq", 1)

    def head_rest(keep, got):
        for bit in range(1, head_bits):
            keep, send = sums([(keep, got)])
            got = exchange(send, "head", bit)
        return keep[0], got[0]

    first = head_rest(input_keep[0], after(input_got[0], key_half[0]))
    second = head_rest(input_keep[1], after(input_got[1], first[0]))

    value_half = sums([(value_half[0], after(value_got, second[0]))])
    value_pair = rest(*value_half, stages[2:])

    out_first_got, out_second_got = after((out_first_got, out_second_got), value_half[0])
    out_half = sums([(out_terms[0], out_first_got), (out_terms[2], out_second_got)], merge=True)
    out_pair = rest(*out_half, stages[2:])

    query_first_got, query_second_got = after((query_first_got, query_second_got), out_half[0])
    query_terms = sums([(query_terms[0], query_first_got), (query_terms[2], query_second_got)])
    query_first_got = exchange(query_terms[1], "seq", 1)
    query_second_got = exchange(query_terms[3], "seq", 0)

    first, second = after((first, second), query_terms[0])
    input_grad = jnp.concatenate(
        [(keep.astype(f32) + got.astype(f32)).astype(bf16) for keep, got in (first, second)], 1
    )
    query_half = sums(
        [(query_terms[0], query_first_got), (query_terms[2], query_second_got)], merge=True
    )
    query_pair = rest(*query_half, stages[2:])
    out_weight_grad = out_pair[0].astype(f32) + out_pair[1].astype(f32)
    proj_weight_grad = finish(query_pair + value_pair + key_pair)
    return (input_grad, jnp.transpose(proj_weight_grad, (1, 0, 2)), out_weight_grad)


def solution(mesh):
    in_specs = (
        P("seq", None),
        P("seq", None),
        P("seq"),
        P(None, None, "head"),
        P("head", None),
        P("head"),
    )
    out_specs = (P(("seq", "head"), None), P("seq", None, "head"), P("head", "seq"))
    return jax.shard_map(
        per_device, mesh=mesh, in_specs=in_specs, out_specs=out_specs, check_vma=False
    )
```

```python
import functools

import jax
import jax.numpy as jnp
from jax import lax
from jax.experimental import pallas as pl
from jax.experimental.pallas import tpu as pltpu
from jax.sharding import PartitionSpec as P

D = 2048
HD = 128
BLOCK = 1024
epsilon = 1e-06
f32 = jnp.float32
bf16 = jnp.bfloat16
MIB = 1024 * 1024
COST = pl.CostEstimate(flops=1000000, bytes_accessed=1, transcendentals=0)


def params(mib=16):
    return pltpu.CompilerParams(vmem_limit_bytes=mib * MIB)


def dot(a, b):
    return lax.dot_general(a, b, (((1,), (0,)), ((), ())), preferred_element_type=f32)


def dot_t(a, b):
    return lax.dot_general(a, b, (((1,), (1,)), ((), ())), preferred_element_type=f32)


def exchange(arr, axis, bit):
    count = lax.axis_size(axis)
    return lax.ppermute(arr, axis, [(i, i ^ (1 << bit)) for i in range(count)])


def slot_order(stage_bits):
    order = [0]
    for bit in reversed(stage_bits):
        order = order + [slot | (1 << bit) for slot in order]
    return order


def flip_kernel(value_ref, value_t_ref):
    value_t_ref[...] = value_ref[...].T


def flipped(values):
    count, width = values.shape
    return pl.pallas_call(
        flip_kernel,
        grid=(width // HD,),
        in_specs=[pl.BlockSpec((count, HD), lambda h: (0, h))],
        out_specs=pl.BlockSpec((HD, count), lambda h: (h, 0)),
        out_shape=jax.ShapeDtypeStruct((width, count), bf16),
        compiler_params=params(),
        cost_estimate=COST,
        name="flipped",
    )(values)


def state_kernel(key_ref, value_ref, state_ref, sent_ref, key_t_ref):
    key_t = key_ref[...].T
    key_t_ref[...] = key_t
    state = dot(key_t, value_ref[...])
    state_ref[0] = state
    sent_ref[0] = state.astype(bf16)


def block_states(keys, values):
    count, width = keys.shape
    heads = width // HD
    column = pl.BlockSpec((count, HD), lambda h: (0, h))
    square = pl.BlockSpec((1, HD, HD), lambda h: (h, 0, 0))
    return pl.pallas_call(
        state_kernel,
        grid=(heads,),
        in_specs=[column, column],
        out_specs=[square, square, pl.BlockSpec((HD, count), lambda h: (h, 0))],
        out_shape=[
            jax.ShapeDtypeStruct((heads, HD, HD), f32),
            jax.ShapeDtypeStruct((heads, HD, HD), bf16),
            jax.ShapeDtypeStruct((width, count), bf16),
        ],
        compiler_params=params(),
        cost_estimate=COST,
        name="block_states",
    )(keys, values)


def terms_kernel(number, outputs, position_ref, *refs):
    lefts, right, outs = refs[:number], refs[number], refs[number + 1 :]
    width = outs[0].shape[2]
    jobs = {}
    for out, (left, low, high, slots) in zip(outs, outputs):
        for index, slot in enumerate(slots):
            jobs.setdefault((left, slot), []).append((low, high, out, index))
    for (left, slot), parts in jobs.items():
        start = pl.multiple_of((position_ref[0] ^ slot) * width, width)
        product = dot(lefts[left][...], right[:, pl.ds(start, width)]).astype(bf16)
        for low, high, out, index in parts:
            out[index] = product[low:high]


def gradient_terms(lefts, right, position, outputs):
    count = right.shape[0]
    width = right.shape[1] // lax.axis_size("seq")
    if width % 128:
        blocked = right.reshape(count, -1, width)
        results = []
        for left, low, high, slots in outputs:
            picked = jnp.take(blocked, position ^ jnp.array(slots, jnp.int32), axis=1)
            part = jnp.einsum("at,tnb->nab", lefts[left][low:high], picked, preferred_element_type=f32)
            results.append(part.astype(bf16))
        return results
    shapes = [(len(slots), high - low, width) for _, low, high, slots in outputs]
    size = sum(n * r * w for n, r, w in shapes)
    vmem = pl.BlockSpec(memory_space=pltpu.VMEM)
    return pl.pallas_call(
        functools.partial(terms_kernel, len(lefts), outputs),
        in_specs=[pl.BlockSpec(memory_space=pltpu.SMEM)] + [vmem] * (len(lefts) + 1),
        out_specs=[vmem] * len(outputs),
        out_shape=[jax.ShapeDtypeStruct(shape, bf16) for shape in shapes],
        compiler_params=params(),
        cost_estimate=COST,
        name="gradient_terms",
    )(position[None], *lefts, right)


def sums_kernel(groups, merge, *refs):
    ins, outs = refs[: 2 * groups], refs[2 * groups :]
    low = 0
    for index in range(groups):
        keep, got = ins[2 * index], ins[2 * index + 1]
        half, rows = keep.shape[0] // 2, keep.shape[1]
        if merge:
            kept, sent = (out.at[:, low : low + rows, :] for out in outs)
            low += rows
        else:
            kept, sent = outs[2 * index], outs[2 * index + 1]
        for slot in range(half):
            kept[slot] = (keep[slot].astype(f32) + got[slot].astype(f32)).astype(bf16)
            other = half + slot
            sent[slot] = (keep[other].astype(f32) + got[other].astype(f32)).astype(bf16)


def sums(pairs, merge=False):
    slots, rows, width = pairs[0][0].shape
    total = sum(keep.shape[1] for keep, _ in pairs) if merge else rows
    shape = jax.ShapeDtypeStruct((slots // 2, total, width), bf16)
    vmem = pl.BlockSpec(memory_space=pltpu.VMEM)
    outs = 2 if merge else 2 * len(pairs)
    size = sum(keep.size for keep, _ in pairs)
    return pl.pallas_call(
        functools.partial(sums_kernel, len(pairs), merge),
        in_specs=[vmem] * (2 * len(pairs)),
        out_specs=[vmem] * outs,
        out_shape=[shape] * outs,
        compiler_params=params(),
        cost_estimate=COST,
        name="sums",
    )(*[array for pair in pairs for array in pair])


def middle_kernel(query_ref, grad_ref, mask_ref, gain_ref, state_ref, normed_t_ref, query_grad_ref, query_grad_t_ref, block_grad_ref, sent_ref):
    query = query_ref[...]
    state = state_ref[0]
    mask = mask_ref[...]
    gain = gain_ref[...].astype(f32)
    attended = dot(query, state)
    scale = lax.rsqrt(jnp.mean(attended * attended, -1, keepdims=True) + epsilon)
    unit = attended * scale
    normed_t_ref[...] = (unit * gain * mask).astype(bf16).T
    scaled = grad_ref[...] * mask * gain
    inner = jnp.mean(scaled * attended, -1, keepdims=True)
    attended_grad = (scale * scaled - attended * (scale * scale * scale) * inner).astype(bf16)
    attended_grad_t = attended_grad.T
    block_grad = dot(attended_grad_t, query)
    block_grad_ref[0] = block_grad
    sent_ref[0] = block_grad.astype(bf16)
    query_grad_ref[...] = dot_t(attended_grad, state).astype(bf16)
    query_grad_t_ref[...] = dot(state, attended_grad_t).astype(bf16)


def middle(queries, normed_grad, mask, gain, state):
    count, width = queries.shape
    heads = width // HD
    column = pl.BlockSpec((count, HD), lambda h: (0, h))
    row = pl.BlockSpec((HD, count), lambda h: (h, 0))
    square = pl.BlockSpec((1, HD, HD), lambda h: (h, 0, 0))
    return pl.pallas_call(
        middle_kernel,
        grid=(heads,),
        in_specs=[
            column,
            column,
            pl.BlockSpec((count, 1), lambda h: (0, 0)),
            pl.BlockSpec((1, HD), lambda h: (0, h)),
            square,
        ],
        out_specs=[row, column, row, square, square],
        out_shape=[
            jax.ShapeDtypeStruct((width, count), bf16),
            jax.ShapeDtypeStruct((count, width), bf16),
            jax.ShapeDtypeStruct((width, count), bf16),
            jax.ShapeDtypeStruct((heads, HD, HD), f32),
            jax.ShapeDtypeStruct((heads, HD, HD), bf16),
        ],
        compiler_params=params(),
        cost_estimate=COST,
        name="norm_backward",
    )(queries, normed_grad, mask, gain, state)


def late_kernel(mine_ref, mate_ref, other_ref, *refs):
    for side, state_ref, parts in ((0, mate_ref, refs[0:2] + refs[4:6]), (1, other_ref, refs[2:4] + refs[6:8])):
        own, got, keep, send = parts
        half = keep.shape[0]

        def times(state, block):
            return lax.dot_general(state, block, (((side,), (0,)), ((), ())), preferred_element_type=f32)

        for slot in range(2 * half):
            out = keep if slot < half else send
            for h in range(mine_ref.shape[0]):
                rows = slice(h * HD, (h + 1) * HD)
                total = times(mine_ref[h], own[slot, rows, :]) + times(state_ref[h], got[slot, rows, :])
                out[slot % half, rows, :] = total.astype(bf16)


def late_terms(mine, mate, other, value_keep, value_got, key_keep, key_got):
    slots, rows, width = value_keep.shape
    vmem = pl.BlockSpec(memory_space=pltpu.VMEM)
    shape = jax.ShapeDtypeStruct((slots // 2, rows, width), bf16)
    return pl.pallas_call(
        late_kernel,
        in_specs=[vmem] * 7,
        out_specs=[vmem] * 4,
        out_shape=[shape] * 4,
        compiler_params=params(),
        cost_estimate=COST,
        name="late_terms",
    )(mine, mate, other, value_keep, value_got, key_keep, key_got)


def key_value_kernel(key_ref, value_ref, grad_ref, key_grad_ref, value_grad_ref):
    key_grad_ref[...] = dot(value_ref[...], grad_ref[0]).astype(bf16)
    value_grad_ref[...] = dot_t(key_ref[...], grad_ref[0]).astype(bf16)


def key_value_grads(keys, values, state_grad_t):
    count, width = keys.shape
    column = pl.BlockSpec((count, HD), lambda h: (0, h))
    out = jax.ShapeDtypeStruct((count, width), bf16)
    return pl.pallas_call(
        key_value_kernel,
        grid=(width // HD,),
        in_specs=[column, column, pl.BlockSpec((1, HD, HD), lambda h: (h, 0, 0))],
        out_specs=[column, column],
        out_shape=[out, out],
        compiler_params=params(),
        cost_estimate=COST,
        name="key_value_grads",
    )(keys, values, state_grad_t)


def input_kernel(order, place_ref, query_ref, key_ref, value_ref, weight_ref, keep_ref, send_ref, held_ref):
    total = dot_t(query_ref[...], weight_ref[0])
    total += dot_t(key_ref[...], weight_ref[1])
    total += dot_t(value_ref[...], weight_ref[2])
    held_ref[...] = total.astype(bf16).reshape(held_ref.shape)
    half = len(order) // 2
    for index in range(half):
        keep_ref[index] = held_ref[place_ref[0] ^ order[index]]
        send_ref[index] = held_ref[place_ref[0] ^ order[half + index]]


def input_terms(grads, weight, place, order, chunk, chunks, tile=512):
    count, width = grads[0].shape
    half = len(order) // 2
    rows = count // len(order)
    columns = D // chunks
    first = chunk * columns // tile
    full = pl.BlockSpec((count, width), lambda i, b: (0, 0))
    out = pl.BlockSpec((half, rows, tile), lambda i, b: (0, 0, i))
    shape = jax.ShapeDtypeStruct((half, rows, columns), bf16)
    return pl.pallas_call(
        functools.partial(input_kernel, order),
        grid_spec=pltpu.PrefetchScalarGridSpec(
            num_scalar_prefetch=1,
            grid=(columns // tile,),
            in_specs=[full, full, full, pl.BlockSpec((3, tile, width), lambda i, b: (0, first + i, 0))],
            out_specs=[out, out],
            scratch_shapes=[pltpu.VMEM((len(order), rows, tile), bf16)],
        ),
        out_shape=[shape, shape],
        compiler_params=params(32),
        cost_estimate=COST,
        name="input_terms",
    )(place[None], *grads, weight)


def finish_kernel(*refs):
    out = refs[-1]
    for index in range(3):
        keep, got = refs[2 * index], refs[2 * index + 1]
        out[index] = (keep[...].astype(f32) + got[...].astype(f32)).T


def finish(pairs):
    rows, width = pairs[0].shape
    return pl.pallas_call(
        finish_kernel,
        out_shape=jax.ShapeDtypeStruct((3, width, rows), f32),
        compiler_params=params(),
        cost_estimate=COST,
        name="finish",
    )(*pairs)


def after(value, *others):
    return lax.optimization_barrier((value,) + others)[0]


def per_device(layer_input, output_grad, loss_mask, proj_weight, out_weight, norm_gain):
    position = lax.axis_index("seq")
    place = lax.axis_index("head")
    seq_bits = lax.axis_size("seq").bit_length() - 1
    head_bits = lax.axis_size("head").bit_length() - 1
    stages = list(range(seq_bits))
    bits = [(position >> bit) & 1 == 1 for bit in stages]
    order, swapped = slot_order(stages), slot_order([1, 0] + stages[2:])
    half = len(order) // 2
    head_order = slot_order(list(range(head_bits)))
    weights = jnp.transpose(proj_weight, (1, 0, 2))

    def project(rows, index):
        return jnp.dot(rows, weights[index], preferred_element_type=f32).astype(bf16)

    def terms(left, right, *parts):
        outputs = [(0, 0, left.shape[0], slots) for slots in parts]
        return gradient_terms([left], right, position, outputs)

    values = project(layer_input, 2)
    values_t = flipped(values)
    (value_send,) = terms(values_t, layer_input, order[half:])
    value_got = exchange(value_send, "seq", 0)
    keys = project(after(layer_input, value_send), 1)
    own_state, sent, keys_t = block_states(keys, values)
    mask = loss_mask.astype(f32)[:, None]

    before, total = jnp.zeros_like(own_state), own_state
    for bit in stages[1:]:
        got = exchange(sent, "seq", bit)
        if bit == 1:
            queries = project(after(layer_input, own_state), 0)
            got = after(got, queries)
        elif bit == 2:
            (key_send,) = terms(keys_t, after(layer_input, total), swapped[half:])
            normed_grad = dot_t(after(output_grad, key_send), out_weight)
            key_got = exchange(key_send, "seq", 1)
            got = after(got, normed_grad)
        before = before + jnp.where(bits[bit], got.astype(f32), 0.0)
        total = total + got.astype(f32)
        sent = total.astype(bf16)
    sent = (before + jnp.where(bits[0], 0.0, own_state)).astype(bf16)
    got = exchange(after(sent, value_got), "seq", 0)
    state = (before + got.astype(f32) + own_state).astype(bf16)

    normed_t, query_grad, query_grad_t, own_grad, sent = middle(
        queries, normed_grad, mask, norm_gain[None, :], state
    )

    got = exchange(sent, "seq", 0)
    out_keep, out_send = terms(normed_t, after(output_grad, own_grad), order[:half], order[half:])
    got = after(got, out_keep, key_got).astype(f32)
    total = own_grad + got
    mine, mate = jnp.where(bits[0], own_grad, total), jnp.where(bits[0], total, got)
    out_got = exchange(after(out_send, total), "seq", 0)

    got = exchange(jnp.stack([total, mine]).astype(bf16), "seq", 1)
    query_keep, query_send = terms(query_grad_t, after(layer_input, total), order[:half], order[half:])
    got = after(got, query_keep).astype(f32)
    later = jnp.where(bits[1], 0.0, got[0])
    mine, mate = mine + later, mate + later
    other = got[1] + jnp.where(bits[1], total, 0.0)
    total = total + got[0]
    query_got = exchange(after(query_send, total), "seq", 0)

    for bit in stages[2:]:
        got = exchange(total.astype(bf16), "seq", bit)
        if bit == 2:
            (value_keep,) = terms(values_t, after(layer_input, total), order[:half])
            (key_keep,) = terms(keys_t, after(layer_input, value_keep), swapped[:half])
            got = after(got, key_keep)
        got = got.astype(f32)
        later = jnp.where(bits[bit], 0.0, got)
        mine, mate, other = mine + later, mate + later, other + later
        total = total + got
    state_grad = mine.astype(bf16)

    value_keep, value_send, key_keep, key_send = late_terms(
        state_grad, mate.astype(bf16), other.astype(bf16), value_keep, value_got, key_keep, key_got
    )
    value_got = exchange(value_send, "seq", 1)
    key_got = exchange(key_send, "seq", 0)

    key_grad, value_grad = key_value_grads(keys, values, after(state_grad, value_keep))
    grads = (query_grad, key_grad, value_grad)
    input_keep, input_send = input_terms(grads, weights, place, head_order, 0, 1)

    def stage(keep, got, token, bit, axis="seq"):
        keep, send = sums([(keep, after(got, token))])
        return keep, exchange(send, axis, bit)

    def rest(keep, got, bits_left):
        for bit in bits_left:
            keep, got = stage(keep, got, keep, bit)
        return keep[0], got[0]

    out_keep, out_got = stage(out_keep, out_got, input_keep, 1)
    value_keep, value_got = stage(value_keep, value_got, out_keep, 2)
    input_got = exchange(after(input_send, value_keep), "head", 0)
    for bit in range(1, head_bits):
        input_keep, input_got = stage(input_keep, input_got, value_keep, bit, "head")
    query_keep, query_got = stage(query_keep, query_got, (input_keep, value_got), 1)
    out_keep, out_got = stage(out_keep, out_got, query_keep, 2)
    key_keep, key_got = stage(key_keep, key_got, out_keep, 2)
    query_keep, query_got = stage(query_keep, query_got, key_keep, 2)

    out_pair = rest(out_keep, out_got, stages[3:])
    value_pair = rest(value_keep, value_got, stages[3:])
    key_pair = rest(key_keep, key_got, stages[3:])
    query_pair = rest(query_keep, query_got, stages[3:])
    input_got = after(input_got, query_keep)
    input_grad = (input_keep[0].astype(f32) + input_got[0].astype(f32)).astype(bf16)
    out_weight_grad = out_pair[0].astype(f32) + out_pair[1].astype(f32)
    proj_weight_grad = finish(query_pair + value_pair + key_pair)
    return (input_grad, jnp.transpose(proj_weight_grad, (1, 0, 2)), out_weight_grad)


def solution(mesh):
    in_specs = (
        P("seq", None),
        P("seq", None),
        P("seq"),
        P(None, None, "head"),
        P("head", None),
        P("head"),
    )
    out_specs = (P(("seq", "head"), None), P("seq", None, "head"), P("head", "seq"))
    return jax.shard_map(
        per_device, mesh=mesh, in_specs=in_specs, out_specs=out_specs, check_vma=False
    )
```

```python
import functools

import jax
import jax.numpy as jnp
from jax import lax
from jax.experimental import pallas as pl
from jax.experimental.pallas import tpu as pltpu
from jax.sharding import PartitionSpec as P

D = 2048
HD = 128
BLOCK = 1024
epsilon = 1e-06
f32 = jnp.float32
bf16 = jnp.bfloat16
MIB = 1024 * 1024
COST = pl.CostEstimate(flops=1000000, bytes_accessed=1, transcendentals=0)


def params(mib=16):
    return pltpu.CompilerParams(vmem_limit_bytes=mib * MIB)


def dot(a, b):
    return lax.dot_general(a, b, (((1,), (0,)), ((), ())), preferred_element_type=f32)


def dot_t(a, b):
    return lax.dot_general(a, b, (((1,), (1,)), ((), ())), preferred_element_type=f32)


def exchange(arr, axis, bit):
    count = lax.axis_size(axis)
    return lax.ppermute(arr, axis, [(i, i ^ (1 << bit)) for i in range(count)])


def slot_order(stage_bits):
    order = [0]
    for bit in reversed(stage_bits):
        order = order + [slot | (1 << bit) for slot in order]
    return order


def flip_kernel(value_ref, value_t_ref):
    value_t_ref[...] = value_ref[...].T


def flipped(values):
    count, width = values.shape
    return pl.pallas_call(
        flip_kernel,
        grid=(width // HD,),
        in_specs=[pl.BlockSpec((count, HD), lambda h: (0, h))],
        out_specs=pl.BlockSpec((HD, count), lambda h: (h, 0)),
        out_shape=jax.ShapeDtypeStruct((width, count), bf16),
        compiler_params=params(),
        cost_estimate=COST,
        name="flipped",
    )(values)


def state_kernel(key_ref, value_ref, state_ref, sent_ref, key_t_ref):
    key_t = key_ref[...].T
    key_t_ref[...] = key_t
    state = dot(key_t, value_ref[...])
    state_ref[0] = state
    sent_ref[0] = state.astype(bf16)


def block_states(keys, values):
    count, width = keys.shape
    heads = width // HD
    column = pl.BlockSpec((count, HD), lambda h: (0, h))
    square = pl.BlockSpec((1, HD, HD), lambda h: (h, 0, 0))
    return pl.pallas_call(
        state_kernel,
        grid=(heads,),
        in_specs=[column, column],
        out_specs=[square, square, pl.BlockSpec((HD, count), lambda h: (h, 0))],
        out_shape=[
            jax.ShapeDtypeStruct((heads, HD, HD), f32),
            jax.ShapeDtypeStruct((heads, HD, HD), bf16),
            jax.ShapeDtypeStruct((width, count), bf16),
        ],
        compiler_params=params(),
        cost_estimate=COST,
        name="block_states",
    )(keys, values)


def terms_kernel(number, outputs, position_ref, *refs):
    lefts, right, outs = refs[:number], refs[number], refs[number + 1 :]
    width = outs[0].shape[2]
    jobs = {}
    for out, (left, low, high, slots) in zip(outs, outputs):
        for index, slot in enumerate(slots):
            jobs.setdefault((left, slot), []).append((low, high, out, index))
    for (left, slot), parts in jobs.items():
        start = pl.multiple_of((position_ref[0] ^ slot) * width, width)
        product = dot(lefts[left][...], right[:, pl.ds(start, width)]).astype(bf16)
        for low, high, out, index in parts:
            out[index] = product[low:high]


def gradient_terms(lefts, right, info, outputs):
    count = right.shape[0]
    width = right.shape[1] // lax.axis_size("seq")
    if width % 128:
        blocked = right.reshape(count, -1, width)
        results = []
        for left, low, high, slots in outputs:
            picked = jnp.take(blocked, info[0] ^ jnp.array(slots, jnp.int32), axis=1)
            part = jnp.einsum("at,tnb->nab", lefts[left][low:high], picked, preferred_element_type=f32)
            results.append(part.astype(bf16))
        return results
    shapes = [(len(slots), high - low, width) for _, low, high, slots in outputs]
    size = sum(n * r * w for n, r, w in shapes)
    vmem = pl.BlockSpec(memory_space=pltpu.VMEM)
    return pl.pallas_call(
        functools.partial(terms_kernel, len(lefts), outputs),
        in_specs=[pl.BlockSpec(memory_space=pltpu.SMEM)] + [vmem] * (len(lefts) + 1),
        out_specs=[vmem] * len(outputs),
        out_shape=[jax.ShapeDtypeStruct(shape, bf16) for shape in shapes],
        compiler_params=params(),
        cost_estimate=COST,
        name="gradient_terms",
    )(info, *lefts, right)


def sums_kernel(groups, merge, *refs):
    ins, outs = refs[: 2 * groups], refs[2 * groups :]
    low = 0
    for index in range(groups):
        keep, got = ins[2 * index], ins[2 * index + 1]
        half, rows = keep.shape[0] // 2, keep.shape[1]
        if merge:
            kept, sent = (out.at[:, low : low + rows, :] for out in outs)
            low += rows
        else:
            kept, sent = outs[2 * index], outs[2 * index + 1]
        for slot in range(half):
            kept[slot] = (keep[slot].astype(f32) + got[slot].astype(f32)).astype(bf16)
            other = half + slot
            sent[slot] = (keep[other].astype(f32) + got[other].astype(f32)).astype(bf16)


def sums(pairs, merge=False):
    slots, rows, width = pairs[0][0].shape
    total = sum(keep.shape[1] for keep, _ in pairs) if merge else rows
    shape = jax.ShapeDtypeStruct((slots // 2, total, width), bf16)
    vmem = pl.BlockSpec(memory_space=pltpu.VMEM)
    outs = 2 if merge else 2 * len(pairs)
    size = sum(keep.size for keep, _ in pairs)
    return pl.pallas_call(
        functools.partial(sums_kernel, len(pairs), merge),
        in_specs=[vmem] * (2 * len(pairs)),
        out_specs=[vmem] * outs,
        out_shape=[shape] * outs,
        compiler_params=params(),
        cost_estimate=COST,
        name="sums",
    )(*[array for pair in pairs for array in pair])


def flag(info_ref, bit):
    return ((info_ref[0] >> bit) & 1).astype(f32)


def small(kernel, info, arrays, shapes, name):
    vmem = pl.BlockSpec(memory_space=pltpu.VMEM)
    return pl.pallas_call(
        kernel,
        in_specs=[pl.BlockSpec(memory_space=pltpu.SMEM)] + [vmem] * len(arrays),
        out_specs=[vmem] * len(shapes),
        out_shape=[jax.ShapeDtypeStruct(shape, kind) for shape, kind in shapes],
        compiler_params=params(),
        cost_estimate=COST,
        name=name,
    )(info, *arrays)


def prefix_kernel(bit, first, last, info_ref, *refs):
    if first:
        own_ref, got_ref, before_ref, total_ref, sent_ref = refs
        before, total = 0.0, own_ref[...]
    else:
        own_ref, old_ref, sum_ref, got_ref, before_ref, total_ref, sent_ref = refs
        before, total = old_ref[...], sum_ref[...]
    got = got_ref[...].astype(f32)
    before = before + got * flag(info_ref, bit)
    total = total + got
    before_ref[...] = before
    total_ref[...] = total
    sent = before + own_ref[...] * (1.0 - flag(info_ref, 0)) if last else total
    sent_ref[...] = sent.astype(bf16)


def prefix_step(info, bit, first, last, own, before, total, got):
    arrays = [own, got] if first else [own, before, total, got]
    shapes = [(own.shape, f32), (own.shape, f32), (own.shape, bf16)]
    return small(functools.partial(prefix_kernel, bit, first, last), info, arrays, shapes, "prefix_step")


def suffix_first_kernel(info_ref, own_ref, got_ref, total_ref, mine_ref, mate_ref, sent_ref):
    upper = flag(info_ref, 0)
    own, got = own_ref[...], got_ref[...].astype(f32)
    total = own + got
    mine = own + got * (1.0 - upper)
    total_ref[...] = total
    mine_ref[...] = mine
    mate_ref[...] = got + own * upper
    sent_ref[0] = total.astype(bf16)
    sent_ref[1] = mine.astype(bf16)


def suffix_first(info, own, got):
    shape = own.shape
    shapes = [(shape, f32), (shape, f32), (shape, f32), ((2,) + shape, bf16)]
    return small(suffix_first_kernel, info, [own, got], shapes, "suffix_first")


def suffix_kernel(bit, info_ref, *refs):
    arrays, (total_ref, mine_ref, mate_ref, other_ref, sent_ref) = refs[:-5], refs[-5:]
    upper = flag(info_ref, bit)
    total = arrays[0][...]
    if bit == 1:
        got = arrays[3][0].astype(f32)
        other = arrays[3][1].astype(f32) + total * upper
        later = got * (1.0 - upper)
    else:
        got = arrays[4][...].astype(f32)
        later = got * (1.0 - upper)
        other = arrays[3][...] + later
    total_ref[...] = total + got
    mine_ref[...] = arrays[1][...] + later
    mate_ref[...] = arrays[2][...] + later
    other_ref[...] = other
    sent_ref[...] = (total + got).astype(bf16)


def suffix_step(info, bit, arrays):
    shape = arrays[0].shape
    shapes = [(shape, f32)] * 4 + [(shape, bf16)]
    return small(functools.partial(suffix_kernel, bit), info, arrays, shapes, "suffix_step")


def middle_kernel(query_ref, grad_ref, mask_ref, gain_ref, own_ref, before_ref, got_ref, normed_t_ref, query_grad_ref, query_grad_t_ref, block_grad_ref, sent_ref, held_ref):
    mask_row = mask_ref[...].astype(f32)

    @pl.when(pl.program_id(0) == 0)
    def _():
        held_ref[...] = jnp.broadcast_to(mask_row, held_ref.shape[::-1]).T

    query = query_ref[...]
    state = (before_ref[0] + got_ref[0].astype(f32) + own_ref[0]).astype(bf16)
    mask = held_ref[...]
    gain = gain_ref[...].astype(f32)
    attended = dot(query, state)
    scale = lax.rsqrt(jnp.mean(attended * attended, -1, keepdims=True) + epsilon)
    unit = attended * scale
    normed_t_ref[...] = (unit * gain * mask).astype(bf16).T
    scaled = grad_ref[...] * mask * gain
    inner = jnp.mean(scaled * attended, -1, keepdims=True)
    attended_grad = (scale * scaled - attended * (scale * scale * scale) * inner).astype(bf16)
    attended_grad_t = attended_grad.T
    block_grad = dot(attended_grad_t, query)
    block_grad_ref[0] = block_grad
    sent_ref[0] = block_grad.astype(bf16)
    query_grad_ref[...] = dot_t(attended_grad, state).astype(bf16)
    query_grad_t_ref[...] = dot(state, attended_grad_t).astype(bf16)


def middle(queries, normed_grad, mask, gain, own, before, got):
    count, width = queries.shape
    heads = width // HD
    column = pl.BlockSpec((count, HD), lambda h: (0, h))
    row = pl.BlockSpec((HD, count), lambda h: (h, 0))
    square = pl.BlockSpec((1, HD, HD), lambda h: (h, 0, 0))
    return pl.pallas_call(
        middle_kernel,
        grid=(heads,),
        in_specs=[
            column,
            column,
            pl.BlockSpec((1, count), lambda h: (0, 0)),
            pl.BlockSpec((1, HD), lambda h: (0, h)),
            square,
            square,
            square,
        ],
        out_specs=[row, column, row, square, square],
        out_shape=[
            jax.ShapeDtypeStruct((width, count), bf16),
            jax.ShapeDtypeStruct((count, width), bf16),
            jax.ShapeDtypeStruct((width, count), bf16),
            jax.ShapeDtypeStruct((heads, HD, HD), f32),
            jax.ShapeDtypeStruct((heads, HD, HD), bf16),
        ],
        scratch_shapes=[pltpu.VMEM((count, HD), f32)],
        compiler_params=params(),
        cost_estimate=pl.CostEstimate(
            flops=32 * count * width * HD, bytes_accessed=1, transcendentals=0
        ),
        name="norm_backward",
    )(queries, normed_grad, mask, gain, own, before, got)


def late_kernel(mine_ref, mate_ref, other_ref, *refs):
    for side, state_ref, parts in ((0, mate_ref, refs[0:2] + refs[4:6]), (1, other_ref, refs[2:4] + refs[6:8])):
        own, got, keep, send = parts
        half = keep.shape[0]

        def times(state, block):
            return lax.dot_general(state, block, (((side,), (0,)), ((), ())), preferred_element_type=f32)

        for slot in range(2 * half):
            out = keep if slot < half else send
            for h in range(mine_ref.shape[0]):
                rows = slice(h * HD, (h + 1) * HD)
                total = times(mine_ref[h].astype(bf16), own[slot, rows, :])
                total += times(state_ref[h].astype(bf16), got[slot, rows, :])
                out[slot % half, rows, :] = total.astype(bf16)


def late_terms(mine, mate, other, value_keep, value_got, key_keep, key_got):
    slots, rows, width = value_keep.shape
    vmem = pl.BlockSpec(memory_space=pltpu.VMEM)
    shape = jax.ShapeDtypeStruct((slots // 2, rows, width), bf16)
    return pl.pallas_call(
        late_kernel,
        in_specs=[vmem] * 7,
        out_specs=[vmem] * 4,
        out_shape=[shape] * 4,
        compiler_params=params(),
        cost_estimate=COST,
        name="late_terms",
    )(mine, mate, other, value_keep, value_got, key_keep, key_got)


def key_value_kernel(key_ref, value_ref, grad_ref, key_grad_ref, value_grad_ref):
    state_grad = grad_ref[0].astype(bf16)
    key_grad_ref[...] = dot(value_ref[...], state_grad).astype(bf16)
    value_grad_ref[...] = dot_t(key_ref[...], state_grad).astype(bf16)


def key_value_grads(keys, values, state_grad_t):
    count, width = keys.shape
    column = pl.BlockSpec((count, HD), lambda h: (0, h))
    out = jax.ShapeDtypeStruct((count, width), bf16)
    return pl.pallas_call(
        key_value_kernel,
        grid=(width // HD,),
        in_specs=[column, column, pl.BlockSpec((1, HD, HD), lambda h: (h, 0, 0))],
        out_specs=[column, column],
        out_shape=[out, out],
        compiler_params=params(),
        cost_estimate=COST,
        name="key_value_grads",
    )(keys, values, state_grad_t)


def input_kernel(order, place_ref, query_ref, key_ref, value_ref, weight_ref, keep_ref, send_ref, held_ref):
    total = dot_t(query_ref[...], weight_ref[0])
    total += dot_t(key_ref[...], weight_ref[1])
    total += dot_t(value_ref[...], weight_ref[2])
    held_ref[...] = total.astype(bf16).reshape(held_ref.shape)
    half = len(order) // 2
    for index in range(half):
        keep_ref[index] = held_ref[place_ref[1] ^ order[index]]
        send_ref[index] = held_ref[place_ref[1] ^ order[half + index]]


def input_terms(grads, weight, info, order, chunk, chunks, tile=512):
    count, width = grads[0].shape
    half = len(order) // 2
    rows = count // len(order)
    columns = D // chunks
    first = chunk * columns // tile
    full = pl.BlockSpec((count, width), lambda i, b: (0, 0))
    out = pl.BlockSpec((half, rows, tile), lambda i, b: (0, 0, i))
    shape = jax.ShapeDtypeStruct((half, rows, columns), bf16)
    return pl.pallas_call(
        functools.partial(input_kernel, order),
        grid_spec=pltpu.PrefetchScalarGridSpec(
            num_scalar_prefetch=1,
            grid=(columns // tile,),
            in_specs=[full, full, full, pl.BlockSpec((3, tile, width), lambda i, b: (0, first + i, 0))],
            out_specs=[out, out],
            scratch_shapes=[pltpu.VMEM((len(order), rows, tile), bf16)],
        ),
        out_shape=[shape, shape],
        compiler_params=params(20),
        cost_estimate=COST,
        name="input_terms",
    )(info, *grads, weight)


def finish_kernel(*refs):
    out = refs[-1]
    for index in range(3):
        keep, got = refs[2 * index], refs[2 * index + 1]
        out[index] = (keep[...].astype(f32) + got[...].astype(f32)).T


def finish(pairs):
    rows, width = pairs[0].shape
    return pl.pallas_call(
        finish_kernel,
        out_shape=jax.ShapeDtypeStruct((3, width, rows), f32),
        compiler_params=params(),
        cost_estimate=COST,
        name="finish",
    )(*pairs)


def after(value, *others):
    return lax.optimization_barrier((value,) + others)[0]


def per_device(layer_input, output_grad, loss_mask, proj_weight, out_weight, norm_gain):
    count = layer_input.shape[0]
    seq_bits = lax.axis_size("seq").bit_length() - 1
    head_bits = lax.axis_size("head").bit_length() - 1
    stages = list(range(seq_bits))
    order, swapped = slot_order(stages), slot_order([1, 0] + stages[2:])
    half = len(order) // 2
    head_order = slot_order(list(range(head_bits)))
    info = jnp.stack([lax.axis_index("seq"), lax.axis_index("head")]).astype(jnp.int32)
    layer_input, output_grad, loss_mask, proj_weight, norm_gain = after(
        (layer_input, output_grad, loss_mask, proj_weight, norm_gain), info
    )
    weights = jnp.transpose(proj_weight, (1, 0, 2))
    mask = loss_mask.reshape(1, count)

    def project(rows, index):
        return jnp.dot(rows, weights[index], preferred_element_type=f32).astype(bf16)

    def terms(left, right, *parts):
        outputs = [(0, 0, left.shape[0], slots) for slots in parts]
        return gradient_terms([left], right, info, outputs)

    values = project(layer_input, 2)
    values_t = flipped(values)
    (value_send,) = terms(values_t, layer_input, order[half:])
    value_got = exchange(value_send, "seq", 0)
    keys = project(after(layer_input, value_send), 1)
    own_state, sent, keys_t = block_states(keys, values)

    before, total = None, own_state
    for bit in stages[1:]:
        got = exchange(sent, "seq", bit)
        if bit == 1:
            queries = project(after(layer_input, own_state), 0)
            got = after(got, queries)
        elif bit == 2:
            (key_send,) = terms(keys_t, after(layer_input, total), swapped[half:])
            key_got = exchange(key_send, "seq", 1)
            got = after(got, key_send)
        before, total, sent = prefix_step(info, bit, bit == 1, bit == stages[-1], own_state, before, total, got)
    got = exchange(after(sent, value_got), "seq", 0)
    normed_grad = dot_t(after(output_grad, sent), out_weight)
    got = after(got, normed_grad)

    normed_t, query_grad, query_grad_t, own_grad, sent = middle(
        queries, normed_grad, mask, norm_gain[None, :], own_state, before, got
    )

    got = exchange(sent, "seq", 0)
    out_keep, out_send = terms(normed_t, after(output_grad, own_grad), order[:half], order[half:])
    got = after(got, out_keep, key_got)
    total, mine, mate, sent = suffix_first(info, own_grad, got)
    out_got = exchange(after(out_send, total), "seq", 0)

    got = exchange(sent, "seq", 1)
    query_keep, query_send = terms(query_grad_t, after(layer_input, total), order[:half], order[half:])
    got = after(got, query_keep)
    suffix = suffix_step(info, 1, [total, mine, mate, got])
    query_got = exchange(after(query_send, suffix[0]), "seq", 0)

    for bit in stages[2:]:
        got = exchange(suffix[4], "seq", bit)
        if bit == 2:
            (value_keep,) = terms(values_t, after(layer_input, suffix[0]), order[:half])
            (key_keep,) = terms(keys_t, after(layer_input, value_keep), swapped[:half])
            got = after(got, key_keep)
        suffix = suffix_step(info, bit, list(suffix[:4]) + [got])
    total, mine, mate, other, sent = suffix

    value_keep, value_send, key_keep, key_send = late_terms(
        mine, mate, other, value_keep, value_got, key_keep, key_got
    )
    value_got = exchange(value_send, "seq", 1)
    key_got = exchange(key_send, "seq", 0)

    key_grad, value_grad = key_value_grads(keys, values, after(mine, value_keep))
    grads = (query_grad, key_grad, value_grad)
    first_keep, first_send = input_terms(grads, weights, info, head_order, 0, 2)

    def stage(keep, got, token, bit, axis="seq"):
        keep, send = sums([(keep, after(got, token))])
        return keep, exchange(send, axis, bit)

    def rest(keep, got, bits_left):
        for bit in bits_left:
            keep, got = stage(keep, got, keep, bit)
        return keep[0], got[0]

    out_keep, out_got = stage(out_keep, out_got, first_keep, 1)
    second_keep, second_send = input_terms(grads, after(weights, out_keep), info, head_order, 1, 2)
    value_keep, value_got = stage(value_keep, value_got, second_keep, 2)
    first_got = exchange(after(first_send, value_keep), "head", 0)
    second_got = exchange(after(second_send, value_keep), "head", 0)
    for bit in range(1, head_bits):
        first_keep, first_got = stage(first_keep, first_got, out_got, bit, "head")
        second_keep, second_got = stage(second_keep, second_got, first_keep, bit, "head")
    out_keep, out_got = stage(out_keep, out_got, second_keep, 2)
    query_keep, query_got = stage(query_keep, query_got, (out_keep, value_got), 1)
    key_keep, key_got = stage(key_keep, key_got, (query_keep, out_got, first_got, second_got), 2)
    query_keep, query_got = stage(query_keep, query_got, key_keep, 2)

    out_pair = rest(out_keep, out_got, stages[3:])
    value_pair = rest(value_keep, value_got, stages[3:])
    key_pair = rest(key_keep, key_got, stages[3:])
    query_pair = rest(query_keep, query_got, stages[3:])
    input_grad = jnp.concatenate(
        [
            (keep[0].astype(f32) + got[0].astype(f32)).astype(bf16)
            for keep, got in ((first_keep, first_got), (second_keep, second_got))
        ],
        1,
    )
    out_weight_grad = out_pair[0].astype(f32) + out_pair[1].astype(f32)
    proj_weight_grad = finish(query_pair + value_pair + key_pair)
    return (input_grad, jnp.transpose(proj_weight_grad, (1, 0, 2)), out_weight_grad)


def solution(mesh):
    in_specs = (
        P("seq", None),
        P("seq", None),
        P("seq"),
        P(None, None, "head"),
        P("head", None),
        P("head"),
    )
    out_specs = (P(("seq", "head"), None), P("seq", None, "head"), P("head", "seq"))
    return jax.shard_map(
        per_device, mesh=mesh, in_specs=in_specs, out_specs=out_specs, check_vma=False
    )
```

```python
import functools

import jax
import jax.numpy as jnp
from jax import lax
from jax.experimental import pallas as pl
from jax.experimental.pallas import tpu as pltpu
from jax.sharding import PartitionSpec as P

D = 2048
HD = 128
BLOCK = 1024
epsilon = 1e-06
f32 = jnp.float32
bf16 = jnp.bfloat16
MIB = 1024 * 1024
COST = pl.CostEstimate(flops=1000000, bytes_accessed=1, transcendentals=0)


def params(mib=16):
    return pltpu.CompilerParams(vmem_limit_bytes=mib * MIB)


def dot(a, b):
    return lax.dot_general(a, b, (((1,), (0,)), ((), ())), preferred_element_type=f32)


def dot_t(a, b):
    return lax.dot_general(a, b, (((1,), (1,)), ((), ())), preferred_element_type=f32)


def exchange(arr, axis, bit):
    count = lax.axis_size(axis)
    return lax.ppermute(arr, axis, [(i, i ^ (1 << bit)) for i in range(count)])


def slot_order(stage_bits):
    order = [0]
    for bit in reversed(stage_bits):
        order = order + [slot | (1 << bit) for slot in order]
    return order


def state_kernel(key_ref, value_ref, state_ref, sent_ref, key_t_ref, value_t_ref):
    key_t = key_ref[...].T
    key_t_ref[...] = key_t
    value_t_ref[...] = value_ref[...].T
    state = dot(key_t, value_ref[...])
    state_ref[0] = state
    sent_ref[0] = state.astype(bf16)


def block_states(keys, values):
    count, width = keys.shape
    heads = width // HD
    column = pl.BlockSpec((count, HD), lambda h: (0, h))
    row = pl.BlockSpec((HD, count), lambda h: (h, 0))
    square = pl.BlockSpec((1, HD, HD), lambda h: (h, 0, 0))
    return pl.pallas_call(
        state_kernel,
        grid=(heads,),
        in_specs=[column, column],
        out_specs=[square, square, row, row],
        out_shape=[
            jax.ShapeDtypeStruct((heads, HD, HD), f32),
            jax.ShapeDtypeStruct((heads, HD, HD), bf16),
            jax.ShapeDtypeStruct((width, count), bf16),
            jax.ShapeDtypeStruct((width, count), bf16),
        ],
        compiler_params=params(),
        cost_estimate=COST,
        name="block_states",
    )(keys, values)


def terms_kernel(number, outputs, position_ref, *refs):
    lefts, right, outs = refs[:number], refs[number], refs[number + 1 :]
    width = outs[0].shape[2]
    jobs = {}
    for out, (left, low, high, slots) in zip(outs, outputs):
        for index, slot in enumerate(slots):
            jobs.setdefault((left, slot), []).append((low, high, out, index))
    for (left, slot), parts in jobs.items():
        start = pl.multiple_of((position_ref[0] ^ slot) * width, width)
        product = dot(lefts[left][...], right[:, pl.ds(start, width)]).astype(bf16)
        for low, high, out, index in parts:
            out[index] = product[low:high]


def gradient_terms(lefts, right, info, outputs):
    count = right.shape[0]
    width = right.shape[1] // lax.axis_size("seq")
    if width % 128:
        blocked = right.reshape(count, -1, width)
        results = []
        for left, low, high, slots in outputs:
            picked = jnp.take(blocked, info[0] ^ jnp.array(slots, jnp.int32), axis=1)
            part = jnp.einsum("at,tnb->nab", lefts[left][low:high], picked, preferred_element_type=f32)
            results.append(part.astype(bf16))
        return results
    shapes = [(len(slots), high - low, width) for _, low, high, slots in outputs]
    size = sum(n * r * w for n, r, w in shapes)
    vmem = pl.BlockSpec(memory_space=pltpu.VMEM)
    return pl.pallas_call(
        functools.partial(terms_kernel, len(lefts), outputs),
        in_specs=[pl.BlockSpec(memory_space=pltpu.SMEM)] + [vmem] * (len(lefts) + 1),
        out_specs=[vmem] * len(outputs),
        out_shape=[jax.ShapeDtypeStruct(shape, bf16) for shape in shapes],
        compiler_params=params(),
        cost_estimate=COST,
        name="gradient_terms",
    )(info, *lefts, right)


def sums_kernel(groups, merge, *refs):
    ins, outs = refs[: 2 * groups], refs[2 * groups :]
    low = 0
    for index in range(groups):
        keep, got = ins[2 * index], ins[2 * index + 1]
        half, rows = keep.shape[0] // 2, keep.shape[1]
        if merge:
            kept, sent = (out.at[:, low : low + rows, :] for out in outs)
            low += rows
        else:
            kept, sent = outs[2 * index], outs[2 * index + 1]
        for slot in range(half):
            kept[slot] = (keep[slot].astype(f32) + got[slot].astype(f32)).astype(bf16)
            other = half + slot
            sent[slot] = (keep[other].astype(f32) + got[other].astype(f32)).astype(bf16)


def sums(pairs, merge=False):
    slots, rows, width = pairs[0][0].shape
    total = sum(keep.shape[1] for keep, _ in pairs) if merge else rows
    shape = jax.ShapeDtypeStruct((slots // 2, total, width), bf16)
    vmem = pl.BlockSpec(memory_space=pltpu.VMEM)
    outs = 2 if merge else 2 * len(pairs)
    size = sum(keep.size for keep, _ in pairs)
    return pl.pallas_call(
        functools.partial(sums_kernel, len(pairs), merge),
        in_specs=[vmem] * (2 * len(pairs)),
        out_specs=[vmem] * outs,
        out_shape=[shape] * outs,
        compiler_params=params(),
        cost_estimate=COST,
        name="sums",
    )(*[array for pair in pairs for array in pair])


def flag(info_ref, bit):
    return ((info_ref[0] >> bit) & 1).astype(f32)


def small(kernel, info, arrays, shapes, name):
    vmem = pl.BlockSpec(memory_space=pltpu.VMEM)
    return pl.pallas_call(
        kernel,
        in_specs=[pl.BlockSpec(memory_space=pltpu.SMEM)] + [vmem] * len(arrays),
        out_specs=[vmem] * len(shapes),
        out_shape=[jax.ShapeDtypeStruct(shape, kind) for shape, kind in shapes],
        compiler_params=params(),
        cost_estimate=COST,
        name=name,
    )(info, *arrays)


def prefix_kernel(bit, info_ref, *refs):
    before_ref, total_ref, sent_ref = refs[-3:]
    total, got = refs[0][...], refs[1][...].astype(f32)
    before = got * flag(info_ref, bit)
    if bit:
        before += refs[2][...]
    before_ref[...] = before
    total_ref[...] = total + got
    sent_ref[...] = (total + got).astype(bf16)


def prefix_step(info, bit, arrays):
    shape = arrays[0].shape
    shapes = [(shape, f32), (shape, f32), (shape, bf16)]
    return small(functools.partial(prefix_kernel, bit), info, arrays, shapes, "prefix_step")


def suffix_first_kernel(info_ref, own_ref, got_ref, total_ref, mine_ref, mate_ref, sent_ref):
    upper = flag(info_ref, 0)
    own, got = own_ref[...], got_ref[...].astype(f32)
    total = own + got
    mine = own + got * (1.0 - upper)
    total_ref[...] = total
    mine_ref[...] = mine
    mate_ref[...] = got + own * upper
    sent_ref[0] = total.astype(bf16)
    sent_ref[1] = mine.astype(bf16)


def suffix_first(info, own, got):
    shape = own.shape
    shapes = [(shape, f32), (shape, f32), (shape, f32), ((2,) + shape, bf16)]
    return small(suffix_first_kernel, info, [own, got], shapes, "suffix_first")


def suffix_kernel(bit, info_ref, *refs):
    arrays, (total_ref, mine_ref, mate_ref, other_ref, sent_ref) = refs[:-5], refs[-5:]
    upper = flag(info_ref, bit)
    total = arrays[0][...]
    if bit == 1:
        got = arrays[3][0].astype(f32)
        other = arrays[3][1].astype(f32) + total * upper
        later = got * (1.0 - upper)
    else:
        got = arrays[4][...].astype(f32)
        later = got * (1.0 - upper)
        other = arrays[3][...] + later
    total_ref[...] = total + got
    mine_ref[...] = arrays[1][...] + later
    mate_ref[...] = arrays[2][...] + later
    other_ref[...] = other
    sent_ref[...] = (total + got).astype(bf16)


def suffix_step(info, bit, arrays):
    shape = arrays[0].shape
    shapes = [(shape, f32)] * 4 + [(shape, bf16)]
    return small(functools.partial(suffix_kernel, bit), info, arrays, shapes, "suffix_step")


def middle_kernel(query_ref, grad_ref, mask_ref, gain_ref, own_ref, before_ref, normed_t_ref, query_grad_ref, query_grad_t_ref, block_grad_ref, sent_ref, held_ref):
    mask_row = mask_ref[...].astype(f32)

    @pl.when(pl.program_id(0) == 0)
    def _():
        held_ref[...] = jnp.broadcast_to(mask_row, held_ref.shape[::-1]).T

    query = query_ref[...]
    state = (before_ref[0] + own_ref[0]).astype(bf16)
    mask = held_ref[...]
    gain = gain_ref[...].astype(f32)
    attended = dot(query, state)
    scale = lax.rsqrt(jnp.mean(attended * attended, -1, keepdims=True) + epsilon)
    unit = attended * scale
    normed_t_ref[...] = (unit * gain * mask).astype(bf16).T
    scaled = grad_ref[...] * mask * gain
    inner = jnp.mean(scaled * attended, -1, keepdims=True)
    attended_grad = (scale * scaled - attended * (scale * scale * scale) * inner).astype(bf16)
    attended_grad_t = attended_grad.T
    block_grad = dot(attended_grad_t, query)
    block_grad_ref[0] = block_grad
    sent_ref[0] = block_grad.astype(bf16)
    query_grad_ref[...] = dot_t(attended_grad, state).astype(bf16)
    query_grad_t_ref[...] = dot(state, attended_grad_t).astype(bf16)


def middle(queries, normed_grad, mask, gain, own, before):
    count, width = queries.shape
    heads = width // HD
    column = pl.BlockSpec((count, HD), lambda h: (0, h))
    row = pl.BlockSpec((HD, count), lambda h: (h, 0))
    square = pl.BlockSpec((1, HD, HD), lambda h: (h, 0, 0))
    return pl.pallas_call(
        middle_kernel,
        grid=(heads,),
        in_specs=[
            column,
            column,
            pl.BlockSpec((1, count), lambda h: (0, 0)),
            pl.BlockSpec((1, HD), lambda h: (0, h)),
            square,
            square,
        ],
        out_specs=[row, column, row, square, square],
        out_shape=[
            jax.ShapeDtypeStruct((width, count), bf16),
            jax.ShapeDtypeStruct((count, width), bf16),
            jax.ShapeDtypeStruct((width, count), bf16),
            jax.ShapeDtypeStruct((heads, HD, HD), f32),
            jax.ShapeDtypeStruct((heads, HD, HD), bf16),
        ],
        scratch_shapes=[pltpu.VMEM((count, HD), f32)],
        compiler_params=params(),
        cost_estimate=pl.CostEstimate(
            flops=64 * count * width * HD, bytes_accessed=1, transcendentals=0
        ),
        name="norm_backward",
    )(queries, normed_grad, mask, gain, own, before)


def late_kernel(mine_ref, mate_ref, other_ref, *refs):
    for side, state_ref, parts in ((0, mate_ref, refs[0:2] + refs[4:6]), (1, other_ref, refs[2:4] + refs[6:8])):
        own, got, keep, send = parts
        half = keep.shape[0]

        def times(state, block):
            return lax.dot_general(state, block, (((side,), (0,)), ((), ())), preferred_element_type=f32)

        for slot in range(2 * half):
            out = keep if slot < half else send
            for h in range(mine_ref.shape[0]):
                rows = slice(h * HD, (h + 1) * HD)
                total = times(mine_ref[h].astype(bf16), own[slot, rows, :])
                total += times(state_ref[h].astype(bf16), got[slot, rows, :])
                out[slot % half, rows, :] = total.astype(bf16)


def late_terms(mine, mate, other, value_keep, value_got, key_keep, key_got):
    slots, rows, width = value_keep.shape
    vmem = pl.BlockSpec(memory_space=pltpu.VMEM)
    shape = jax.ShapeDtypeStruct((slots // 2, rows, width), bf16)
    return pl.pallas_call(
        late_kernel,
        in_specs=[vmem] * 7,
        out_specs=[vmem] * 4,
        out_shape=[shape] * 4,
        compiler_params=params(),
        cost_estimate=COST,
        name="late_terms",
    )(mine, mate, other, value_keep, value_got, key_keep, key_got)


def key_value_kernel(key_ref, value_ref, grad_ref, key_grad_ref, value_grad_ref):
    state_grad = grad_ref[0].astype(bf16)
    key_grad_ref[...] = dot(value_ref[...], state_grad).astype(bf16)
    value_grad_ref[...] = dot_t(key_ref[...], state_grad).astype(bf16)


def key_value_grads(keys, values, state_grad_t):
    count, width = keys.shape
    column = pl.BlockSpec((count, HD), lambda h: (0, h))
    out = jax.ShapeDtypeStruct((count, width), bf16)
    return pl.pallas_call(
        key_value_kernel,
        grid=(width // HD,),
        in_specs=[column, column, pl.BlockSpec((1, HD, HD), lambda h: (h, 0, 0))],
        out_specs=[column, column],
        out_shape=[out, out],
        compiler_params=params(),
        cost_estimate=COST,
        name="key_value_grads",
    )(keys, values, state_grad_t)


def input_kernel(order, place_ref, query_ref, key_ref, value_ref, weight_ref, keep_ref, send_ref, held_ref):
    total = dot_t(query_ref[...], weight_ref[0])
    total += dot_t(key_ref[...], weight_ref[1])
    total += dot_t(value_ref[...], weight_ref[2])
    held_ref[...] = total.astype(bf16).reshape(held_ref.shape)
    half = len(order) // 2
    for index in range(half):
        keep_ref[index] = held_ref[place_ref[1] ^ order[index]]
        send_ref[index] = held_ref[place_ref[1] ^ order[half + index]]


def input_terms(grads, weight, info, order, chunk, chunks, tile=512):
    count, width = grads[0].shape
    half = len(order) // 2
    rows = count // len(order)
    columns = D // chunks
    first = chunk * columns // tile
    full = pl.BlockSpec((count, width), lambda i, b: (0, 0))
    out = pl.BlockSpec((half, rows, tile), lambda i, b: (0, 0, i))
    shape = jax.ShapeDtypeStruct((half, rows, columns), bf16)
    return pl.pallas_call(
        functools.partial(input_kernel, order),
        grid_spec=pltpu.PrefetchScalarGridSpec(
            num_scalar_prefetch=1,
            grid=(columns // tile,),
            in_specs=[full, full, full, pl.BlockSpec((3, tile, width), lambda i, b: (0, first + i, 0))],
            out_specs=[out, out],
            scratch_shapes=[pltpu.VMEM((len(order), rows, tile), bf16)],
        ),
        out_shape=[shape, shape],
        compiler_params=params(20),
        cost_estimate=COST,
        name="input_terms",
    )(info, *grads, weight)


def finish_kernel(*refs):
    out = refs[-1]
    for index in range(3):
        keep, got = refs[2 * index], refs[2 * index + 1]
        out[index] = (keep[...].astype(f32) + got[...].astype(f32)).T


def finish(pairs):
    rows, width = pairs[0].shape
    return pl.pallas_call(
        finish_kernel,
        out_shape=jax.ShapeDtypeStruct((3, width, rows), f32),
        compiler_params=params(),
        cost_estimate=COST,
        name="finish",
    )(*pairs)


def after(value, *others):
    return lax.optimization_barrier((value,) + others)[0]


def per_device(layer_input, output_grad, loss_mask, proj_weight, out_weight, norm_gain):
    count = layer_input.shape[0]
    seq_bits = lax.axis_size("seq").bit_length() - 1
    head_bits = lax.axis_size("head").bit_length() - 1
    stages = list(range(seq_bits))
    order, swapped = slot_order(stages), slot_order([1, 0] + stages[2:])
    half = len(order) // 2
    head_order = slot_order(list(range(head_bits)))
    info = jnp.stack([lax.axis_index("seq"), lax.axis_index("head")]).astype(jnp.int32)
    layer_input, output_grad, loss_mask, proj_weight, norm_gain = after(
        (layer_input, output_grad, loss_mask, proj_weight, norm_gain), info
    )
    weights = jnp.transpose(proj_weight, (1, 0, 2))
    mask = loss_mask.reshape(1, count)

    def project(rows, index):
        return jnp.dot(rows, weights[index], preferred_element_type=f32).astype(bf16)

    def terms(left, right, *parts):
        outputs = [(0, 0, left.shape[0], slots) for slots in parts]
        return gradient_terms([left], right, info, outputs)

    values = project(layer_input, 2)
    keys = project(after(layer_input, values), 1)
    own_state, sent, keys_t, values_t = block_states(keys, values)

    got = exchange(sent, "seq", 0)
    (value_send,) = terms(values_t, after(layer_input, own_state), order[half:])
    queries = project(after(layer_input, value_send), 0)
    got = after(got, queries)
    before, total, sent = prefix_step(info, 0, [own_state, got])
    value_got = exchange(after(value_send, total), "seq", 0)
    for bit in stages[1:]:
        got = exchange(sent, "seq", bit)
        if bit == 1:
            normed_grad = dot_t(after(output_grad, total), out_weight)
            got = after(got, normed_grad)
        elif bit == 2:
            (key_send,) = terms(keys_t, after(layer_input, total), swapped[half:])
            key_got = exchange(key_send, "seq", 1)
            got = after(got, key_send)
        before, total, sent = prefix_step(info, bit, [total, got, before])

    normed_t, query_grad, query_grad_t, own_grad, sent = middle(
        queries, normed_grad, mask, norm_gain[None, :], own_state, before
    )

    got = exchange(sent, "seq", 0)
    out_keep, out_send = terms(normed_t, after(output_grad, own_grad), order[:half], order[half:])
    got = after(got, out_keep, value_got)
    total, mine, mate, sent = suffix_first(info, own_grad, got)
    out_got = exchange(after(out_send, total), "seq", 0)

    got = exchange(sent, "seq", 1)
    query_keep, query_send = terms(query_grad_t, after(layer_input, total), order[:half], order[half:])
    got = after(got, query_keep, key_got)
    suffix = suffix_step(info, 1, [total, mine, mate, got])
    query_got = exchange(after(query_send, suffix[0]), "seq", 0)

    for bit in stages[2:]:
        got = exchange(suffix[4], "seq", bit)
        if bit == 2:
            (value_keep,) = terms(values_t, after(layer_input, suffix[0]), order[:half])
            (key_keep,) = terms(keys_t, after(layer_input, value_keep), swapped[:half])
            got = after(got, key_keep)
        suffix = suffix_step(info, bit, list(suffix[:4]) + [got])
    total, mine, mate, other, sent = suffix

    value_keep, value_send, key_keep, key_send = late_terms(
        mine, mate, other, value_keep, value_got, key_keep, key_got
    )
    value_got = exchange(value_send, "seq", 1)
    key_got = exchange(key_send, "seq", 0)

    key_grad, value_grad = key_value_grads(keys, values, after(mine, value_keep))
    grads = (query_grad, key_grad, value_grad)
    first_keep, first_send = input_terms(grads, weights, info, head_order, 0, 2)

    def stage(keep, got, token, bit, axis="seq"):
        keep, send = sums([(keep, after(got, token))])
        return keep, exchange(send, axis, bit)

    def rest(keep, got, bits_left):
        for bit in bits_left:
            keep, got = stage(keep, got, keep, bit)
        return keep[0], got[0]

    out_keep, out_got = stage(out_keep, out_got, first_keep, 1)
    second_keep, second_send = input_terms(grads, after(weights, out_keep), info, head_order, 1, 2)
    value_keep, value_got = stage(value_keep, value_got, second_keep, 2)
    first_got = exchange(after(first_send, value_keep), "head", 0)
    second_got = exchange(after(second_send, value_keep), "head", 0)
    query_keep, query_got = stage(query_keep, query_got, value_keep, 1)
    out_keep, out_got = stage(out_keep, out_got, (query_keep, value_got), 2)
    for bit in range(1, head_bits):
        first_keep, first_got = stage(first_keep, first_got, out_keep, bit, "head")
        second_keep, second_got = stage(second_keep, second_got, first_keep, bit, "head")
    key_keep, key_got = stage(key_keep, key_got, second_keep, 2)
    query_keep, query_got = stage(query_keep, query_got, (key_keep, out_got), 2)

    out_pair = rest(out_keep, out_got, stages[3:])
    value_pair = rest(value_keep, value_got, stages[3:])
    key_pair = rest(key_keep, key_got, stages[3:])
    query_pair = rest(query_keep, query_got, stages[3:])
    input_grad = jnp.concatenate(
        [
            (keep[0].astype(f32) + got[0].astype(f32)).astype(bf16)
            for keep, got in ((first_keep, first_got), (second_keep, second_got))
        ],
        1,
    )
    out_weight_grad = out_pair[0].astype(f32) + out_pair[1].astype(f32)
    proj_weight_grad = finish(query_pair + value_pair + key_pair)
    return (input_grad, jnp.transpose(proj_weight_grad, (1, 0, 2)), out_weight_grad)


def solution(mesh):
    in_specs = (
        P("seq", None),
        P("seq", None),
        P("seq"),
        P(None, None, "head"),
        P("head", None),
        P("head"),
    )
    out_specs = (P(("seq", "head"), None), P("seq", None, "head"), P("head", "seq"))
    return jax.shard_map(
        per_device, mesh=mesh, in_specs=in_specs, out_specs=out_specs, check_vma=False
    )
```

```python
import functools

import jax
import jax.numpy as jnp
from jax import lax
from jax.experimental import pallas as pl
from jax.experimental.pallas import tpu as pltpu
from jax.sharding import PartitionSpec as P

D = 2048
HD = 128
BLOCK = 1024
epsilon = 1e-06
f32 = jnp.float32
bf16 = jnp.bfloat16
MIB = 1024 * 1024
COST = pl.CostEstimate(flops=1000000, bytes_accessed=1, transcendentals=0)


def params(mib=16):
    return pltpu.CompilerParams(vmem_limit_bytes=mib * MIB)


def dot(a, b):
    return lax.dot_general(a, b, (((1,), (0,)), ((), ())), preferred_element_type=f32)


def dot_t(a, b):
    return lax.dot_general(a, b, (((1,), (1,)), ((), ())), preferred_element_type=f32)


def exchange(arr, axis, bit):
    count = lax.axis_size(axis)
    return lax.ppermute(arr, axis, [(i, i ^ (1 << bit)) for i in range(count)])


def slot_order(stage_bits):
    order = [0]
    for bit in reversed(stage_bits):
        order = order + [slot | (1 << bit) for slot in order]
    return order


def states_kernel(rows_ref, weight_ref, key_ref, value_ref, state_ref, sent_ref, key_t_ref, value_t_ref):
    heads = state_ref.shape[0]
    product = dot(rows_ref[...], weight_ref[0]).astype(bf16)

    @pl.when(pl.program_id(0) == 0)
    def _():
        value_ref[...] = product
        for h in range(heads):
            columns = slice(h * HD, (h + 1) * HD)
            value_t_ref[columns, :] = value_ref[:, columns].T

    @pl.when(pl.program_id(0) == 1)
    def _():
        key_ref[...] = product
        for h in range(heads):
            columns = slice(h * HD, (h + 1) * HD)
            key_t = key_ref[:, columns].T
            key_t_ref[columns, :] = key_t
            state = dot(key_t, value_ref[:, columns])
            state_ref[h] = state
            sent_ref[h] = state.astype(bf16)


def block_states(rows, weights):
    count, depth = rows.shape
    width = weights.shape[2]
    heads = width // HD
    full = pl.BlockSpec((count, width), lambda i: (0, 0))
    full_t = pl.BlockSpec((width, count), lambda i: (0, 0))
    squares = pl.BlockSpec((heads, HD, HD), lambda i: (0, 0, 0))
    return pl.pallas_call(
        states_kernel,
        grid=(2,),
        in_specs=[
            pl.BlockSpec((count, depth), lambda i: (0, 0)),
            pl.BlockSpec((1, depth, width), lambda i: (2 - i, 0, 0)),
        ],
        out_specs=[full, full, squares, squares, full_t, full_t],
        out_shape=[
            jax.ShapeDtypeStruct((count, width), bf16),
            jax.ShapeDtypeStruct((count, width), bf16),
            jax.ShapeDtypeStruct((heads, HD, HD), f32),
            jax.ShapeDtypeStruct((heads, HD, HD), bf16),
            jax.ShapeDtypeStruct((width, count), bf16),
            jax.ShapeDtypeStruct((width, count), bf16),
        ],
        compiler_params=params(32),
        cost_estimate=COST,
        name="block_states",
    )(rows, weights)


def terms_kernel(number, outputs, position_ref, *refs):
    lefts, right, outs = refs[:number], refs[number], refs[number + 1 :]
    width = outs[0].shape[2]
    jobs = {}
    for out, (left, low, high, slots) in zip(outs, outputs):
        for index, slot in enumerate(slots):
            jobs.setdefault((left, slot), []).append((low, high, out, index))
    for (left, slot), parts in jobs.items():
        start = pl.multiple_of((position_ref[0] ^ slot) * width, width)
        product = dot(lefts[left][...], right[:, pl.ds(start, width)]).astype(bf16)
        for low, high, out, index in parts:
            out[index] = product[low:high]


def gradient_terms(lefts, right, info, outputs):
    count = right.shape[0]
    width = right.shape[1] // lax.axis_size("seq")
    if width % 128:
        blocked = right.reshape(count, -1, width)
        results = []
        for left, low, high, slots in outputs:
            picked = jnp.take(blocked, info[0] ^ jnp.array(slots, jnp.int32), axis=1)
            part = jnp.einsum("at,tnb->nab", lefts[left][low:high], picked, preferred_element_type=f32)
            results.append(part.astype(bf16))
        return results
    shapes = [(len(slots), high - low, width) for _, low, high, slots in outputs]
    size = sum(n * r * w for n, r, w in shapes)
    vmem = pl.BlockSpec(memory_space=pltpu.VMEM)
    return pl.pallas_call(
        functools.partial(terms_kernel, len(lefts), outputs),
        in_specs=[pl.BlockSpec(memory_space=pltpu.SMEM)] + [vmem] * (len(lefts) + 1),
        out_specs=[vmem] * len(outputs),
        out_shape=[jax.ShapeDtypeStruct(shape, bf16) for shape in shapes],
        compiler_params=params(),
        cost_estimate=COST,
        name="gradient_terms",
    )(info, *lefts, right)


def sums_kernel(groups, merge, *refs):
    ins, outs = refs[: 2 * groups], refs[2 * groups :]
    low = 0
    for index in range(groups):
        keep, got = ins[2 * index], ins[2 * index + 1]
        half, rows = keep.shape[0] // 2, keep.shape[1]
        if merge:
            kept, sent = (out.at[:, low : low + rows, :] for out in outs)
            low += rows
        else:
            kept, sent = outs[2 * index], outs[2 * index + 1]
        for slot in range(half):
            kept[slot] = (keep[slot].astype(f32) + got[slot].astype(f32)).astype(bf16)
            other = half + slot
            sent[slot] = (keep[other].astype(f32) + got[other].astype(f32)).astype(bf16)


def sums(pairs, merge=False):
    slots, rows, width = pairs[0][0].shape
    total = sum(keep.shape[1] for keep, _ in pairs) if merge else rows
    shape = jax.ShapeDtypeStruct((slots // 2, total, width), bf16)
    vmem = pl.BlockSpec(memory_space=pltpu.VMEM)
    outs = 2 if merge else 2 * len(pairs)
    size = sum(keep.size for keep, _ in pairs)
    return pl.pallas_call(
        functools.partial(sums_kernel, len(pairs), merge),
        in_specs=[vmem] * (2 * len(pairs)),
        out_specs=[vmem] * outs,
        out_shape=[shape] * outs,
        compiler_params=params(),
        cost_estimate=COST,
        name="sums",
    )(*[array for pair in pairs for array in pair])


def flag(info_ref, bit):
    return ((info_ref[0] >> bit) & 1).astype(f32)


def small(kernel, info, arrays, shapes, name):
    vmem = pl.BlockSpec(memory_space=pltpu.VMEM)
    return pl.pallas_call(
        kernel,
        in_specs=[pl.BlockSpec(memory_space=pltpu.SMEM)] + [vmem] * len(arrays),
        out_specs=[vmem] * len(shapes),
        out_shape=[jax.ShapeDtypeStruct(shape, kind) for shape, kind in shapes],
        compiler_params=params(),
        cost_estimate=COST,
        name=name,
    )(info, *arrays)


def mark_kernel(info_ref, out_ref):
    out_ref[...] = jnp.full(out_ref.shape, flag(info_ref, 0))


def prefix_kernel(bit, info_ref, *refs):
    before_ref, total_ref, sent_ref = refs[-3:]
    total, got = refs[0][...], refs[1][...].astype(f32)
    before = got * flag(info_ref, bit)
    if bit:
        before += refs[2][...]
    before_ref[...] = before
    total_ref[...] = total + got
    sent_ref[...] = (total + got).astype(bf16)


def prefix_step(info, bit, arrays):
    shape = arrays[0].shape
    shapes = [(shape, f32), (shape, f32), (shape, bf16)]
    return small(functools.partial(prefix_kernel, bit), info, arrays, shapes, "prefix_step")


def suffix_first_kernel(info_ref, own_ref, got_ref, total_ref, mine_ref, mate_ref, sent_ref):
    upper = flag(info_ref, 0)
    own, got = own_ref[...], got_ref[...].astype(f32)
    total = own + got
    mine = own + got * (1.0 - upper)
    total_ref[...] = total
    mine_ref[...] = mine
    mate_ref[...] = got + own * upper
    sent_ref[0] = total.astype(bf16)
    sent_ref[1] = mine.astype(bf16)


def suffix_first(info, own, got):
    shape = own.shape
    shapes = [(shape, f32), (shape, f32), (shape, f32), ((2,) + shape, bf16)]
    return small(suffix_first_kernel, info, [own, got], shapes, "suffix_first")


def suffix_kernel(bit, info_ref, *refs):
    arrays, (total_ref, mine_ref, mate_ref, other_ref, sent_ref) = refs[:-5], refs[-5:]
    upper = flag(info_ref, bit)
    total = arrays[0][...]
    if bit == 1:
        got = arrays[3][0].astype(f32)
        other = arrays[3][1].astype(f32) + total * upper
        later = got * (1.0 - upper)
    else:
        got = arrays[4][...].astype(f32)
        later = got * (1.0 - upper)
        other = arrays[3][...] + later
    total_ref[...] = total + got
    mine_ref[...] = arrays[1][...] + later
    mate_ref[...] = arrays[2][...] + later
    other_ref[...] = other
    sent_ref[...] = (total + got).astype(bf16)


def suffix_step(info, bit, arrays):
    shape = arrays[0].shape
    shapes = [(shape, f32)] * 4 + [(shape, bf16)]
    return small(functools.partial(suffix_kernel, bit), info, arrays, shapes, "suffix_step")


def middle_kernel(query_ref, grad_ref, mask_ref, gain_ref, own_ref, before_ref, normed_t_ref, query_grad_ref, query_grad_t_ref, block_grad_ref, sent_ref, held_ref):
    mask_row = mask_ref[...].astype(f32)

    @pl.when(pl.program_id(0) == 0)
    def _():
        held_ref[...] = jnp.broadcast_to(mask_row, held_ref.shape[::-1]).T

    query = query_ref[...]
    state = (before_ref[0] + own_ref[0]).astype(bf16)
    mask = held_ref[...]
    gain = gain_ref[...].astype(f32)
    attended = dot(query, state)
    scale = lax.rsqrt(jnp.mean(attended * attended, -1, keepdims=True) + epsilon)
    unit = attended * scale
    normed_t_ref[...] = (unit * gain * mask).astype(bf16).T
    scaled = grad_ref[...] * mask * gain
    inner = jnp.mean(scaled * attended, -1, keepdims=True)
    attended_grad = (scale * scaled - attended * (scale * scale * scale) * inner).astype(bf16)
    attended_grad_t = attended_grad.T
    block_grad = dot(attended_grad_t, query)
    block_grad_ref[0] = block_grad
    sent_ref[0] = block_grad.astype(bf16)
    query_grad_ref[...] = dot_t(attended_grad, state).astype(bf16)
    query_grad_t_ref[...] = dot(state, attended_grad_t).astype(bf16)


def middle(queries, normed_grad, mask, gain, own, before):
    count, width = queries.shape
    heads = width // HD
    column = pl.BlockSpec((count, HD), lambda h: (0, h))
    row = pl.BlockSpec((HD, count), lambda h: (h, 0))
    square = pl.BlockSpec((1, HD, HD), lambda h: (h, 0, 0))
    return pl.pallas_call(
        middle_kernel,
        grid=(heads,),
        in_specs=[
            column,
            column,
            pl.BlockSpec((1, count), lambda h: (0, 0)),
            pl.BlockSpec((1, HD), lambda h: (0, h)),
            square,
            square,
        ],
        out_specs=[row, column, row, square, square],
        out_shape=[
            jax.ShapeDtypeStruct((width, count), bf16),
            jax.ShapeDtypeStruct((count, width), bf16),
            jax.ShapeDtypeStruct((width, count), bf16),
            jax.ShapeDtypeStruct((heads, HD, HD), f32),
            jax.ShapeDtypeStruct((heads, HD, HD), bf16),
        ],
        scratch_shapes=[pltpu.VMEM((count, HD), f32)],
        compiler_params=params(),
        cost_estimate=pl.CostEstimate(
            flops=64 * count * width * HD, bytes_accessed=1, transcendentals=0
        ),
        name="norm_backward",
    )(queries, normed_grad, mask, gain, own, before)


def late_kernel(mine_ref, mate_ref, other_ref, *refs):
    for side, state_ref, parts in ((0, mate_ref, refs[0:2] + refs[4:6]), (1, other_ref, refs[2:4] + refs[6:8])):
        own, got, keep, send = parts
        half = keep.shape[0]

        def times(state, block):
            return lax.dot_general(state, block, (((side,), (0,)), ((), ())), preferred_element_type=f32)

        for slot in range(2 * half):
            out = keep if slot < half else send
            for h in range(mine_ref.shape[0]):
                rows = slice(h * HD, (h + 1) * HD)
                total = times(mine_ref[h].astype(bf16), own[slot, rows, :])
                total += times(state_ref[h].astype(bf16), got[slot, rows, :])
                out[slot % half, rows, :] = total.astype(bf16)


def late_terms(mine, mate, other, value_keep, value_got, key_keep, key_got):
    slots, rows, width = value_keep.shape
    vmem = pl.BlockSpec(memory_space=pltpu.VMEM)
    shape = jax.ShapeDtypeStruct((slots // 2, rows, width), bf16)
    return pl.pallas_call(
        late_kernel,
        in_specs=[vmem] * 7,
        out_specs=[vmem] * 4,
        out_shape=[shape] * 4,
        compiler_params=params(),
        cost_estimate=COST,
        name="late_terms",
    )(mine, mate, other, value_keep, value_got, key_keep, key_got)


def key_value_kernel(key_ref, value_ref, grad_ref, key_grad_ref, value_grad_ref):
    state_grad = grad_ref[0].astype(bf16)
    key_grad_ref[...] = dot(value_ref[...], state_grad).astype(bf16)
    value_grad_ref[...] = dot_t(key_ref[...], state_grad).astype(bf16)


def key_value_grads(keys, values, state_grad_t):
    count, width = keys.shape
    column = pl.BlockSpec((count, HD), lambda h: (0, h))
    out = jax.ShapeDtypeStruct((count, width), bf16)
    return pl.pallas_call(
        key_value_kernel,
        grid=(width // HD,),
        in_specs=[column, column, pl.BlockSpec((1, HD, HD), lambda h: (h, 0, 0))],
        out_specs=[column, column],
        out_shape=[out, out],
        compiler_params=params(),
        cost_estimate=COST,
        name="key_value_grads",
    )(keys, values, state_grad_t)


def input_kernel(order, place_ref, query_ref, key_ref, value_ref, weight_ref, keep_ref, send_ref, held_ref):
    total = dot_t(query_ref[...], weight_ref[0])
    total += dot_t(key_ref[...], weight_ref[1])
    total += dot_t(value_ref[...], weight_ref[2])
    held_ref[...] = total.astype(bf16).reshape(held_ref.shape)
    half = len(order) // 2
    for index in range(half):
        keep_ref[index] = held_ref[place_ref[1] ^ order[index]]
        send_ref[index] = held_ref[place_ref[1] ^ order[half + index]]


def input_terms(grads, weight, info, order, chunk, chunks, tile=512):
    count, width = grads[0].shape
    half = len(order) // 2
    rows = count // len(order)
    columns = D // chunks
    first = chunk * columns // tile
    full = pl.BlockSpec((count, width), lambda i, b: (0, 0))
    out = pl.BlockSpec((half, rows, tile), lambda i, b: (0, 0, i))
    shape = jax.ShapeDtypeStruct((half, rows, columns), bf16)
    return pl.pallas_call(
        functools.partial(input_kernel, order),
        grid_spec=pltpu.PrefetchScalarGridSpec(
            num_scalar_prefetch=1,
            grid=(columns // tile,),
            in_specs=[full, full, full, pl.BlockSpec((3, tile, width), lambda i, b: (0, first + i, 0))],
            out_specs=[out, out],
            scratch_shapes=[pltpu.VMEM((len(order), rows, tile), bf16)],
        ),
        out_shape=[shape, shape],
        compiler_params=params(20),
        cost_estimate=COST,
        name="input_terms",
    )(info, *grads, weight)


def finish_kernel(query_keep_ref, query_got_ref, late_keep_ref, late_got_ref, out_ref):
    width = query_keep_ref.shape[0]
    out_ref[0] = (query_keep_ref[...].astype(f32) + query_got_ref[...].astype(f32)).T
    for index in range(2):
        rows = slice(index * width, (index + 1) * width)
        out_ref[1 + index] = (late_keep_ref[rows, :].astype(f32) + late_got_ref[rows, :].astype(f32)).T


def finish(query_keep, query_got, late_keep, late_got):
    rows, width = query_keep.shape
    return pl.pallas_call(
        finish_kernel,
        out_shape=jax.ShapeDtypeStruct((3, width, rows), f32),
        compiler_params=params(),
        cost_estimate=COST,
        name="finish",
    )(query_keep, query_got, late_keep, late_got)


def after(value, *others):
    return lax.optimization_barrier((value,) + others)[0]


def per_device(layer_input, output_grad, loss_mask, proj_weight, out_weight, norm_gain):
    count = layer_input.shape[0]
    seq_bits = lax.axis_size("seq").bit_length() - 1
    head_bits = lax.axis_size("head").bit_length() - 1
    stages = list(range(seq_bits))
    order, swapped = slot_order(stages), slot_order([1, 0] + stages[2:])
    half = len(order) // 2
    head_order = slot_order(list(range(head_bits)))
    info = jnp.stack([lax.axis_index("seq"), lax.axis_index("head")]).astype(jnp.int32)
    layer_input, output_grad, loss_mask, proj_weight, norm_gain = after(
        (layer_input, output_grad, loss_mask, proj_weight, norm_gain), info
    )
    weights = jnp.transpose(proj_weight, (1, 0, 2))
    mask = loss_mask.reshape(1, count)

    def project(rows, index):
        return jnp.dot(rows, weights[index], preferred_element_type=f32).astype(bf16)

    def terms(left, right, *parts):
        outputs = [(0, 0, left.shape[0], slots) for slots in parts]
        return gradient_terms([left], right, info, outputs)

    keys, values, own_state, sent, keys_t, values_t = block_states(layer_input, weights)

    got = exchange(sent, "seq", 0)
    (value_send,) = terms(values_t, after(layer_input, own_state), order[half:])
    queries = project(after(layer_input, value_send), 0)
    got = after(got, queries)
    before, total, sent = prefix_step(info, 0, [own_state, got])
    value_got = exchange(after(value_send, total), "seq", 0)
    for bit in stages[1:]:
        got = exchange(sent, "seq", bit)
        if bit == 1:
            normed_grad = dot_t(after(output_grad, total), out_weight)
            (key_send,) = terms(keys_t, after(layer_input, normed_grad), swapped[half:])
            got = after(got, key_send)
        elif bit == 2:
            (mark,) = small(mark_kernel, after(info, total), [], [((8, 128), f32)], "mark")
            key_got = exchange(after(key_send, mark), "seq", 1)
            got = after(got, mark)
        before, total, sent = prefix_step(info, bit, [total, got, before])

    normed_t, query_grad, query_grad_t, own_grad, sent = middle(
        queries, normed_grad, mask, norm_gain[None, :], own_state, before
    )

    got = exchange(sent, "seq", 0)
    out_keep, out_send = terms(normed_t, after(output_grad, own_grad), order[:half], order[half:])
    got = after(got, out_keep, value_got)
    total, mine, mate, sent = suffix_first(info, own_grad, got)
    out_got = exchange(after(out_send, total), "seq", 0)

    got = exchange(sent, "seq", 1)
    query_keep, query_send = terms(query_grad_t, after(layer_input, total), order[:half], order[half:])
    got = after(got, query_keep, key_got)
    suffix = suffix_step(info, 1, [total, mine, mate, got])
    query_got = exchange(after(query_send, suffix[0]), "seq", 0)

    for bit in stages[2:]:
        got = exchange(suffix[4], "seq", bit)
        if bit == 2:
            (value_keep,) = terms(values_t, after(layer_input, suffix[0]), order[:half])
            (key_keep,) = terms(keys_t, after(layer_input, value_keep), swapped[:half])
            got = after(got, key_keep)
        suffix = suffix_step(info, bit, list(suffix[:4]) + [got])
    total, mine, mate, other, sent = suffix

    value_keep, value_send, key_keep, key_send = late_terms(
        mine, mate, other, value_keep, value_got, key_keep, key_got
    )
    value_got = exchange(value_send, "seq", 1)
    key_got = exchange(key_send, "seq", 0)

    key_grad, value_grad = key_value_grads(keys, values, after(mine, value_keep))
    grads = (query_grad, key_grad, value_grad)
    input_keep, input_send = input_terms(grads, weights, info, head_order, 0, 1)

    def stage(keep, got, token, bit, axis="seq"):
        keep, send = sums([(keep, after(got, token))])
        return keep, exchange(send, axis, bit)

    def rest(keep, got, bits_left):
        for bit in bits_left:
            keep, got = stage(keep, got, keep, bit)
        return keep[0], got[0]

    value_got, key_got = after((value_got, key_got), input_keep)
    late_keep, late_send = sums([(value_keep, value_got), (key_keep, key_got)], merge=True)
    late_got = exchange(late_send, "seq", 2)
    out_keep, out_got = stage(out_keep, out_got, late_keep, 1)
    input_got = exchange(after(input_send, out_keep), "head", 0)
    for bit in range(1, head_bits):
        input_keep, input_got = stage(input_keep, input_got, out_keep, bit, "head")
    out_keep, out_got = stage(out_keep, out_got, (input_keep, late_got), 2)
    query_keep, query_got = stage(query_keep, query_got, out_keep, 1)
    query_keep, query_got = stage(query_keep, query_got, (query_keep, out_got, input_got), 2)

    out_pair = rest(out_keep, out_got, stages[3:])
    late_pair = rest(late_keep, late_got, stages[3:])
    query_pair = rest(query_keep, query_got, stages[3:])
    input_grad = (input_keep[0].astype(f32) + input_got[0].astype(f32)).astype(bf16)
    out_weight_grad = out_pair[0].astype(f32) + out_pair[1].astype(f32)
    proj_weight_grad = finish(*query_pair, *late_pair)
    return (input_grad, jnp.transpose(proj_weight_grad, (1, 0, 2)), out_weight_grad)


def solution(mesh):
    in_specs = (
        P("seq", None),
        P("seq", None),
        P("seq"),
        P(None, None, "head"),
        P("head", None),
        P("head"),
    )
    out_specs = (P(("seq", "head"), None), P("seq", None, "head"), P("head", "seq"))
    return jax.shard_map(
        per_device, mesh=mesh, in_specs=in_specs, out_specs=out_specs, check_vma=False
    )
```

```python
import functools

import jax
import jax.numpy as jnp
from jax import lax
from jax.experimental import pallas as pl
from jax.experimental.pallas import tpu as pltpu
from jax.sharding import PartitionSpec as P

D = 2048
HD = 128
BLOCK = 1024
epsilon = 1e-06
f32 = jnp.float32
bf16 = jnp.bfloat16
MIB = 1024 * 1024
COST = pl.CostEstimate(flops=1000000, bytes_accessed=1, transcendentals=0)


def params(mib=16):
    return pltpu.CompilerParams(vmem_limit_bytes=mib * MIB)


def dot(a, b):
    return lax.dot_general(a, b, (((1,), (0,)), ((), ())), preferred_element_type=f32)


def dot_t(a, b):
    return lax.dot_general(a, b, (((1,), (1,)), ((), ())), preferred_element_type=f32)


def exchange(arr, axis, bit):
    count = lax.axis_size(axis)
    return lax.ppermute(arr, axis, [(i, i ^ (1 << bit)) for i in range(count)])


def slot_order(stage_bits):
    order = [0]
    for bit in reversed(stage_bits):
        order = order + [slot | (1 << bit) for slot in order]
    return order


def states_kernel(parts, rows_ref, weight_ref, key_ref, value_ref, state_ref, sent_ref, key_t_ref, value_t_ref, copy_ref, held_ref, sems):
    heads = state_ref.shape[0]
    step = copy_ref.shape[0] // parts
    value_copy = pltpu.make_async_copy(weight_ref.at[2], held_ref.at[0], sems.at[0])
    key_copy = pltpu.make_async_copy(weight_ref.at[1], held_ref.at[1], sems.at[1])
    row_copies = []
    for part in range(parts):
        chunk = pl.ds(part * step, step)
        row_copies.append(pltpu.make_async_copy(rows_ref.at[chunk], copy_ref.at[chunk], sems.at[2 + part]))
    value_copy.start()
    for copy in row_copies:
        copy.start()
    key_copy.start()
    value_copy.wait()
    for part in range(parts):
        row_copies[part].wait()
        chunk = slice(part * step, (part + 1) * step)
        value_ref[chunk, :] = dot(copy_ref[chunk, :], held_ref[0]).astype(bf16)
    for h in range(heads):
        columns = slice(h * HD, (h + 1) * HD)
        value_t_ref[columns, :] = value_ref[:, columns].T
    key_copy.wait()
    key_ref[...] = dot(copy_ref[...], held_ref[1]).astype(bf16)
    for h in range(heads):
        columns = slice(h * HD, (h + 1) * HD)
        key_t = key_ref[:, columns].T
        key_t_ref[columns, :] = key_t
        state = dot(key_t, value_ref[:, columns])
        state_ref[h] = state
        sent_ref[h] = state.astype(bf16)


def block_states(rows, weights, parts=2):
    count, depth = rows.shape
    width = weights.shape[2]
    heads = width // HD
    hbm = pl.BlockSpec(memory_space=pltpu.HBM)
    vmem = pl.BlockSpec(memory_space=pltpu.VMEM)
    return pl.pallas_call(
        functools.partial(states_kernel, parts),
        in_specs=[hbm, hbm],
        out_specs=[vmem] * 7,
        out_shape=[
            jax.ShapeDtypeStruct((count, width), bf16),
            jax.ShapeDtypeStruct((count, width), bf16),
            jax.ShapeDtypeStruct((heads, HD, HD), f32),
            jax.ShapeDtypeStruct((heads, HD, HD), bf16),
            jax.ShapeDtypeStruct((width, count), bf16),
            jax.ShapeDtypeStruct((width, count), bf16),
            jax.ShapeDtypeStruct((count, depth), bf16),
        ],
        scratch_shapes=[pltpu.VMEM((2, depth, width), bf16), pltpu.SemaphoreType.DMA((2 + parts,))],
        compiler_params=params(44),
        cost_estimate=COST,
        name="block_states",
    )(rows, weights)


def terms_kernel(number, outputs, position_ref, *refs):
    lefts, right, outs = refs[:number], refs[number], refs[number + 1 :]
    width = outs[0].shape[2]
    jobs = {}
    for out, (left, low, high, slots) in zip(outs, outputs):
        for index, slot in enumerate(slots):
            jobs.setdefault((left, slot), []).append((low, high, out, index))
    for (left, slot), parts in jobs.items():
        start = pl.multiple_of((position_ref[0] ^ slot) * width, width)
        product = dot(lefts[left][...], right[:, pl.ds(start, width)]).astype(bf16)
        for low, high, out, index in parts:
            out[index] = product[low:high]


def gradient_terms(lefts, right, info, outputs):
    count = right.shape[0]
    width = right.shape[1] // lax.axis_size("seq")
    if width % 128:
        blocked = right.reshape(count, -1, width)
        results = []
        for left, low, high, slots in outputs:
            picked = jnp.take(blocked, info[0] ^ jnp.array(slots, jnp.int32), axis=1)
            part = jnp.einsum("at,tnb->nab", lefts[left][low:high], picked, preferred_element_type=f32)
            results.append(part.astype(bf16))
        return results
    shapes = [(len(slots), high - low, width) for _, low, high, slots in outputs]
    size = sum(n * r * w for n, r, w in shapes)
    vmem = pl.BlockSpec(memory_space=pltpu.VMEM)
    return pl.pallas_call(
        functools.partial(terms_kernel, len(lefts), outputs),
        in_specs=[pl.BlockSpec(memory_space=pltpu.SMEM)] + [vmem] * (len(lefts) + 1),
        out_specs=[vmem] * len(outputs),
        out_shape=[jax.ShapeDtypeStruct(shape, bf16) for shape in shapes],
        compiler_params=params(),
        cost_estimate=COST,
        name="gradient_terms",
    )(info, *lefts, right)


def sums_kernel(groups, merge, *refs):
    ins, outs = refs[: 2 * groups], refs[2 * groups :]
    low = 0
    for index in range(groups):
        keep, got = ins[2 * index], ins[2 * index + 1]
        half, rows = keep.shape[0] // 2, keep.shape[1]
        if merge:
            kept, sent = (out.at[:, low : low + rows, :] for out in outs)
            low += rows
        else:
            kept, sent = outs[2 * index], outs[2 * index + 1]
        for slot in range(half):
            kept[slot] = (keep[slot].astype(f32) + got[slot].astype(f32)).astype(bf16)
            other = half + slot
            sent[slot] = (keep[other].astype(f32) + got[other].astype(f32)).astype(bf16)


def sums(pairs, merge=False):
    slots, rows, width = pairs[0][0].shape
    total = sum(keep.shape[1] for keep, _ in pairs) if merge else rows
    shape = jax.ShapeDtypeStruct((slots // 2, total, width), bf16)
    vmem = pl.BlockSpec(memory_space=pltpu.VMEM)
    outs = 2 if merge else 2 * len(pairs)
    size = sum(keep.size for keep, _ in pairs)
    return pl.pallas_call(
        functools.partial(sums_kernel, len(pairs), merge),
        in_specs=[vmem] * (2 * len(pairs)),
        out_specs=[vmem] * outs,
        out_shape=[shape] * outs,
        compiler_params=params(),
        cost_estimate=COST,
        name="sums",
    )(*[array for pair in pairs for array in pair])


def flag(info_ref, bit):
    return ((info_ref[0] >> bit) & 1).astype(f32)


def small(kernel, info, arrays, shapes, name):
    vmem = pl.BlockSpec(memory_space=pltpu.VMEM)
    return pl.pallas_call(
        kernel,
        in_specs=[pl.BlockSpec(memory_space=pltpu.SMEM)] + [vmem] * len(arrays),
        out_specs=[vmem] * len(shapes),
        out_shape=[jax.ShapeDtypeStruct(shape, kind) for shape, kind in shapes],
        compiler_params=params(),
        cost_estimate=COST,
        name=name,
    )(info, *arrays)


def mark_kernel(info_ref, out_ref):
    out_ref[...] = jnp.full(out_ref.shape, flag(info_ref, 0))


def prefix_kernel(bit, info_ref, *refs):
    before_ref, total_ref, sent_ref = refs[-3:]
    total, got = refs[0][...], refs[1][...].astype(f32)
    before = got * flag(info_ref, bit)
    if bit:
        before += refs[2][...]
    before_ref[...] = before
    total_ref[...] = total + got
    sent_ref[...] = (total + got).astype(bf16)


def prefix_step(info, bit, arrays):
    shape = arrays[0].shape
    shapes = [(shape, f32), (shape, f32), (shape, bf16)]
    return small(functools.partial(prefix_kernel, bit), info, arrays, shapes, "prefix_step")


def suffix_first_kernel(info_ref, own_ref, got_ref, total_ref, mine_ref, mate_ref, sent_ref):
    upper = flag(info_ref, 0)
    own, got = own_ref[...], got_ref[...].astype(f32)
    total = own + got
    mine = own + got * (1.0 - upper)
    total_ref[...] = total
    mine_ref[...] = mine
    mate_ref[...] = got + own * upper
    sent_ref[0] = total.astype(bf16)
    sent_ref[1] = mine.astype(bf16)


def suffix_first(info, own, got):
    shape = own.shape
    shapes = [(shape, f32), (shape, f32), (shape, f32), ((2,) + shape, bf16)]
    return small(suffix_first_kernel, info, [own, got], shapes, "suffix_first")


def suffix_kernel(bit, info_ref, *refs):
    arrays, (total_ref, mine_ref, mate_ref, other_ref, sent_ref) = refs[:-5], refs[-5:]
    upper = flag(info_ref, bit)
    total = arrays[0][...]
    if bit == 1:
        got = arrays[3][0].astype(f32)
        other = arrays[3][1].astype(f32) + total * upper
        later = got * (1.0 - upper)
    else:
        got = arrays[4][...].astype(f32)
        later = got * (1.0 - upper)
        other = arrays[3][...] + later
    total_ref[...] = total + got
    mine_ref[...] = arrays[1][...] + later
    mate_ref[...] = arrays[2][...] + later
    other_ref[...] = other
    sent_ref[...] = (total + got).astype(bf16)


def suffix_step(info, bit, arrays):
    shape = arrays[0].shape
    shapes = [(shape, f32)] * 4 + [(shape, bf16)]
    return small(functools.partial(suffix_kernel, bit), info, arrays, shapes, "suffix_step")


def middle_kernel(query_ref, grad_ref, mask_ref, gain_ref, own_ref, before_ref, normed_t_ref, query_grad_ref, query_grad_t_ref, block_grad_ref, sent_ref, held_ref):
    mask_row = mask_ref[...].astype(f32)

    @pl.when(pl.program_id(0) == 0)
    def _():
        held_ref[...] = jnp.broadcast_to(mask_row, held_ref.shape[::-1]).T

    query = query_ref[...]
    state = (before_ref[0] + own_ref[0]).astype(bf16)
    mask = held_ref[...]
    gain = gain_ref[...].astype(f32)
    attended = dot(query, state)
    scale = lax.rsqrt(jnp.mean(attended * attended, -1, keepdims=True) + epsilon)
    unit = attended * scale
    normed_t_ref[...] = (unit * gain * mask).astype(bf16).T
    scaled = grad_ref[...] * mask * gain
    inner = jnp.mean(scaled * attended, -1, keepdims=True)
    attended_grad = (scale * scaled - attended * (scale * scale * scale) * inner).astype(bf16)
    attended_grad_t = attended_grad.T
    block_grad = dot(attended_grad_t, query)
    block_grad_ref[0] = block_grad
    sent_ref[0] = block_grad.astype(bf16)
    query_grad_ref[...] = dot_t(attended_grad, state).astype(bf16)
    query_grad_t_ref[...] = dot(state, attended_grad_t).astype(bf16)


def middle(queries, normed_grad, mask, gain, own, before):
    count, width = queries.shape
    heads = width // HD
    column = pl.BlockSpec((count, HD), lambda h: (0, h))
    row = pl.BlockSpec((HD, count), lambda h: (h, 0))
    square = pl.BlockSpec((1, HD, HD), lambda h: (h, 0, 0))
    return pl.pallas_call(
        middle_kernel,
        grid=(heads,),
        in_specs=[
            column,
            column,
            pl.BlockSpec((1, count), lambda h: (0, 0)),
            pl.BlockSpec((1, HD), lambda h: (0, h)),
            square,
            square,
        ],
        out_specs=[row, column, row, square, square],
        out_shape=[
            jax.ShapeDtypeStruct((width, count), bf16),
            jax.ShapeDtypeStruct((count, width), bf16),
            jax.ShapeDtypeStruct((width, count), bf16),
            jax.ShapeDtypeStruct((heads, HD, HD), f32),
            jax.ShapeDtypeStruct((heads, HD, HD), bf16),
        ],
        scratch_shapes=[pltpu.VMEM((count, HD), f32)],
        compiler_params=params(),
        cost_estimate=pl.CostEstimate(
            flops=64 * count * width * HD, bytes_accessed=1, transcendentals=0
        ),
        name="norm_backward",
    )(queries, normed_grad, mask, gain, own, before)


def late_kernel(mine_ref, mate_ref, other_ref, *refs):
    for side, state_ref, parts in ((0, mate_ref, refs[0:2] + refs[4:6]), (1, other_ref, refs[2:4] + refs[6:8])):
        own, got, keep, send = parts
        half = keep.shape[0]

        def times(state, block):
            return lax.dot_general(state, block, (((side,), (0,)), ((), ())), preferred_element_type=f32)

        for slot in range(2 * half):
            out = keep if slot < half else send
            for h in range(mine_ref.shape[0]):
                rows = slice(h * HD, (h + 1) * HD)
                total = times(mine_ref[h].astype(bf16), own[slot, rows, :])
                total += times(state_ref[h].astype(bf16), got[slot, rows, :])
                out[slot % half, rows, :] = total.astype(bf16)


def late_terms(mine, mate, other, value_keep, value_got, key_keep, key_got):
    slots, rows, width = value_keep.shape
    vmem = pl.BlockSpec(memory_space=pltpu.VMEM)
    shape = jax.ShapeDtypeStruct((slots // 2, rows, width), bf16)
    return pl.pallas_call(
        late_kernel,
        in_specs=[vmem] * 7,
        out_specs=[vmem] * 4,
        out_shape=[shape] * 4,
        compiler_params=params(),
        cost_estimate=COST,
        name="late_terms",
    )(mine, mate, other, value_keep, value_got, key_keep, key_got)


def key_value_kernel(key_ref, value_ref, grad_ref, key_grad_ref, value_grad_ref):
    state_grad = grad_ref[0].astype(bf16)
    key_grad_ref[...] = dot(value_ref[...], state_grad).astype(bf16)
    value_grad_ref[...] = dot_t(key_ref[...], state_grad).astype(bf16)


def key_value_grads(keys, values, state_grad_t):
    count, width = keys.shape
    column = pl.BlockSpec((count, HD), lambda h: (0, h))
    out = jax.ShapeDtypeStruct((count, width), bf16)
    return pl.pallas_call(
        key_value_kernel,
        grid=(width // HD,),
        in_specs=[column, column, pl.BlockSpec((1, HD, HD), lambda h: (h, 0, 0))],
        out_specs=[column, column],
        out_shape=[out, out],
        compiler_params=params(),
        cost_estimate=COST,
        name="key_value_grads",
    )(keys, values, state_grad_t)


def input_kernel(order, place_ref, query_ref, key_ref, value_ref, weight_ref, keep_ref, send_ref, held_ref):
    total = dot_t(query_ref[...], weight_ref[0])
    total += dot_t(key_ref[...], weight_ref[1])
    total += dot_t(value_ref[...], weight_ref[2])
    held_ref[...] = total.astype(bf16).reshape(held_ref.shape)
    half = len(order) // 2
    for index in range(half):
        keep_ref[index] = held_ref[place_ref[1] ^ order[index]]
        send_ref[index] = held_ref[place_ref[1] ^ order[half + index]]


def input_terms(grads, weight, info, order, chunk, chunks, tile=512):
    count, width = grads[0].shape
    half = len(order) // 2
    rows = count // len(order)
    columns = D // chunks
    first = chunk * columns // tile
    full = pl.BlockSpec((count, width), lambda i, b: (0, 0))
    out = pl.BlockSpec((half, rows, tile), lambda i, b: (0, 0, i))
    shape = jax.ShapeDtypeStruct((half, rows, columns), bf16)
    return pl.pallas_call(
        functools.partial(input_kernel, order),
        grid_spec=pltpu.PrefetchScalarGridSpec(
            num_scalar_prefetch=1,
            grid=(columns // tile,),
            in_specs=[full, full, full, pl.BlockSpec((3, tile, width), lambda i, b: (0, first + i, 0))],
            out_specs=[out, out],
            scratch_shapes=[pltpu.VMEM((len(order), rows, tile), bf16)],
        ),
        out_shape=[shape, shape],
        compiler_params=params(20),
        cost_estimate=COST,
        name="input_terms",
    )(info, *grads, weight)


def finish_kernel(query_keep_ref, query_got_ref, late_keep_ref, late_got_ref, out_ref):
    width = query_keep_ref.shape[0]
    out_ref[0] = (query_keep_ref[...].astype(f32) + query_got_ref[...].astype(f32)).T
    for index in range(2):
        rows = slice(index * width, (index + 1) * width)
        out_ref[1 + index] = (late_keep_ref[rows, :].astype(f32) + late_got_ref[rows, :].astype(f32)).T


def finish(query_keep, query_got, late_keep, late_got):
    rows, width = query_keep.shape
    return pl.pallas_call(
        finish_kernel,
        out_shape=jax.ShapeDtypeStruct((3, width, rows), f32),
        compiler_params=params(),
        cost_estimate=COST,
        name="finish",
    )(query_keep, query_got, late_keep, late_got)


def after(value, *others):
    return lax.optimization_barrier((value,) + others)[0]


def per_device(layer_input, output_grad, loss_mask, proj_weight, out_weight, norm_gain):
    count = layer_input.shape[0]
    seq_bits = lax.axis_size("seq").bit_length() - 1
    head_bits = lax.axis_size("head").bit_length() - 1
    stages = list(range(seq_bits))
    order, swapped = slot_order(stages), slot_order([1, 0] + stages[2:])
    half = len(order) // 2
    head_order = slot_order(list(range(head_bits)))
    info = jnp.stack([lax.axis_index("seq"), lax.axis_index("head")]).astype(jnp.int32)
    layer_input, output_grad, loss_mask, proj_weight, norm_gain = after(
        (layer_input, output_grad, loss_mask, proj_weight, norm_gain), info
    )
    weights = jnp.transpose(proj_weight, (1, 0, 2))
    mask = loss_mask.reshape(1, count)

    def project(rows, index):
        return jnp.dot(rows, weights[index], preferred_element_type=f32).astype(bf16)

    def terms(left, right, *parts):
        outputs = [(0, 0, left.shape[0], slots) for slots in parts]
        return gradient_terms([left], right, info, outputs)

    keys, values, own_state, sent, keys_t, values_t, layer_input = block_states(layer_input, weights)

    got = exchange(sent, "seq", 0)
    (value_send,) = terms(values_t, after(layer_input, own_state), order[half:])
    queries = project(after(layer_input, value_send), 0)
    got = after(got, queries)
    before, total, sent = prefix_step(info, 0, [own_state, got])
    value_got = exchange(after(value_send, total), "seq", 0)
    for bit in stages[1:]:
        got = exchange(sent, "seq", bit)
        if bit == 1:
            normed_grad = dot_t(after(output_grad, total), out_weight)
            (key_send,) = terms(keys_t, after(layer_input, normed_grad), swapped[half:])
            got = after(got, key_send)
        elif bit == 2:
            (mark,) = small(mark_kernel, after(info, total), [], [((8, 128), f32)], "mark")
            key_got = exchange(after(key_send, mark), "seq", 1)
            got = after(got, mark)
        before, total, sent = prefix_step(info, bit, [total, got, before])

    normed_t, query_grad, query_grad_t, own_grad, sent = middle(
        queries, normed_grad, mask, norm_gain[None, :], own_state, before
    )

    got = exchange(sent, "seq", 0)
    out_keep, out_send = terms(normed_t, after(output_grad, own_grad), order[:half], order[half:])
    got = after(got, out_keep, value_got)
    total, mine, mate, sent = suffix_first(info, own_grad, got)
    out_got = exchange(after(out_send, total), "seq", 0)

    got = exchange(sent, "seq", 1)
    query_keep, query_send = terms(query_grad_t, after(layer_input, total), order[:half], order[half:])
    got = after(got, query_keep, key_got)
    suffix = suffix_step(info, 1, [total, mine, mate, got])
    query_got = exchange(after(query_send, suffix[0]), "seq", 0)

    for bit in stages[2:]:
        got = exchange(suffix[4], "seq", bit)
        if bit == 2:
            (value_keep,) = terms(values_t, after(layer_input, suffix[0]), order[:half])
            (key_keep,) = terms(keys_t, after(layer_input, value_keep), swapped[:half])
            got = after(got, key_keep)
        suffix = suffix_step(info, bit, list(suffix[:4]) + [got])
    total, mine, mate, other, sent = suffix

    value_keep, value_send, key_keep, key_send = late_terms(
        mine, mate, other, value_keep, value_got, key_keep, key_got
    )
    value_got = exchange(value_send, "seq", 1)
    key_got = exchange(key_send, "seq", 0)

    key_grad, value_grad = key_value_grads(keys, values, after(mine, value_keep))
    grads = (query_grad, key_grad, value_grad)
    input_keep, input_send = input_terms(grads, weights, info, head_order, 0, 1)

    def stage(keep, got, token, bit, axis="seq"):
        keep, send = sums([(keep, after(got, token))])
        return keep, exchange(send, axis, bit)

    def rest(keep, got, bits_left):
        for bit in bits_left:
            keep, got = stage(keep, got, keep, bit)
        return keep[0], got[0]

    value_got, key_got = after((value_got, key_got), input_keep)
    late_keep, late_send = sums([(value_keep, value_got), (key_keep, key_got)], merge=True)
    late_got = exchange(late_send, "seq", 2)
    out_keep, out_got = stage(out_keep, out_got, late_keep, 1)
    input_got = exchange(after(input_send, out_keep), "head", 0)
    for bit in range(1, head_bits):
        input_keep, input_got = stage(input_keep, input_got, out_keep, bit, "head")
    out_keep, out_got = stage(out_keep, out_got, (input_keep, late_got), 2)
    query_keep, query_got = stage(query_keep, query_got, out_keep, 1)
    query_keep, query_got = stage(query_keep, query_got, (query_keep, out_got, input_got), 2)

    out_pair = rest(out_keep, out_got, stages[3:])
    late_pair = rest(late_keep, late_got, stages[3:])
    query_pair = rest(query_keep, query_got, stages[3:])
    input_grad = (input_keep[0].astype(f32) + input_got[0].astype(f32)).astype(bf16)
    out_weight_grad = out_pair[0].astype(f32) + out_pair[1].astype(f32)
    proj_weight_grad = finish(*query_pair, *late_pair)
    return (input_grad, jnp.transpose(proj_weight_grad, (1, 0, 2)), out_weight_grad)


def solution(mesh):
    in_specs = (
        P("seq", None),
        P("seq", None),
        P("seq"),
        P(None, None, "head"),
        P("head", None),
        P("head"),
    )
    out_specs = (P(("seq", "head"), None), P("seq", None, "head"), P("head", "seq"))
    return jax.shard_map(
        per_device, mesh=mesh, in_specs=in_specs, out_specs=out_specs, check_vma=False
    )
```

```python
import functools

import jax
import jax.numpy as jnp
from jax import lax
from jax.experimental import pallas as pl
from jax.experimental.pallas import tpu as pltpu
from jax.sharding import PartitionSpec as P

D = 2048
HD = 128
BLOCK = 1024
epsilon = 1e-06
f32 = jnp.float32
bf16 = jnp.bfloat16
MIB = 1024 * 1024
COST = pl.CostEstimate(flops=1000000, bytes_accessed=1, transcendentals=0)


def params(mib=16):
    return pltpu.CompilerParams(vmem_limit_bytes=mib * MIB)


def dot(a, b):
    return lax.dot_general(a, b, (((1,), (0,)), ((), ())), preferred_element_type=f32)


def dot_t(a, b):
    return lax.dot_general(a, b, (((1,), (1,)), ((), ())), preferred_element_type=f32)


def exchange(arr, axis, bit):
    count = lax.axis_size(axis)
    return lax.ppermute(arr, axis, [(i, i ^ (1 << bit)) for i in range(count)])


def slot_order(stage_bits):
    order = [0]
    for bit in reversed(stage_bits):
        order = order + [slot | (1 << bit) for slot in order]
    return order


def states_kernel(parts, rows_ref, weight_ref, key_ref, value_ref, state_ref, sent_ref, key_t_ref, value_t_ref, copy_ref, held_ref, sems):
    heads = state_ref.shape[0]
    step = copy_ref.shape[0] // parts
    value_copy = pltpu.make_async_copy(weight_ref.at[2], held_ref.at[0], sems.at[0])
    key_copy = pltpu.make_async_copy(weight_ref.at[1], held_ref.at[1], sems.at[1])
    row_copies = []
    for part in range(parts):
        chunk = pl.ds(part * step, step)
        row_copies.append(pltpu.make_async_copy(rows_ref.at[chunk], copy_ref.at[chunk], sems.at[2 + part]))
    value_copy.start()
    for copy in row_copies:
        copy.start()
    key_copy.start()
    value_copy.wait()
    for part in range(parts):
        row_copies[part].wait()
        chunk = slice(part * step, (part + 1) * step)
        value_ref[chunk, :] = dot(copy_ref[chunk, :], held_ref[0]).astype(bf16)
    for h in range(heads):
        columns = slice(h * HD, (h + 1) * HD)
        value_t_ref[columns, :] = value_ref[:, columns].T
    key_copy.wait()
    key_ref[...] = dot(copy_ref[...], held_ref[1]).astype(bf16)
    for h in range(heads):
        columns = slice(h * HD, (h + 1) * HD)
        key_t = key_ref[:, columns].T
        key_t_ref[columns, :] = key_t
        state = dot(key_t, value_ref[:, columns])
        state_ref[h] = state
        sent_ref[h] = state.astype(bf16)


def block_states(rows, weights, parts=2):
    count, depth = rows.shape
    width = weights.shape[2]
    heads = width // HD
    hbm = pl.BlockSpec(memory_space=pltpu.HBM)
    vmem = pl.BlockSpec(memory_space=pltpu.VMEM)
    return pl.pallas_call(
        functools.partial(states_kernel, parts),
        in_specs=[hbm, hbm],
        out_specs=[vmem] * 7,
        out_shape=[
            jax.ShapeDtypeStruct((count, width), bf16),
            jax.ShapeDtypeStruct((count, width), bf16),
            jax.ShapeDtypeStruct((heads, HD, HD), f32),
            jax.ShapeDtypeStruct((heads, HD, HD), bf16),
            jax.ShapeDtypeStruct((width, count), bf16),
            jax.ShapeDtypeStruct((width, count), bf16),
            jax.ShapeDtypeStruct((count, depth), bf16),
        ],
        scratch_shapes=[pltpu.VMEM((2, depth, width), bf16), pltpu.SemaphoreType.DMA((2 + parts,))],
        compiler_params=params(44),
        cost_estimate=COST,
        name="block_states",
    )(rows, weights)


def terms_kernel(number, outputs, position_ref, *refs):
    lefts, right, outs = refs[:number], refs[number], refs[number + 1 :]
    width = outs[0].shape[2]
    jobs = {}
    for out, (left, low, high, slots) in zip(outs, outputs):
        for index, slot in enumerate(slots):
            jobs.setdefault((left, slot), []).append((low, high, out, index))
    for (left, slot), parts in jobs.items():
        start = pl.multiple_of((position_ref[0] ^ slot) * width, width)
        product = dot(lefts[left][...], right[:, pl.ds(start, width)]).astype(bf16)
        for low, high, out, index in parts:
            out[index] = product[low:high]


def gradient_terms(lefts, right, info, outputs):
    count = right.shape[0]
    width = right.shape[1] // lax.axis_size("seq")
    if width % 128:
        blocked = right.reshape(count, -1, width)
        results = []
        for left, low, high, slots in outputs:
            picked = jnp.take(blocked, info[0] ^ jnp.array(slots, jnp.int32), axis=1)
            part = jnp.einsum("at,tnb->nab", lefts[left][low:high], picked, preferred_element_type=f32)
            results.append(part.astype(bf16))
        return results
    shapes = [(len(slots), high - low, width) for _, low, high, slots in outputs]
    size = sum(n * r * w for n, r, w in shapes)
    vmem = pl.BlockSpec(memory_space=pltpu.VMEM)
    return pl.pallas_call(
        functools.partial(terms_kernel, len(lefts), outputs),
        in_specs=[pl.BlockSpec(memory_space=pltpu.SMEM)] + [vmem] * (len(lefts) + 1),
        out_specs=[vmem] * len(outputs),
        out_shape=[jax.ShapeDtypeStruct(shape, bf16) for shape in shapes],
        compiler_params=params(),
        cost_estimate=COST,
        name="gradient_terms",
    )(info, *lefts, right)


def sums_kernel(groups, merge, *refs):
    ins, outs = refs[: 2 * groups], refs[2 * groups :]
    low = 0
    for index in range(groups):
        keep, got = ins[2 * index], ins[2 * index + 1]
        half, rows = keep.shape[0] // 2, keep.shape[1]
        if merge:
            kept, sent = (out.at[:, low : low + rows, :] for out in outs)
            low += rows
        else:
            kept, sent = outs[2 * index], outs[2 * index + 1]
        for slot in range(half):
            kept[slot] = (keep[slot].astype(f32) + got[slot].astype(f32)).astype(bf16)
            other = half + slot
            sent[slot] = (keep[other].astype(f32) + got[other].astype(f32)).astype(bf16)


def sums(pairs, merge=False):
    slots, rows, width = pairs[0][0].shape
    total = sum(keep.shape[1] for keep, _ in pairs) if merge else rows
    shape = jax.ShapeDtypeStruct((slots // 2, total, width), bf16)
    vmem = pl.BlockSpec(memory_space=pltpu.VMEM)
    outs = 2 if merge else 2 * len(pairs)
    size = sum(keep.size for keep, _ in pairs)
    return pl.pallas_call(
        functools.partial(sums_kernel, len(pairs), merge),
        in_specs=[vmem] * (2 * len(pairs)),
        out_specs=[vmem] * outs,
        out_shape=[shape] * outs,
        compiler_params=params(),
        cost_estimate=COST,
        name="sums",
    )(*[array for pair in pairs for array in pair])


def flag(info_ref, bit):
    return ((info_ref[0] >> bit) & 1).astype(f32)


def small(kernel, info, arrays, shapes, name):
    vmem = pl.BlockSpec(memory_space=pltpu.VMEM)
    return pl.pallas_call(
        kernel,
        in_specs=[pl.BlockSpec(memory_space=pltpu.SMEM)] + [vmem] * len(arrays),
        out_specs=[vmem] * len(shapes),
        out_shape=[jax.ShapeDtypeStruct(shape, kind) for shape, kind in shapes],
        compiler_params=params(),
        cost_estimate=COST,
        name=name,
    )(info, *arrays)


def mark_kernel(info_ref, out_ref):
    out_ref[...] = jnp.full(out_ref.shape, flag(info_ref, 0))


def prefix_kernel(bit, info_ref, *refs):
    before_ref, total_ref, sent_ref = refs[-3:]
    total, got = refs[0][...], refs[1][...].astype(f32)
    before = got * flag(info_ref, bit)
    if bit:
        before += refs[2][...]
    before_ref[...] = before
    total_ref[...] = total + got
    sent_ref[...] = (total + got).astype(bf16)


def prefix_step(info, bit, arrays):
    shape = arrays[0].shape
    shapes = [(shape, f32), (shape, f32), (shape, bf16)]
    return small(functools.partial(prefix_kernel, bit), info, arrays, shapes, "prefix_step")


def suffix_first_kernel(info_ref, own_ref, got_ref, total_ref, mine_ref, mate_ref, sent_ref):
    upper = flag(info_ref, 0)
    own, got = own_ref[...], got_ref[...].astype(f32)
    total = own + got
    mine = own + got * (1.0 - upper)
    total_ref[...] = total
    mine_ref[...] = mine
    mate_ref[...] = got + own * upper
    sent_ref[0] = total.astype(bf16)
    sent_ref[1] = mine.astype(bf16)


def suffix_first(info, own, got):
    shape = own.shape
    shapes = [(shape, f32), (shape, f32), (shape, f32), ((2,) + shape, bf16)]
    return small(suffix_first_kernel, info, [own, got], shapes, "suffix_first")


def suffix_kernel(bit, info_ref, *refs):
    arrays, (total_ref, mine_ref, mate_ref, other_ref, sent_ref) = refs[:-5], refs[-5:]
    upper = flag(info_ref, bit)
    total = arrays[0][...]
    if bit == 1:
        got = arrays[3][0].astype(f32)
        other = arrays[3][1].astype(f32) + total * upper
        later = got * (1.0 - upper)
    else:
        got = arrays[4][...].astype(f32)
        later = got * (1.0 - upper)
        other = arrays[3][...] + later
    total_ref[...] = total + got
    mine_ref[...] = arrays[1][...] + later
    mate_ref[...] = arrays[2][...] + later
    other_ref[...] = other
    sent_ref[...] = (total + got).astype(bf16)


def suffix_step(info, bit, arrays):
    shape = arrays[0].shape
    shapes = [(shape, f32)] * 4 + [(shape, bf16)]
    return small(functools.partial(suffix_kernel, bit), info, arrays, shapes, "suffix_step")


def middle_kernel(query_ref, grad_ref, mask_ref, gain_ref, own_ref, before_ref, normed_t_ref, query_grad_ref, query_grad_t_ref, block_grad_ref, sent_ref, held_ref):
    mask_row = mask_ref[...].astype(f32)

    @pl.when(pl.program_id(0) == 0)
    def _():
        held_ref[...] = jnp.broadcast_to(mask_row, held_ref.shape[::-1]).T

    query = query_ref[...]
    state = (before_ref[0] + own_ref[0]).astype(bf16)
    mask = held_ref[...]
    gain = gain_ref[...].astype(f32)
    attended = dot(query, state)
    scale = lax.rsqrt(jnp.mean(attended * attended, -1, keepdims=True) + epsilon)
    unit = attended * scale
    normed_t_ref[...] = (unit * gain * mask).astype(bf16).T
    scaled = grad_ref[...] * mask * gain
    inner = jnp.mean(scaled * attended, -1, keepdims=True)
    attended_grad = (scale * scaled - attended * (scale * scale * scale) * inner).astype(bf16)
    attended_grad_t = attended_grad.T
    block_grad = dot(attended_grad_t, query)
    block_grad_ref[0] = block_grad
    sent_ref[0] = block_grad.astype(bf16)
    query_grad_ref[...] = dot_t(attended_grad, state).astype(bf16)
    query_grad_t_ref[...] = dot(state, attended_grad_t).astype(bf16)


def middle(queries, normed_grad, mask, gain, own, before):
    count, width = queries.shape
    heads = width // HD
    column = pl.BlockSpec((count, HD), lambda h: (0, h))
    row = pl.BlockSpec((HD, count), lambda h: (h, 0))
    square = pl.BlockSpec((1, HD, HD), lambda h: (h, 0, 0))
    return pl.pallas_call(
        middle_kernel,
        grid=(heads,),
        in_specs=[
            column,
            column,
            pl.BlockSpec((1, count), lambda h: (0, 0)),
            pl.BlockSpec((1, HD), lambda h: (0, h)),
            square,
            square,
        ],
        out_specs=[row, column, row, square, square],
        out_shape=[
            jax.ShapeDtypeStruct((width, count), bf16),
            jax.ShapeDtypeStruct((count, width), bf16),
            jax.ShapeDtypeStruct((width, count), bf16),
            jax.ShapeDtypeStruct((heads, HD, HD), f32),
            jax.ShapeDtypeStruct((heads, HD, HD), bf16),
        ],
        scratch_shapes=[pltpu.VMEM((count, HD), f32)],
        compiler_params=params(),
        cost_estimate=pl.CostEstimate(
            flops=64 * count * width * HD, bytes_accessed=1, transcendentals=0
        ),
        name="norm_backward",
    )(queries, normed_grad, mask, gain, own, before)


def late_kernel(mine_ref, mate_ref, other_ref, *refs):
    for side, state_ref, parts in ((0, mate_ref, refs[0:2] + refs[4:6]), (1, other_ref, refs[2:4] + refs[6:8])):
        own, got, keep, send = parts
        half = keep.shape[0]

        def times(state, block):
            return lax.dot_general(state, block, (((side,), (0,)), ((), ())), preferred_element_type=f32)

        for slot in range(2 * half):
            out = keep if slot < half else send
            for h in range(mine_ref.shape[0]):
                rows = slice(h * HD, (h + 1) * HD)
                total = times(mine_ref[h].astype(bf16), own[slot, rows, :])
                total += times(state_ref[h].astype(bf16), got[slot, rows, :])
                out[slot % half, rows, :] = total.astype(bf16)


def late_terms(mine, mate, other, value_keep, value_got, key_keep, key_got):
    slots, rows, width = value_keep.shape
    vmem = pl.BlockSpec(memory_space=pltpu.VMEM)
    shape = jax.ShapeDtypeStruct((slots // 2, rows, width), bf16)
    return pl.pallas_call(
        late_kernel,
        in_specs=[vmem] * 7,
        out_specs=[vmem] * 4,
        out_shape=[shape] * 4,
        compiler_params=params(),
        cost_estimate=COST,
        name="late_terms",
    )(mine, mate, other, value_keep, value_got, key_keep, key_got)


def key_value_kernel(key_ref, value_ref, grad_ref, key_grad_ref, value_grad_ref):
    state_grad = grad_ref[0].astype(bf16)
    key_grad_ref[...] = dot(value_ref[...], state_grad).astype(bf16)
    value_grad_ref[...] = dot_t(key_ref[...], state_grad).astype(bf16)


def key_value_grads(keys, values, state_grad_t):
    count, width = keys.shape
    column = pl.BlockSpec((count, HD), lambda h: (0, h))
    out = jax.ShapeDtypeStruct((count, width), bf16)
    return pl.pallas_call(
        key_value_kernel,
        grid=(width // HD,),
        in_specs=[column, column, pl.BlockSpec((1, HD, HD), lambda h: (h, 0, 0))],
        out_specs=[column, column],
        out_shape=[out, out],
        compiler_params=params(),
        cost_estimate=COST,
        name="key_value_grads",
    )(keys, values, state_grad_t)


def input_kernel(order, place_ref, query_ref, key_ref, value_ref, weight_ref, keep_ref, send_ref, held_ref):
    total = dot_t(query_ref[...], weight_ref[0])
    total += dot_t(key_ref[...], weight_ref[1])
    total += dot_t(value_ref[...], weight_ref[2])
    held_ref[...] = total.astype(bf16).reshape(held_ref.shape)
    half = len(order) // 2
    for index in range(half):
        keep_ref[index] = held_ref[place_ref[1] ^ order[index]]
        send_ref[index] = held_ref[place_ref[1] ^ order[half + index]]


def input_terms(grads, weight, info, order, chunk, chunks, tile=512):
    count, width = grads[0].shape
    half = len(order) // 2
    rows = count // len(order)
    columns = D // chunks
    first = chunk * columns // tile
    full = pl.BlockSpec((count, width), lambda i, b: (0, 0))
    out = pl.BlockSpec((half, rows, tile), lambda i, b: (0, 0, i))
    shape = jax.ShapeDtypeStruct((half, rows, columns), bf16)
    return pl.pallas_call(
        functools.partial(input_kernel, order),
        grid_spec=pltpu.PrefetchScalarGridSpec(
            num_scalar_prefetch=1,
            grid=(columns // tile,),
            in_specs=[full, full, full, pl.BlockSpec((3, tile, width), lambda i, b: (0, first + i, 0))],
            out_specs=[out, out],
            scratch_shapes=[pltpu.VMEM((len(order), rows, tile), bf16)],
        ),
        out_shape=[shape, shape],
        compiler_params=params(20),
        cost_estimate=COST,
        name="input_terms",
    )(info, *grads, weight)


def finish_kernel(query_keep_ref, query_got_ref, late_keep_ref, late_got_ref, out_ref):
    width = query_keep_ref.shape[0]
    out_ref[0] = (query_keep_ref[...].astype(f32) + query_got_ref[...].astype(f32)).T
    for index in range(2):
        rows = slice(index * width, (index + 1) * width)
        out_ref[1 + index] = (late_keep_ref[rows, :].astype(f32) + late_got_ref[rows, :].astype(f32)).T


def finish(query_keep, query_got, late_keep, late_got):
    rows, width = query_keep.shape
    return pl.pallas_call(
        finish_kernel,
        out_shape=jax.ShapeDtypeStruct((3, width, rows), f32),
        compiler_params=params(),
        cost_estimate=COST,
        name="finish",
    )(query_keep, query_got, late_keep, late_got)


def after(value, *others):
    return lax.optimization_barrier((value,) + others)[0]


def per_device(layer_input, output_grad, loss_mask, proj_weight, out_weight, norm_gain):
    count = layer_input.shape[0]
    seq_bits = lax.axis_size("seq").bit_length() - 1
    head_bits = lax.axis_size("head").bit_length() - 1
    stages = list(range(seq_bits))
    order, swapped = slot_order(stages), slot_order([1, 0] + stages[2:])
    half = len(order) // 2
    head_order = slot_order(list(range(head_bits)))
    info = jnp.stack([lax.axis_index("seq"), lax.axis_index("head")]).astype(jnp.int32)
    layer_input, output_grad, loss_mask, proj_weight, norm_gain = after(
        (layer_input, output_grad, loss_mask, proj_weight, norm_gain), info
    )
    weights = jnp.transpose(proj_weight, (1, 0, 2))
    mask = loss_mask.reshape(1, count)

    def project(rows, index):
        return jnp.dot(rows, weights[index], preferred_element_type=f32).astype(bf16)

    def terms(left, right, *parts):
        outputs = [(0, 0, left.shape[0], slots) for slots in parts]
        return gradient_terms([left], right, info, outputs)

    side = proj_weight.shape[2] // 2

    def both_terms(left, right):
        outputs = []
        for low, slots in ((0, order), (side, swapped)):
            outputs += [(0, low, low + side, slots[:half]), (0, low, low + side, slots[half:])]
        return gradient_terms([left], right, info, outputs)

    keys, values, own_state, sent, keys_t, values_t, layer_input = block_states(layer_input, weights)

    got = exchange(sent, "seq", 0)
    (value_send,) = terms(values_t, after(layer_input, own_state), order[half:])
    queries = project(after(layer_input, value_send), 0)
    got = after(got, queries)
    before, total, sent = prefix_step(info, 0, [own_state, got])
    value_got = exchange(after(value_send, total), "seq", 0)
    for bit in stages[1:]:
        got = exchange(sent, "seq", bit)
        if bit == 1:
            normed_grad = dot_t(after(output_grad, total), out_weight)
            (key_send,) = terms(keys_t, after(layer_input, normed_grad), swapped[half:])
            got = after(got, key_send)
        elif bit == 2:
            (mark,) = small(mark_kernel, after(info, total), [], [((8, 128), f32)], "mark")
            key_got = exchange(after(key_send, mark), "seq", 1)
            got = after(got, mark)
        before, total, sent = prefix_step(info, bit, [total, got, before])

    normed_t, query_grad, query_grad_t, own_grad, sent = middle(
        queries, normed_grad, mask, norm_gain[None, :], own_state, before
    )

    got = exchange(sent, "seq", 0)
    out_keep, out_send = terms(normed_t, after(output_grad, own_grad), order[:half], order[half:])
    got = after(got, out_keep, value_got)
    total, mine, mate, sent = suffix_first(info, own_grad, got)
    out_got = exchange(after(out_send, total), "seq", 0)

    got = exchange(sent, "seq", 1)
    first_keep, first_send, second_keep, second_send = both_terms(query_grad_t, after(layer_input, total))
    got = after(got, first_keep, key_got)
    suffix = suffix_step(info, 1, [total, mine, mate, got])

    for bit in stages[2:]:
        got = exchange(suffix[4], "seq", bit)
        if bit == 2:
            (value_keep,) = terms(values_t, after(layer_input, suffix[0]), order[:half])
            second_got = exchange(after(second_send, value_keep), "seq", 1)
            (key_keep,) = terms(keys_t, after(layer_input, value_keep), swapped[:half])
            got = after(got, key_keep)
        suffix = suffix_step(info, bit, list(suffix[:4]) + [got])
    total, mine, mate, other, sent = suffix

    value_keep, value_send, key_keep, key_send = late_terms(
        mine, mate, other, value_keep, value_got, key_keep, key_got
    )
    value_got = exchange(value_send, "seq", 1)
    key_got = exchange(key_send, "seq", 0)

    key_grad, value_grad = key_value_grads(keys, values, after(mine, value_keep))
    def stage(keep, got, token, bit, axis="seq"):
        keep, send = sums([(keep, after(got, token))])
        return keep, exchange(send, axis, bit)

    def rest(keep, got, bits_left):
        for bit in bits_left:
            keep, got = stage(keep, got, keep, bit)
        return keep[0], got[0]

    second_keep, second_got = stage(second_keep, second_got, key_grad, 0)
    grads = after((query_grad, key_grad, value_grad), second_keep)
    input_keep, input_send = input_terms(grads, weights, info, head_order, 0, 1)
    value_got, key_got = after((value_got, key_got), input_keep)
    key_half = key_keep
    late_keep, late_send = sums([(value_keep, value_got), (key_keep, key_got)], merge=True)
    late_got = exchange(late_send, "seq", 2)
    out_keep, out_got = stage(out_keep, out_got, late_keep, 1)
    first_got = exchange(after(first_send, key_half), "seq", 0)
    input_got = exchange(after(input_send, out_keep), "head", 0)
    for bit in range(1, head_bits):
        input_keep, input_got = stage(input_keep, input_got, out_keep, bit, "head")
    out_keep, out_got = stage(out_keep, out_got, (input_keep, late_got), 2)
    first_keep, first_got = stage(first_keep, first_got, out_keep, 1)
    first_got = after(first_got, first_keep, out_got)
    query_keep, query_send = sums([(first_keep, first_got), (second_keep, second_got)], merge=True)
    query_got = exchange(query_send, "seq", 2)

    out_pair = rest(out_keep, out_got, stages[3:])
    late_pair = rest(late_keep, late_got, stages[3:])
    query_pair = rest(query_keep, query_got, stages[3:])
    input_grad = (input_keep[0].astype(f32) + input_got[0].astype(f32)).astype(bf16)
    out_weight_grad = out_pair[0].astype(f32) + out_pair[1].astype(f32)
    proj_weight_grad = finish(*query_pair, *late_pair)
    return (input_grad, jnp.transpose(proj_weight_grad, (1, 0, 2)), out_weight_grad)


def solution(mesh):
    in_specs = (
        P("seq", None),
        P("seq", None),
        P("seq"),
        P(None, None, "head"),
        P("head", None),
        P("head"),
    )
    out_specs = (P(("seq", "head"), None), P("seq", None, "head"), P("head", "seq"))
    return jax.shard_map(
        per_device, mesh=mesh, in_specs=in_specs, out_specs=out_specs, check_vma=False
    )
```

```python
import functools

import jax
import jax.numpy as jnp
from jax import lax
from jax.experimental import pallas as pl
from jax.experimental.pallas import tpu as pltpu
from jax.sharding import PartitionSpec as P

D = 2048
HD = 128
BLOCK = 1024
epsilon = 1e-06
f32 = jnp.float32
bf16 = jnp.bfloat16
MIB = 1024 * 1024
COST = pl.CostEstimate(flops=1000000, bytes_accessed=1, transcendentals=0)


def params(mib=16):
    return pltpu.CompilerParams(vmem_limit_bytes=mib * MIB)


def dot(a, b):
    return lax.dot_general(a, b, (((1,), (0,)), ((), ())), preferred_element_type=f32)


def dot_t(a, b):
    return lax.dot_general(a, b, (((1,), (1,)), ((), ())), preferred_element_type=f32)


def exchange(arr, axis, bit):
    count = lax.axis_size(axis)
    return lax.ppermute(arr, axis, [(i, i ^ (1 << bit)) for i in range(count)])


def slot_order(stage_bits):
    order = [0]
    for bit in reversed(stage_bits):
        order = order + [slot | (1 << bit) for slot in order]
    return order


def states_kernel(parts, rows_ref, weight_ref, key_ref, value_ref, state_ref, sent_ref, key_t_ref, value_t_ref, copy_ref, held_ref, sems):
    heads = state_ref.shape[0]
    step = copy_ref.shape[0] // parts
    value_copy = pltpu.make_async_copy(weight_ref.at[2], held_ref.at[0], sems.at[0])
    key_copy = pltpu.make_async_copy(weight_ref.at[1], held_ref.at[1], sems.at[1])
    row_copies = []
    for part in range(parts):
        chunk = pl.ds(part * step, step)
        row_copies.append(pltpu.make_async_copy(rows_ref.at[chunk], copy_ref.at[chunk], sems.at[2 + part]))
    value_copy.start()
    for copy in row_copies:
        copy.start()
    key_copy.start()
    value_copy.wait()
    for part in range(parts):
        row_copies[part].wait()
        chunk = slice(part * step, (part + 1) * step)
        value_ref[chunk, :] = dot(copy_ref[chunk, :], held_ref[0]).astype(bf16)
    for h in range(heads):
        columns = slice(h * HD, (h + 1) * HD)
        value_t_ref[columns, :] = value_ref[:, columns].T
    key_copy.wait()
    key_ref[...] = dot(copy_ref[...], held_ref[1]).astype(bf16)
    for h in range(heads):
        columns = slice(h * HD, (h + 1) * HD)
        key_t = key_ref[:, columns].T
        key_t_ref[columns, :] = key_t
        state = dot(key_t, value_ref[:, columns])
        state_ref[h] = state
        sent_ref[h] = state.astype(bf16)


def block_states(rows, weights, parts=2):
    count, depth = rows.shape
    width = weights.shape[2]
    heads = width // HD
    hbm = pl.BlockSpec(memory_space=pltpu.HBM)
    vmem = pl.BlockSpec(memory_space=pltpu.VMEM)
    return pl.pallas_call(
        functools.partial(states_kernel, parts),
        in_specs=[hbm, hbm],
        out_specs=[vmem] * 7,
        out_shape=[
            jax.ShapeDtypeStruct((count, width), bf16),
            jax.ShapeDtypeStruct((count, width), bf16),
            jax.ShapeDtypeStruct((heads, HD, HD), f32),
            jax.ShapeDtypeStruct((heads, HD, HD), bf16),
            jax.ShapeDtypeStruct((width, count), bf16),
            jax.ShapeDtypeStruct((width, count), bf16),
            jax.ShapeDtypeStruct((count, depth), bf16),
        ],
        scratch_shapes=[pltpu.VMEM((2, depth, width), bf16), pltpu.SemaphoreType.DMA((2 + parts,))],
        compiler_params=params(44),
        cost_estimate=COST,
        name="block_states",
    )(rows, weights)


def terms_kernel(number, outputs, position_ref, *refs):
    lefts, right, outs = refs[:number], refs[number], refs[number + 1 :]
    width = outs[0].shape[2]
    jobs = {}
    for out, (left, low, high, slots) in zip(outs, outputs):
        for index, slot in enumerate(slots):
            jobs.setdefault((left, slot), []).append((low, high, out, index))
    for (left, slot), parts in jobs.items():
        start = pl.multiple_of((position_ref[0] ^ slot) * width, width)
        product = dot(lefts[left][...], right[:, pl.ds(start, width)]).astype(bf16)
        for low, high, out, index in parts:
            out[index] = product[low:high]


def gradient_terms(lefts, right, info, outputs):
    count = right.shape[0]
    width = right.shape[1] // lax.axis_size("seq")
    if width % 128:
        blocked = right.reshape(count, -1, width)
        results = []
        for left, low, high, slots in outputs:
            picked = jnp.take(blocked, info[0] ^ jnp.array(slots, jnp.int32), axis=1)
            part = jnp.einsum("at,tnb->nab", lefts[left][low:high], picked, preferred_element_type=f32)
            results.append(part.astype(bf16))
        return results
    shapes = [(len(slots), high - low, width) for _, low, high, slots in outputs]
    size = sum(n * r * w for n, r, w in shapes)
    vmem = pl.BlockSpec(memory_space=pltpu.VMEM)
    return pl.pallas_call(
        functools.partial(terms_kernel, len(lefts), outputs),
        in_specs=[pl.BlockSpec(memory_space=pltpu.SMEM)] + [vmem] * (len(lefts) + 1),
        out_specs=[vmem] * len(outputs),
        out_shape=[jax.ShapeDtypeStruct(shape, bf16) for shape in shapes],
        compiler_params=params(),
        cost_estimate=COST,
        name="gradient_terms",
    )(info, *lefts, right)


def sums_kernel(groups, merge, *refs):
    ins, outs = refs[: 2 * groups], refs[2 * groups :]
    low = 0
    for index in range(groups):
        keep, got = ins[2 * index], ins[2 * index + 1]
        half, rows = keep.shape[0] // 2, keep.shape[1]
        if merge:
            kept, sent = (out.at[:, low : low + rows, :] for out in outs)
            low += rows
        else:
            kept, sent = outs[2 * index], outs[2 * index + 1]
        for slot in range(half):
            kept[slot] = (keep[slot].astype(f32) + got[slot].astype(f32)).astype(bf16)
            other = half + slot
            sent[slot] = (keep[other].astype(f32) + got[other].astype(f32)).astype(bf16)


def sums(pairs, merge=False):
    slots, rows, width = pairs[0][0].shape
    total = sum(keep.shape[1] for keep, _ in pairs) if merge else rows
    shape = jax.ShapeDtypeStruct((slots // 2, total, width), bf16)
    vmem = pl.BlockSpec(memory_space=pltpu.VMEM)
    outs = 2 if merge else 2 * len(pairs)
    size = sum(keep.size for keep, _ in pairs)
    return pl.pallas_call(
        functools.partial(sums_kernel, len(pairs), merge),
        in_specs=[vmem] * (2 * len(pairs)),
        out_specs=[vmem] * outs,
        out_shape=[shape] * outs,
        compiler_params=params(),
        cost_estimate=COST,
        name="sums",
    )(*[array for pair in pairs for array in pair])


def flag(info_ref, bit):
    return ((info_ref[0] >> bit) & 1).astype(f32)


def small(kernel, info, arrays, shapes, name, flops=1000000):
    vmem = pl.BlockSpec(memory_space=pltpu.VMEM)
    return pl.pallas_call(
        kernel,
        in_specs=[pl.BlockSpec(memory_space=pltpu.SMEM)] + [vmem] * len(arrays),
        out_specs=[vmem] * len(shapes),
        out_shape=[jax.ShapeDtypeStruct(shape, kind) for shape, kind in shapes],
        compiler_params=params(),
        cost_estimate=pl.CostEstimate(flops=flops, bytes_accessed=1, transcendentals=0),
        name=name,
    )(info, *arrays)


def mark_kernel(info_ref, out_ref):
    out_ref[...] = jnp.full(out_ref.shape, flag(info_ref, 0))


def prefix_kernel(bit, info_ref, *refs):
    before_ref, total_ref, sent_ref = refs[-3:]
    total, got = refs[0][...], refs[1][...].astype(f32)
    before = got * flag(info_ref, bit)
    if bit:
        before += refs[2][...]
    before_ref[...] = before
    total_ref[...] = total + got
    sent_ref[...] = (total + got).astype(bf16)


def prefix_step(info, bit, arrays):
    shape = arrays[0].shape
    shapes = [(shape, f32), (shape, f32), (shape, bf16)]
    return small(functools.partial(prefix_kernel, bit), info, arrays, shapes, "prefix_step")


def suffix_first_kernel(info_ref, own_ref, got_ref, total_ref, mine_ref, mate_ref, sent_ref):
    upper = flag(info_ref, 0)
    own, got = own_ref[...], got_ref[...].astype(f32)
    total = own + got
    mine = own + got * (1.0 - upper)
    total_ref[...] = total
    mine_ref[...] = mine
    mate_ref[...] = got + own * upper
    sent_ref[0] = total.astype(bf16)
    sent_ref[1] = mine.astype(bf16)


def suffix_first(info, own, got):
    shape = own.shape
    shapes = [(shape, f32), (shape, f32), (shape, f32), ((2,) + shape, bf16)]
    return small(suffix_first_kernel, info, [own, got], shapes, "suffix_first")


def suffix_kernel(bit, info_ref, *refs):
    arrays, (total_ref, mine_ref, mate_ref, other_ref, sent_ref) = refs[:-5], refs[-5:]
    upper = flag(info_ref, bit)
    total = arrays[0][...]
    if bit == 1:
        got = arrays[3][0].astype(f32)
        other = arrays[3][1].astype(f32) + total * upper
        later = got * (1.0 - upper)
    else:
        got = arrays[4][...].astype(f32)
        later = got * (1.0 - upper)
        other = arrays[3][...] + later
    total_ref[...] = total + got
    mine_ref[...] = arrays[1][...] + later
    mate_ref[...] = arrays[2][...] + later
    other_ref[...] = other
    sent_ref[...] = (total + got).astype(bf16)


def suffix_step(info, bit, arrays):
    shape = arrays[0].shape
    shapes = [(shape, f32)] * 4 + [(shape, bf16)]
    return small(functools.partial(suffix_kernel, bit), info, arrays, shapes, "suffix_step", 4000000000 if bit == 2 else 1000000)


def middle_kernel(query_ref, grad_ref, mask_ref, gain_ref, own_ref, before_ref, normed_t_ref, query_grad_ref, query_grad_t_ref, block_grad_ref, sent_ref, held_ref):
    mask_row = mask_ref[...].astype(f32)

    @pl.when(pl.program_id(0) == 0)
    def _():
        held_ref[...] = jnp.broadcast_to(mask_row, held_ref.shape[::-1]).T

    query = query_ref[...]
    state = (before_ref[0] + own_ref[0]).astype(bf16)
    mask = held_ref[...]
    gain = gain_ref[...].astype(f32)
    attended = dot(query, state)
    scale = lax.rsqrt(jnp.mean(attended * attended, -1, keepdims=True) + epsilon)
    unit = attended * scale
    normed_t_ref[...] = (unit * gain * mask).astype(bf16).T
    scaled = grad_ref[...] * mask * gain
    inner = jnp.mean(scaled * attended, -1, keepdims=True)
    attended_grad = (scale * scaled - attended * (scale * scale * scale) * inner).astype(bf16)
    attended_grad_t = attended_grad.T
    block_grad = dot(attended_grad_t, query)
    block_grad_ref[0] = block_grad
    sent_ref[0] = block_grad.astype(bf16)
    query_grad_ref[...] = dot_t(attended_grad, state).astype(bf16)
    query_grad_t_ref[...] = dot(state, attended_grad_t).astype(bf16)


def middle(queries, normed_grad, mask, gain, own, before):
    count, width = queries.shape
    heads = width // HD
    column = pl.BlockSpec((count, HD), lambda h: (0, h))
    row = pl.BlockSpec((HD, count), lambda h: (h, 0))
    square = pl.BlockSpec((1, HD, HD), lambda h: (h, 0, 0))
    return pl.pallas_call(
        middle_kernel,
        grid=(heads,),
        in_specs=[
            column,
            column,
            pl.BlockSpec((1, count), lambda h: (0, 0)),
            pl.BlockSpec((1, HD), lambda h: (0, h)),
            square,
            square,
        ],
        out_specs=[row, column, row, square, square],
        out_shape=[
            jax.ShapeDtypeStruct((width, count), bf16),
            jax.ShapeDtypeStruct((count, width), bf16),
            jax.ShapeDtypeStruct((width, count), bf16),
            jax.ShapeDtypeStruct((heads, HD, HD), f32),
            jax.ShapeDtypeStruct((heads, HD, HD), bf16),
        ],
        scratch_shapes=[pltpu.VMEM((count, HD), f32)],
        compiler_params=params(),
        cost_estimate=pl.CostEstimate(
            flops=64 * count * width * HD, bytes_accessed=1, transcendentals=0
        ),
        name="norm_backward",
    )(queries, normed_grad, mask, gain, own, before)


def late_kernel(side, cut, mine_ref, state_ref, own_ref, low_ref, high_ref, keep_ref, send_ref):
    half = keep_ref.shape[0]

    def times(state, block):
        return lax.dot_general(state, block, (((side,), (0,)), ((), ())), preferred_element_type=f32)

    for slot in range(2 * half):
        out = keep_ref if slot < half else send_ref
        for h in range(mine_ref.shape[0]):
            rows = slice(h * HD, (h + 1) * HD)
            got = low_ref[slot, rows, :] if slot < cut else high_ref[slot - cut, rows, :]
            total = times(mine_ref[h].astype(bf16), own_ref[slot, rows, :])
            total += times(state_ref[h].astype(bf16), got)
            out[slot % half, rows, :] = total.astype(bf16)


def late_terms(side, mine, state, own, low, high):
    slots, rows, width = own.shape
    vmem = pl.BlockSpec(memory_space=pltpu.VMEM)
    shape = jax.ShapeDtypeStruct((slots // 2, rows, width), bf16)
    return pl.pallas_call(
        functools.partial(late_kernel, side, low.shape[0]),
        in_specs=[vmem] * 5,
        out_specs=[vmem] * 2,
        out_shape=[shape] * 2,
        compiler_params=params(),
        cost_estimate=COST,
        name="late_terms",
    )(mine, state, own, low, high)


def key_value_kernel(key_ref, value_ref, grad_ref, key_grad_ref, value_grad_ref):
    state_grad = grad_ref[0].astype(bf16)
    key_grad_ref[...] = dot(value_ref[...], state_grad).astype(bf16)
    value_grad_ref[...] = dot_t(key_ref[...], state_grad).astype(bf16)


def key_value_grads(keys, values, state_grad_t):
    count, width = keys.shape
    column = pl.BlockSpec((count, HD), lambda h: (0, h))
    out = jax.ShapeDtypeStruct((count, width), bf16)
    return pl.pallas_call(
        key_value_kernel,
        grid=(width // HD,),
        in_specs=[column, column, pl.BlockSpec((1, HD, HD), lambda h: (h, 0, 0))],
        out_specs=[column, column],
        out_shape=[out, out],
        compiler_params=params(),
        cost_estimate=COST,
        name="key_value_grads",
    )(keys, values, state_grad_t)


def input_kernel(order, place_ref, query_ref, key_ref, value_ref, weight_ref, keep_ref, send_ref, held_ref):
    total = dot_t(query_ref[...], weight_ref[0])
    total += dot_t(key_ref[...], weight_ref[1])
    total += dot_t(value_ref[...], weight_ref[2])
    held_ref[...] = total.astype(bf16).reshape(held_ref.shape)
    half = len(order) // 2
    for index in range(half):
        keep_ref[index] = held_ref[place_ref[1] ^ order[index]]
        send_ref[index] = held_ref[place_ref[1] ^ order[half + index]]


def input_terms(grads, weight, info, order, chunk, chunks, tile=512):
    count, width = grads[0].shape
    half = len(order) // 2
    rows = count // len(order)
    columns = D // chunks
    first = chunk * columns // tile
    full = pl.BlockSpec((count, width), lambda i, b: (0, 0))
    out = pl.BlockSpec((half, rows, tile), lambda i, b: (0, 0, i))
    shape = jax.ShapeDtypeStruct((half, rows, columns), bf16)
    return pl.pallas_call(
        functools.partial(input_kernel, order),
        grid_spec=pltpu.PrefetchScalarGridSpec(
            num_scalar_prefetch=1,
            grid=(columns // tile,),
            in_specs=[full, full, full, pl.BlockSpec((3, tile, width), lambda i, b: (0, first + i, 0))],
            out_specs=[out, out],
            scratch_shapes=[pltpu.VMEM((len(order), rows, tile), bf16)],
        ),
        out_shape=[shape, shape],
        compiler_params=params(20),
        cost_estimate=COST,
        name="input_terms",
    )(info, *grads, weight)


def finish_kernel(*refs):
    out = refs[-1]
    for index in range(3):
        keep, got = refs[2 * index], refs[2 * index + 1]
        out[index] = (keep[...].astype(f32) + got[...].astype(f32)).T


def finish(*arrays):
    rows, width = arrays[0].shape
    return pl.pallas_call(
        finish_kernel,
        out_shape=jax.ShapeDtypeStruct((3, width, rows), f32),
        compiler_params=params(),
        cost_estimate=COST,
        name="finish",
    )(*arrays)


def after(value, *others):
    return lax.optimization_barrier((value,) + others)[0]


def per_device(layer_input, output_grad, loss_mask, proj_weight, out_weight, norm_gain):
    count = layer_input.shape[0]
    seq_bits = lax.axis_size("seq").bit_length() - 1
    head_bits = lax.axis_size("head").bit_length() - 1
    stages = list(range(seq_bits))
    order, swapped = slot_order(stages), slot_order([1, 0] + stages[2:])
    half = len(order) // 2
    head_order = slot_order(list(range(head_bits)))
    info = jnp.stack([lax.axis_index("seq"), lax.axis_index("head")]).astype(jnp.int32)
    layer_input, output_grad, loss_mask, proj_weight, norm_gain = after(
        (layer_input, output_grad, loss_mask, proj_weight, norm_gain), info
    )
    weights = jnp.transpose(proj_weight, (1, 0, 2))
    mask = loss_mask.reshape(1, count)

    def project(rows, index):
        return jnp.dot(rows, weights[index], preferred_element_type=f32).astype(bf16)

    def terms(left, right, *parts):
        outputs = [(0, 0, left.shape[0], slots) for slots in parts]
        return gradient_terms([left], right, info, outputs)

    keys, values, own_state, sent, keys_t, values_t, layer_input = block_states(layer_input, weights)

    got = exchange(sent, "seq", 0)
    cut = half + 3 * half // 4
    value_send, value_rest = terms(values_t, after(layer_input, own_state), order[half:cut], order[cut:])
    queries = project(after(layer_input, value_send), 0)
    got = after(got, queries)
    before, total, sent = prefix_step(info, 0, [own_state, got])
    value_got = exchange(after(value_send, total), "seq", 0)
    for bit in stages[1:]:
        got = exchange(sent, "seq", bit)
        if bit == 1:
            normed_grad = dot_t(after(output_grad, total), out_weight)
            key_send, key_rest = terms(
                keys_t, after(layer_input, normed_grad), swapped[half:cut], swapped[cut:]
            )
            got = after(got, key_send)
        elif bit == 2:
            (mark,) = small(mark_kernel, after(info, total), [], [((8, 128), f32)], "mark")
            key_got = exchange(after(key_send, mark), "seq", 1)
            got = after(got, mark)
        before, total, sent = prefix_step(info, bit, [total, got, before])

    normed_t, query_grad, query_grad_t, own_grad, sent = middle(
        queries, normed_grad, mask, norm_gain[None, :], own_state, before
    )

    got = exchange(sent, "seq", 0)
    out_keep, out_send = terms(normed_t, after(output_grad, own_grad), order[:half], order[half:])
    got = after(got, out_keep, value_got)
    total, mine, mate, sent = suffix_first(info, own_grad, got)
    value_rest = exchange(after(value_rest, total), "seq", 0)

    got = exchange(sent, "seq", 1)
    query_keep, query_send = terms(query_grad_t, after(layer_input, total), order[:half], order[half:])
    value_rest = after(value_rest, query_keep)
    out_got = exchange(after(out_send, value_rest), "seq", 0)
    got = after(got, query_keep, key_got, value_rest)
    suffix = suffix_step(info, 1, [total, mine, mate, got])
    query_got = exchange(after(query_send, suffix[0]), "seq", 0)

    for bit in stages[2:]:
        got = exchange(suffix[4], "seq", bit)
        if bit == 2:
            (value_keep,) = terms(values_t, after(layer_input, suffix[0]), order[:half])
            key_rest = exchange(after(key_rest, value_keep), "seq", 1)
            (key_keep,) = terms(keys_t, after(layer_input, value_keep), swapped[:half])
            got = after(got, key_keep)
        suffix = suffix_step(info, bit, list(suffix[:4]) + [got])
    total, mine, mate, other, sent = suffix

    value_keep, value_send = late_terms(0, mine, mate, after(value_keep, key_rest), value_got, value_rest)
    value_got = exchange(value_send, "seq", 1)
    key_grad, value_grad = key_value_grads(keys, values, after(mine, value_keep))
    key_keep, key_send = late_terms(1, mine, other, after(key_keep, key_grad), key_got, key_rest)
    key_got = exchange(key_send, "seq", 0)
    grads = after((query_grad, key_grad, value_grad), key_keep)
    grads, out_got = after((grads, out_got), key_keep)
    first_keep, first_send = input_terms(grads, weights, info, head_order, 0, 2)

    def stage(keep, got, token, bit, axis="seq"):
        keep, send = sums([(keep, after(got, token))])
        return keep, exchange(send, axis, bit)

    def rest(keep, got, bits_left):
        for bit in bits_left:
            keep, got = stage(keep, got, keep, bit)
        return keep[0], got[0]

    value_keep, value_got = stage(value_keep, value_got, first_keep, 2)
    out_keep, out_send = sums([(out_keep, after(out_got, value_keep))])
    second_keep, second_send = input_terms(grads, after(weights, out_keep), info, head_order, 1, 2)
    out_got = exchange(out_send, "seq", 1)
    key_keep, key_got = stage(key_keep, key_got, (second_keep, value_got), 2)
    first_got = exchange(after(first_send, key_keep), "head", 0)
    second_got = exchange(after(second_send, key_keep), "head", 0)
    for bit in range(1, head_bits):
        first_keep, first_got = stage(first_keep, first_got, key_keep, bit, "head")
        second_keep, second_got = stage(second_keep, second_got, first_keep, bit, "head")
    out_keep, out_got = stage(out_keep, out_got, second_keep, 2)
    query_keep, query_got = stage(query_keep, query_got, (out_keep, key_got), 1)
    query_keep, query_got = stage(query_keep, query_got, (query_keep, out_got), 2)

    out_pair = rest(out_keep, out_got, stages[3:])
    value_pair = rest(value_keep, value_got, stages[3:])
    key_pair = rest(key_keep, key_got, stages[3:])
    query_pair = rest(query_keep, query_got, stages[3:])
    input_grad = jnp.concatenate(
        [
            (keep[0].astype(f32) + got[0].astype(f32)).astype(bf16)
            for keep, got in ((first_keep, first_got), (second_keep, second_got))
        ],
        1,
    )
    out_weight_grad = out_pair[0].astype(f32) + out_pair[1].astype(f32)
    proj_weight_grad = finish(*query_pair, *value_pair, *key_pair)
    return (input_grad, jnp.transpose(proj_weight_grad, (1, 0, 2)), out_weight_grad)


def solution(mesh):
    in_specs = (
        P("seq", None),
        P("seq", None),
        P("seq"),
        P(None, None, "head"),
        P("head", None),
        P("head"),
    )
    out_specs = (P(("seq", "head"), None), P("seq", None, "head"), P("head", "seq"))
    return jax.shard_map(
        per_device, mesh=mesh, in_specs=in_specs, out_specs=out_specs, check_vma=False
    )
```

```python
import functools

import jax
import jax.numpy as jnp
from jax import lax
from jax.experimental import pallas as pl
from jax.experimental.pallas import tpu as pltpu
from jax.sharding import PartitionSpec as P

D = 2048
HD = 128
BLOCK = 1024
epsilon = 1e-06
f32 = jnp.float32
bf16 = jnp.bfloat16
MIB = 1024 * 1024
COST = pl.CostEstimate(flops=1000000, bytes_accessed=1, transcendentals=0)


def params(mib=16):
    return pltpu.CompilerParams(vmem_limit_bytes=mib * MIB)


def dot(a, b):
    return lax.dot_general(a, b, (((1,), (0,)), ((), ())), preferred_element_type=f32)


def dot_t(a, b):
    return lax.dot_general(a, b, (((1,), (1,)), ((), ())), preferred_element_type=f32)


def exchange(arr, axis, bit):
    count = lax.axis_size(axis)
    return lax.ppermute(arr, axis, [(i, i ^ (1 << bit)) for i in range(count)])


def slot_order(stage_bits):
    order = [0]
    for bit in reversed(stage_bits):
        order = order + [slot | (1 << bit) for slot in order]
    return order


def states_kernel(parts, rows_ref, weight_ref, key_ref, value_ref, state_ref, sent_ref, key_t_ref, value_t_ref, copy_ref, held_ref, sems):
    heads = state_ref.shape[0]
    step = copy_ref.shape[0] // parts
    value_copy = pltpu.make_async_copy(weight_ref.at[2], held_ref.at[0], sems.at[0])
    key_copy = pltpu.make_async_copy(weight_ref.at[1], held_ref.at[1], sems.at[1])
    row_copies = []
    for part in range(parts):
        chunk = pl.ds(part * step, step)
        row_copies.append(pltpu.make_async_copy(rows_ref.at[chunk], copy_ref.at[chunk], sems.at[2 + part]))
    value_copy.start()
    for copy in row_copies:
        copy.start()
    key_copy.start()
    value_copy.wait()
    for part in range(parts):
        row_copies[part].wait()
        chunk = slice(part * step, (part + 1) * step)
        value_ref[chunk, :] = dot(copy_ref[chunk, :], held_ref[0]).astype(bf16)
    for h in range(heads):
        columns = slice(h * HD, (h + 1) * HD)
        value_t_ref[columns, :] = value_ref[:, columns].T
    key_copy.wait()
    key_ref[...] = dot(copy_ref[...], held_ref[1]).astype(bf16)
    for h in range(heads):
        columns = slice(h * HD, (h + 1) * HD)
        key_t = key_ref[:, columns].T
        key_t_ref[columns, :] = key_t
        state = dot(key_t, value_ref[:, columns])
        state_ref[h] = state
        sent_ref[h] = state.astype(bf16)


def block_states(rows, weights, parts=2):
    count, depth = rows.shape
    width = weights.shape[2]
    heads = width // HD
    hbm = pl.BlockSpec(memory_space=pltpu.HBM)
    vmem = pl.BlockSpec(memory_space=pltpu.VMEM)
    return pl.pallas_call(
        functools.partial(states_kernel, parts),
        in_specs=[hbm, hbm],
        out_specs=[vmem] * 7,
        out_shape=[
            jax.ShapeDtypeStruct((count, width), bf16),
            jax.ShapeDtypeStruct((count, width), bf16),
            jax.ShapeDtypeStruct((heads, HD, HD), f32),
            jax.ShapeDtypeStruct((heads, HD, HD), bf16),
            jax.ShapeDtypeStruct((width, count), bf16),
            jax.ShapeDtypeStruct((width, count), bf16),
            jax.ShapeDtypeStruct((count, depth), bf16),
        ],
        scratch_shapes=[pltpu.VMEM((2, depth, width), bf16), pltpu.SemaphoreType.DMA((2 + parts,))],
        compiler_params=params(44),
        cost_estimate=COST,
        name="block_states",
    )(rows, weights)


def terms_kernel(number, outputs, position_ref, *refs):
    lefts, right, outs = refs[:number], refs[number], refs[number + 1 :]
    width = outs[0].shape[2]
    jobs = {}
    for out, (left, low, high, slots) in zip(outs, outputs):
        for index, slot in enumerate(slots):
            jobs.setdefault((left, slot), []).append((low, high, out, index))
    for (left, slot), parts in jobs.items():
        start = pl.multiple_of((position_ref[0] ^ slot) * width, width)
        product = dot(lefts[left][...], right[:, pl.ds(start, width)]).astype(bf16)
        for low, high, out, index in parts:
            out[index] = product[low:high]


def gradient_terms(lefts, right, info, outputs):
    count = right.shape[0]
    width = right.shape[1] // lax.axis_size("seq")
    if width % 128:
        blocked = right.reshape(count, -1, width)
        results = []
        for left, low, high, slots in outputs:
            picked = jnp.take(blocked, info[0] ^ jnp.array(slots, jnp.int32), axis=1)
            part = jnp.einsum("at,tnb->nab", lefts[left][low:high], picked, preferred_element_type=f32)
            results.append(part.astype(bf16))
        return results
    shapes = [(len(slots), high - low, width) for _, low, high, slots in outputs]
    size = sum(n * r * w for n, r, w in shapes)
    vmem = pl.BlockSpec(memory_space=pltpu.VMEM)
    return pl.pallas_call(
        functools.partial(terms_kernel, len(lefts), outputs),
        in_specs=[pl.BlockSpec(memory_space=pltpu.SMEM)] + [vmem] * (len(lefts) + 1),
        out_specs=[vmem] * len(outputs),
        out_shape=[jax.ShapeDtypeStruct(shape, bf16) for shape in shapes],
        compiler_params=params(),
        cost_estimate=COST,
        name="gradient_terms",
    )(info, *lefts, right)


def sums_kernel(groups, merge, *refs):
    ins, outs = refs[: 2 * groups], refs[2 * groups :]
    low = 0
    for index in range(groups):
        keep, got = ins[2 * index], ins[2 * index + 1]
        half, rows = keep.shape[0] // 2, keep.shape[1]
        if merge:
            kept, sent = (out.at[:, low : low + rows, :] for out in outs)
            low += rows
        else:
            kept, sent = outs[2 * index], outs[2 * index + 1]
        for slot in range(half):
            kept[slot] = (keep[slot].astype(f32) + got[slot].astype(f32)).astype(bf16)
            other = half + slot
            sent[slot] = (keep[other].astype(f32) + got[other].astype(f32)).astype(bf16)


def sums(pairs, merge=False):
    slots, rows, width = pairs[0][0].shape
    total = sum(keep.shape[1] for keep, _ in pairs) if merge else rows
    shape = jax.ShapeDtypeStruct((slots // 2, total, width), bf16)
    vmem = pl.BlockSpec(memory_space=pltpu.VMEM)
    outs = 2 if merge else 2 * len(pairs)
    size = sum(keep.size for keep, _ in pairs)
    return pl.pallas_call(
        functools.partial(sums_kernel, len(pairs), merge),
        in_specs=[vmem] * (2 * len(pairs)),
        out_specs=[vmem] * outs,
        out_shape=[shape] * outs,
        compiler_params=params(),
        cost_estimate=COST,
        name="sums",
    )(*[array for pair in pairs for array in pair])


def flag(info_ref, bit):
    return ((info_ref[0] >> bit) & 1).astype(f32)


def small(kernel, info, arrays, shapes, name):
    vmem = pl.BlockSpec(memory_space=pltpu.VMEM)
    return pl.pallas_call(
        kernel,
        in_specs=[pl.BlockSpec(memory_space=pltpu.SMEM)] + [vmem] * len(arrays),
        out_specs=[vmem] * len(shapes),
        out_shape=[jax.ShapeDtypeStruct(shape, kind) for shape, kind in shapes],
        compiler_params=params(),
        cost_estimate=COST,
        name=name,
    )(info, *arrays)


def mark_kernel(info_ref, out_ref):
    out_ref[...] = jnp.full(out_ref.shape, flag(info_ref, 0))


def prefix_kernel(bit, info_ref, total_ref, got_ref, *refs):
    got = got_ref[...].astype(f32)
    before = got * flag(info_ref, bit)
    if bit:
        before += refs[0][...]
        refs = refs[1:]
    refs[0][...] = before
    if len(refs) > 1:
        total = total_ref[...] + got
        refs[1][...] = total
        refs[2][...] = total.astype(bf16)


def prefix_step(info, bit, arrays, last):
    shape = arrays[0].shape
    shapes = [(shape, f32)] if last else [(shape, f32), (shape, f32), (shape, bf16)]
    return small(functools.partial(prefix_kernel, bit), info, arrays, shapes, "prefix_step")


def suffix_first_kernel(info_ref, own_ref, got_ref, total_ref, mine_ref, mate_ref, sent_ref):
    upper = flag(info_ref, 0)
    own, got = own_ref[...], got_ref[...].astype(f32)
    total = own + got
    mine = own + got * (1.0 - upper)
    total_ref[...] = total
    mine_ref[...] = mine
    mate_ref[...] = got + own * upper
    sent_ref[0] = total.astype(bf16)
    sent_ref[1] = mine.astype(bf16)


def suffix_first(info, own, got):
    shape = own.shape
    shapes = [(shape, f32), (shape, f32), (shape, f32), ((2,) + shape, bf16)]
    return small(suffix_first_kernel, info, [own, got], shapes, "suffix_first")


def suffix_kernel(bit, inputs, info_ref, *refs):
    arrays, outs = refs[:inputs], refs[inputs:]
    upper = flag(info_ref, bit)
    total = arrays[0][...]
    if bit == 1:
        got = arrays[3][0].astype(f32)
        other = arrays[3][1].astype(f32) + total * upper
        later = got * (1.0 - upper)
    else:
        got = arrays[4][...].astype(f32)
        later = got * (1.0 - upper)
        other = arrays[3][...] + later
    outs[0][...] = arrays[1][...] + later
    outs[1][...] = arrays[2][...] + later
    outs[2][...] = other
    if len(outs) > 3:
        outs[3][...] = total + got
        outs[4][...] = (total + got).astype(bf16)


def suffix_step(info, bit, arrays, last):
    shape = arrays[0].shape
    shapes = [(shape, f32)] * 3 if last else [(shape, f32)] * 4 + [(shape, bf16)]
    return small(functools.partial(suffix_kernel, bit, len(arrays)), info, arrays, shapes, "suffix_step")


def middle_kernel(query_ref, grad_ref, mask_ref, gain_ref, own_ref, before_ref, normed_t_ref, query_grad_ref, query_grad_t_ref, block_grad_ref, sent_ref, held_ref):
    mask_row = mask_ref[...].astype(f32)

    @pl.when(pl.program_id(0) == 0)
    def _():
        held_ref[...] = jnp.broadcast_to(mask_row, held_ref.shape[::-1]).T

    query = query_ref[...]
    state = (before_ref[0] + own_ref[0]).astype(bf16)
    mask = held_ref[...]
    gain = gain_ref[...].astype(f32)
    attended = dot(query, state)
    scale = lax.rsqrt(jnp.mean(attended * attended, -1, keepdims=True) + epsilon)
    unit = attended * scale
    normed_t_ref[...] = (unit * gain * mask).astype(bf16).T
    scaled = grad_ref[...] * mask * gain
    inner = jnp.mean(scaled * attended, -1, keepdims=True)
    attended_grad = (scale * scaled - attended * (scale * scale * scale) * inner).astype(bf16)
    attended_grad_t = attended_grad.T
    block_grad = dot(attended_grad_t, query)
    block_grad_ref[0] = block_grad
    sent_ref[0] = block_grad.astype(bf16)
    query_grad_ref[...] = dot_t(attended_grad, state).astype(bf16)
    query_grad_t_ref[...] = dot(state, attended_grad_t).astype(bf16)


def middle(queries, normed_grad, mask, gain, own, before):
    count, width = queries.shape
    heads = width // HD
    column = pl.BlockSpec((count, HD), lambda h: (0, h))
    row = pl.BlockSpec((HD, count), lambda h: (h, 0))
    square = pl.BlockSpec((1, HD, HD), lambda h: (h, 0, 0))
    return pl.pallas_call(
        middle_kernel,
        grid=(heads,),
        in_specs=[
            column,
            column,
            pl.BlockSpec((1, count), lambda h: (0, 0)),
            pl.BlockSpec((1, HD), lambda h: (0, h)),
            square,
            square,
        ],
        out_specs=[row, column, row, square, square],
        out_shape=[
            jax.ShapeDtypeStruct((width, count), bf16),
            jax.ShapeDtypeStruct((count, width), bf16),
            jax.ShapeDtypeStruct((width, count), bf16),
            jax.ShapeDtypeStruct((heads, HD, HD), f32),
            jax.ShapeDtypeStruct((heads, HD, HD), bf16),
        ],
        scratch_shapes=[pltpu.VMEM((count, HD), f32)],
        compiler_params=params(),
        cost_estimate=pl.CostEstimate(
            flops=64 * count * width * HD, bytes_accessed=1, transcendentals=0
        ),
        name="norm_backward",
    )(queries, normed_grad, mask, gain, own, before)


def late_kernel(mine_ref, mate_ref, other_ref, *refs):
    for side, state_ref, parts in ((0, mate_ref, refs[0:2] + refs[4:6]), (1, other_ref, refs[2:4] + refs[6:8])):
        own, got, keep, send = parts
        half = keep.shape[0]

        def times(state, block):
            return lax.dot_general(state, block, (((side,), (0,)), ((), ())), preferred_element_type=f32)

        for slot in range(2 * half):
            out = keep if slot < half else send
            for h in range(mine_ref.shape[0]):
                rows = slice(h * HD, (h + 1) * HD)
                total = times(mine_ref[h].astype(bf16), own[slot, rows, :])
                total += times(state_ref[h].astype(bf16), got[slot, rows, :])
                out[slot % half, rows, :] = total.astype(bf16)


def late_terms(mine, mate, other, value_keep, value_got, key_keep, key_got):
    slots, rows, width = value_keep.shape
    vmem = pl.BlockSpec(memory_space=pltpu.VMEM)
    shape = jax.ShapeDtypeStruct((slots // 2, rows, width), bf16)
    return pl.pallas_call(
        late_kernel,
        in_specs=[vmem] * 7,
        out_specs=[vmem] * 4,
        out_shape=[shape] * 4,
        compiler_params=params(),
        cost_estimate=COST,
        name="late_terms",
    )(mine, mate, other, value_keep, value_got, key_keep, key_got)


def key_value_kernel(key_ref, value_ref, grad_ref, key_grad_ref, value_grad_ref):
    state_grad = grad_ref[0].astype(bf16)
    key_grad_ref[...] = dot(value_ref[...], state_grad).astype(bf16)
    value_grad_ref[...] = dot_t(key_ref[...], state_grad).astype(bf16)


def key_value_grads(keys, values, state_grad_t):
    count, width = keys.shape
    column = pl.BlockSpec((count, HD), lambda h: (0, h))
    out = jax.ShapeDtypeStruct((count, width), bf16)
    return pl.pallas_call(
        key_value_kernel,
        grid=(width // HD,),
        in_specs=[column, column, pl.BlockSpec((1, HD, HD), lambda h: (h, 0, 0))],
        out_specs=[column, column],
        out_shape=[out, out],
        compiler_params=params(),
        cost_estimate=COST,
        name="key_value_grads",
    )(keys, values, state_grad_t)


def input_kernel(order, place_ref, query_ref, key_ref, value_ref, weight_ref, keep_ref, send_ref, held_ref):
    total = dot_t(query_ref[...], weight_ref[0])
    total += dot_t(key_ref[...], weight_ref[1])
    total += dot_t(value_ref[...], weight_ref[2])
    held_ref[...] = total.astype(bf16).reshape(held_ref.shape)
    half = len(order) // 2
    for index in range(half):
        keep_ref[index] = held_ref[place_ref[1] ^ order[index]]
        send_ref[index] = held_ref[place_ref[1] ^ order[half + index]]


def input_terms(grads, weight, info, order, chunk, chunks, tile=512):
    count, width = grads[0].shape
    half = len(order) // 2
    rows = count // len(order)
    columns = D // chunks
    first = chunk * columns // tile
    full = pl.BlockSpec((count, width), lambda i, b: (0, 0))
    out = pl.BlockSpec((half, rows, tile), lambda i, b: (0, 0, i))
    shape = jax.ShapeDtypeStruct((half, rows, columns), bf16)
    return pl.pallas_call(
        functools.partial(input_kernel, order),
        grid_spec=pltpu.PrefetchScalarGridSpec(
            num_scalar_prefetch=1,
            grid=(columns // tile,),
            in_specs=[full, full, full, pl.BlockSpec((3, tile, width), lambda i, b: (0, first + i, 0))],
            out_specs=[out, out],
            scratch_shapes=[pltpu.VMEM((len(order), rows, tile), bf16)],
        ),
        out_shape=[shape, shape],
        compiler_params=params(20),
        cost_estimate=COST,
        name="input_terms",
    )(info, *grads, weight)


def finish_kernel(query_keep_ref, query_got_ref, late_keep_ref, late_got_ref, out_ref):
    width = query_keep_ref.shape[0]
    out_ref[0] = (query_keep_ref[...].astype(f32) + query_got_ref[...].astype(f32)).T
    for index in range(2):
        rows = slice(index * width, (index + 1) * width)
        out_ref[1 + index] = (late_keep_ref[rows, :].astype(f32) + late_got_ref[rows, :].astype(f32)).T


def finish(query_keep, query_got, late_keep, late_got):
    rows, width = query_keep.shape
    return pl.pallas_call(
        finish_kernel,
        out_shape=jax.ShapeDtypeStruct((3, width, rows), f32),
        compiler_params=params(),
        cost_estimate=COST,
        name="finish",
    )(query_keep, query_got, late_keep, late_got)


def after(value, *others):
    return lax.optimization_barrier((value,) + others)[0]


def per_device(layer_input, output_grad, loss_mask, proj_weight, out_weight, norm_gain):
    count = layer_input.shape[0]
    seq_bits = lax.axis_size("seq").bit_length() - 1
    head_bits = lax.axis_size("head").bit_length() - 1
    stages = list(range(seq_bits))
    order, swapped = slot_order(stages), slot_order([1, 0] + stages[2:])
    half = len(order) // 2
    head_order = slot_order(list(range(head_bits)))
    info = jnp.stack([lax.axis_index("seq"), lax.axis_index("head")]).astype(jnp.int32)
    layer_input, output_grad, loss_mask, proj_weight, norm_gain = after(
        (layer_input, output_grad, loss_mask, proj_weight, norm_gain), info
    )
    weights = jnp.transpose(proj_weight, (1, 0, 2))
    mask = loss_mask.reshape(1, count)

    def project(rows, index):
        return jnp.dot(rows, weights[index], preferred_element_type=f32).astype(bf16)

    def terms(left, right, *parts):
        outputs = [(0, 0, left.shape[0], slots) for slots in parts]
        return gradient_terms([left], right, info, outputs)

    keys, values, own_state, sent, keys_t, values_t, layer_input = block_states(layer_input, weights)

    got = exchange(sent, "seq", 0)
    (value_send,) = terms(values_t, after(layer_input, own_state), order[half:])
    queries = project(after(layer_input, value_send), 0)
    got = after(got, queries)
    before, total, sent = prefix_step(info, 0, [own_state, got], False)
    value_got = exchange(after(value_send, total), "seq", 0)
    for bit in stages[1:]:
        got = exchange(sent, "seq", bit)
        if bit == 1:
            normed_grad = dot_t(after(output_grad, total), out_weight)
            (key_send,) = terms(keys_t, after(layer_input, normed_grad), swapped[half:])
            got = after(got, key_send)
        elif bit == 2:
            (mark,) = small(mark_kernel, after(info, total), [], [((8, 128), f32)], "mark")
            key_got = exchange(after(key_send, mark), "seq", 1)
            got = after(got, mark)
        before, *sums_on = prefix_step(info, bit, [total, got, before], bit == stages[-1])
        if sums_on:
            total, sent = sums_on

    normed_t, query_grad, query_grad_t, own_grad, sent = middle(
        queries, normed_grad, mask, norm_gain[None, :], own_state, before
    )

    got = exchange(sent, "seq", 0)
    out_keep, out_send = terms(normed_t, after(output_grad, own_grad), order[:half], order[half:])
    got = after(got, out_keep, value_got)
    total, mine, mate, sent = suffix_first(info, own_grad, got)
    out_got = exchange(after(out_send, total), "seq", 0)

    got = exchange(sent, "seq", 1)
    query_keep, query_send = terms(query_grad_t, after(layer_input, total), order[:half], order[half:])
    got = after(got, query_keep, key_got)
    mine, mate, other, *sums_on = suffix_step(info, 1, [total, mine, mate, got], False)
    total, sent = sums_on
    query_got = exchange(after(query_send, total), "seq", 0)

    for bit in stages[2:]:
        got = exchange(sent, "seq", bit)
        if bit == 2:
            (value_keep,) = terms(values_t, after(layer_input, total), order[:half])
            (key_keep,) = terms(keys_t, after(layer_input, value_keep), swapped[:half])
            got = after(got, key_keep)
        mine, mate, other, *sums_on = suffix_step(
            info, bit, [total, mine, mate, other, got], bit == stages[-1]
        )
        if sums_on:
            total, sent = sums_on

    value_keep, value_send, key_keep, key_send = late_terms(
        mine, mate, other, value_keep, value_got, key_keep, key_got
    )
    value_got = exchange(value_send, "seq", 1)
    key_got = exchange(key_send, "seq", 0)

    key_grad, value_grad = key_value_grads(keys, values, after(mine, value_keep))
    grads = (query_grad, key_grad, value_grad)
    input_keep, input_send = input_terms(grads, weights, info, head_order, 0, 1)

    def stage(keep, got, token, bit, axis="seq"):
        keep, send = sums([(keep, after(got, token))])
        return keep, exchange(send, axis, bit)

    def rest(keep, got, bits_left):
        for bit in bits_left:
            keep, got = stage(keep, got, keep, bit)
        return keep[0], got[0]

    value_got, key_got = after((value_got, key_got), input_keep)
    late_keep, late_send = sums([(value_keep, value_got), (key_keep, key_got)], merge=True)
    late_got = exchange(late_send, "seq", 2)
    out_keep, out_got = stage(out_keep, out_got, late_keep, 1)
    input_got = exchange(after(input_send, out_keep), "head", 0)
    for bit in range(1, head_bits):
        input_keep, input_got = stage(input_keep, input_got, out_keep, bit, "head")
    out_keep, out_got = stage(out_keep, out_got, (input_keep, late_got), 2)
    query_keep, query_got = stage(query_keep, query_got, out_keep, 1)
    query_keep, query_got = stage(query_keep, query_got, (query_keep, out_got, input_got), 2)

    out_pair = rest(out_keep, out_got, stages[3:])
    late_pair = rest(late_keep, late_got, stages[3:])
    query_pair = rest(query_keep, query_got, stages[3:])
    input_grad = (input_keep[0].astype(f32) + input_got[0].astype(f32)).astype(bf16)
    out_weight_grad = out_pair[0].astype(f32) + out_pair[1].astype(f32)
    proj_weight_grad = finish(*query_pair, *late_pair)
    return (input_grad, jnp.transpose(proj_weight_grad, (1, 0, 2)), out_weight_grad)


def solution(mesh):
    in_specs = (
        P("seq", None),
        P("seq", None),
        P("seq"),
        P(None, None, "head"),
        P("head", None),
        P("head"),
    )
    out_specs = (P(("seq", "head"), None), P("seq", None, "head"), P("head", "seq"))
    return jax.shard_map(
        per_device, mesh=mesh, in_specs=in_specs, out_specs=out_specs, check_vma=False
    )
```

```python
import functools

import jax
import jax.numpy as jnp
from jax import lax
from jax.experimental import pallas as pl
from jax.experimental.pallas import tpu as pltpu
from jax.sharding import PartitionSpec as P

D = 2048
HD = 128
BLOCK = 1024
epsilon = 1e-06
f32 = jnp.float32
bf16 = jnp.bfloat16
MIB = 1024 * 1024
COST = pl.CostEstimate(flops=1000000, bytes_accessed=1, transcendentals=0)


def params(mib=16):
    return pltpu.CompilerParams(vmem_limit_bytes=mib * MIB)


def dot(a, b):
    return lax.dot_general(a, b, (((1,), (0,)), ((), ())), preferred_element_type=f32)


def dot_t(a, b):
    return lax.dot_general(a, b, (((1,), (1,)), ((), ())), preferred_element_type=f32)


def exchange(arr, axis, bit):
    count = lax.axis_size(axis)
    return lax.ppermute(arr, axis, [(i, i ^ (1 << bit)) for i in range(count)])


def slot_order(stage_bits):
    order = [0]
    for bit in reversed(stage_bits):
        order = order + [slot | (1 << bit) for slot in order]
    return order


def states_kernel(parts, rows_ref, weight_ref, key_ref, value_ref, state_ref, sent_ref, key_t_ref, value_t_ref, copy_ref, held_ref, sems):
    heads = state_ref.shape[0]
    step = copy_ref.shape[0] // parts
    value_copy = pltpu.make_async_copy(weight_ref.at[2], held_ref.at[0], sems.at[0])
    key_copy = pltpu.make_async_copy(weight_ref.at[1], held_ref.at[1], sems.at[1])
    row_copies = []
    for part in range(parts):
        chunk = pl.ds(part * step, step)
        row_copies.append(pltpu.make_async_copy(rows_ref.at[chunk], copy_ref.at[chunk], sems.at[2 + part]))
    value_copy.start()
    for copy in row_copies:
        copy.start()
    key_copy.start()
    value_copy.wait()
    for part in range(parts):
        row_copies[part].wait()
        chunk = slice(part * step, (part + 1) * step)
        value_ref[chunk, :] = dot(copy_ref[chunk, :], held_ref[0]).astype(bf16)
    for h in range(heads):
        columns = slice(h * HD, (h + 1) * HD)
        value_t_ref[columns, :] = value_ref[:, columns].T
    key_copy.wait()
    key_ref[...] = dot(copy_ref[...], held_ref[1]).astype(bf16)
    for h in range(heads):
        columns = slice(h * HD, (h + 1) * HD)
        key_t = key_ref[:, columns].T
        key_t_ref[columns, :] = key_t
        state = dot(key_t, value_ref[:, columns])
        state_ref[h] = state
        sent_ref[h] = state.astype(bf16)


def block_states(rows, weights, parts=2):
    count, depth = rows.shape
    width = weights.shape[2]
    heads = width // HD
    hbm = pl.BlockSpec(memory_space=pltpu.HBM)
    vmem = pl.BlockSpec(memory_space=pltpu.VMEM)
    return pl.pallas_call(
        functools.partial(states_kernel, parts),
        in_specs=[hbm, hbm],
        out_specs=[vmem] * 7,
        out_shape=[
            jax.ShapeDtypeStruct((count, width), bf16),
            jax.ShapeDtypeStruct((count, width), bf16),
            jax.ShapeDtypeStruct((heads, HD, HD), f32),
            jax.ShapeDtypeStruct((heads, HD, HD), bf16),
            jax.ShapeDtypeStruct((width, count), bf16),
            jax.ShapeDtypeStruct((width, count), bf16),
            jax.ShapeDtypeStruct((count, depth), bf16),
        ],
        scratch_shapes=[pltpu.VMEM((2, depth, width), bf16), pltpu.SemaphoreType.DMA((2 + parts,))],
        compiler_params=params(44),
        cost_estimate=COST,
        name="block_states",
    )(rows, weights)


def terms_kernel(number, outputs, position_ref, *refs):
    lefts, right, outs = refs[:number], refs[number], refs[number + 1 :]
    width = outs[0].shape[2]
    jobs = {}
    for out, (left, low, high, slots) in zip(outs, outputs):
        for index, slot in enumerate(slots):
            jobs.setdefault((left, slot), []).append((low, high, out, index))
    for (left, slot), parts in jobs.items():
        start = pl.multiple_of((position_ref[0] ^ slot) * width, width)
        product = dot(lefts[left][...], right[:, pl.ds(start, width)]).astype(bf16)
        for low, high, out, index in parts:
            out[index] = product[low:high]


def gradient_terms(lefts, right, info, outputs):
    count = right.shape[0]
    width = right.shape[1] // lax.axis_size("seq")
    if width % 128:
        blocked = right.reshape(count, -1, width)
        results = []
        for left, low, high, slots in outputs:
            picked = jnp.take(blocked, info[0] ^ jnp.array(slots, jnp.int32), axis=1)
            part = jnp.einsum("at,tnb->nab", lefts[left][low:high], picked, preferred_element_type=f32)
            results.append(part.astype(bf16))
        return results
    shapes = [(len(slots), high - low, width) for _, low, high, slots in outputs]
    size = sum(n * r * w for n, r, w in shapes)
    vmem = pl.BlockSpec(memory_space=pltpu.VMEM)
    return pl.pallas_call(
        functools.partial(terms_kernel, len(lefts), outputs),
        in_specs=[pl.BlockSpec(memory_space=pltpu.SMEM)] + [vmem] * (len(lefts) + 1),
        out_specs=[vmem] * len(outputs),
        out_shape=[jax.ShapeDtypeStruct(shape, bf16) for shape in shapes],
        compiler_params=params(),
        cost_estimate=COST,
        name="gradient_terms",
    )(info, *lefts, right)


def sums_kernel(groups, merge, *refs):
    ins, outs = refs[: 2 * groups], refs[2 * groups :]
    low = 0
    for index in range(groups):
        keep, got = ins[2 * index], ins[2 * index + 1]
        half, rows = keep.shape[0] // 2, keep.shape[1]
        if merge:
            kept, sent = (out.at[:, low : low + rows, :] for out in outs)
            low += rows
        else:
            kept, sent = outs[2 * index], outs[2 * index + 1]
        for slot in range(half):
            kept[slot] = (keep[slot].astype(f32) + got[slot].astype(f32)).astype(bf16)
            other = half + slot
            sent[slot] = (keep[other].astype(f32) + got[other].astype(f32)).astype(bf16)


def sums(pairs, merge=False):
    slots, rows, width = pairs[0][0].shape
    total = sum(keep.shape[1] for keep, _ in pairs) if merge else rows
    shape = jax.ShapeDtypeStruct((slots // 2, total, width), bf16)
    vmem = pl.BlockSpec(memory_space=pltpu.VMEM)
    outs = 2 if merge else 2 * len(pairs)
    size = sum(keep.size for keep, _ in pairs)
    return pl.pallas_call(
        functools.partial(sums_kernel, len(pairs), merge),
        in_specs=[vmem] * (2 * len(pairs)),
        out_specs=[vmem] * outs,
        out_shape=[shape] * outs,
        compiler_params=params(),
        cost_estimate=COST,
        name="sums",
    )(*[array for pair in pairs for array in pair])


def flag(info_ref, bit):
    return ((info_ref[0] >> bit) & 1).astype(f32)


def small(kernel, info, arrays, shapes, name):
    vmem = pl.BlockSpec(memory_space=pltpu.VMEM)
    return pl.pallas_call(
        kernel,
        in_specs=[pl.BlockSpec(memory_space=pltpu.SMEM)] + [vmem] * len(arrays),
        out_specs=[vmem] * len(shapes),
        out_shape=[jax.ShapeDtypeStruct(shape, kind) for shape, kind in shapes],
        compiler_params=params(),
        cost_estimate=COST,
        name=name,
    )(info, *arrays)


def mark_kernel(info_ref, out_ref):
    out_ref[...] = jnp.full(out_ref.shape, flag(info_ref, 0))


def prefix_kernel(bit, info_ref, total_ref, got_ref, *refs):
    got = got_ref[...].astype(f32)
    before = got * flag(info_ref, bit)
    if bit:
        before += refs[0][...]
        refs = refs[1:]
    refs[0][...] = before
    if len(refs) > 1:
        total = total_ref[...] + got
        refs[1][...] = total
        refs[2][...] = total.astype(bf16)


def prefix_step(info, bit, arrays, last):
    shape = arrays[0].shape
    shapes = [(shape, f32)] if last else [(shape, f32), (shape, f32), (shape, bf16)]
    return small(functools.partial(prefix_kernel, bit), info, arrays, shapes, "prefix_step")


def suffix_first_kernel(info_ref, own_ref, got_ref, total_ref, mine_ref, mate_ref, sent_ref):
    upper = flag(info_ref, 0)
    own, got = own_ref[...], got_ref[...].astype(f32)
    total = own + got
    mine = own + got * (1.0 - upper)
    total_ref[...] = total
    mine_ref[...] = mine
    mate_ref[...] = got + own * upper
    sent_ref[0] = total.astype(bf16)
    sent_ref[1] = mine.astype(bf16)


def suffix_first(info, own, got):
    shape = own.shape
    shapes = [(shape, f32), (shape, f32), (shape, f32), ((2,) + shape, bf16)]
    return small(suffix_first_kernel, info, [own, got], shapes, "suffix_first")


def suffix_kernel(bit, inputs, info_ref, *refs):
    arrays, outs = refs[:inputs], refs[inputs:]
    upper = flag(info_ref, bit)
    total = arrays[0][...]
    if bit == 1:
        got = arrays[3][0].astype(f32)
        other = arrays[3][1].astype(f32) + total * upper
        later = got * (1.0 - upper)
    else:
        got = arrays[4][...].astype(f32)
        later = got * (1.0 - upper)
        other = arrays[3][...] + later
    outs[0][...] = arrays[1][...] + later
    outs[1][...] = arrays[2][...] + later
    outs[2][...] = other
    if len(outs) > 3:
        outs[3][...] = total + got
        outs[4][...] = (total + got).astype(bf16)


def suffix_step(info, bit, arrays, last):
    shape = arrays[0].shape
    shapes = [(shape, f32)] * 3 if last else [(shape, f32)] * 4 + [(shape, bf16)]
    return small(functools.partial(suffix_kernel, bit, len(arrays)), info, arrays, shapes, "suffix_step")


def middle_kernel(query_ref, grad_ref, mask_ref, gain_ref, own_ref, before_ref, normed_t_ref, query_grad_ref, query_grad_t_ref, block_grad_ref, sent_ref, held_ref):
    mask_row = mask_ref[...].astype(f32)

    @pl.when(pl.program_id(0) == 0)
    def _():
        held_ref[...] = jnp.broadcast_to(mask_row, held_ref.shape[::-1]).T

    query = query_ref[...]
    state = (before_ref[0] + own_ref[0]).astype(bf16)
    mask = held_ref[...]
    gain = gain_ref[...].astype(f32)
    attended = dot(query, state)
    scale = lax.rsqrt(jnp.mean(attended * attended, -1, keepdims=True) + epsilon)
    unit = attended * scale
    normed_t_ref[...] = (unit * gain * mask).astype(bf16).T
    scaled = grad_ref[...] * mask * gain
    inner = jnp.mean(scaled * attended, -1, keepdims=True)
    attended_grad = (scale * scaled - attended * (scale * scale * scale) * inner).astype(bf16)
    attended_grad_t = attended_grad.T
    block_grad = dot(attended_grad_t, query)
    block_grad_ref[0] = block_grad
    sent_ref[0] = block_grad.astype(bf16)
    query_grad_ref[...] = dot_t(attended_grad, state).astype(bf16)
    query_grad_t_ref[...] = dot(state, attended_grad_t).astype(bf16)


def middle(queries, normed_grad, mask, gain, own, before):
    count, width = queries.shape
    heads = width // HD
    column = pl.BlockSpec((count, HD), lambda h: (0, h))
    row = pl.BlockSpec((HD, count), lambda h: (h, 0))
    square = pl.BlockSpec((1, HD, HD), lambda h: (h, 0, 0))
    return pl.pallas_call(
        middle_kernel,
        grid=(heads,),
        in_specs=[
            column,
            column,
            pl.BlockSpec((1, count), lambda h: (0, 0)),
            pl.BlockSpec((1, HD), lambda h: (0, h)),
            square,
            square,
        ],
        out_specs=[row, column, row, square, square],
        out_shape=[
            jax.ShapeDtypeStruct((width, count), bf16),
            jax.ShapeDtypeStruct((count, width), bf16),
            jax.ShapeDtypeStruct((width, count), bf16),
            jax.ShapeDtypeStruct((heads, HD, HD), f32),
            jax.ShapeDtypeStruct((heads, HD, HD), bf16),
        ],
        scratch_shapes=[pltpu.VMEM((count, HD), f32)],
        compiler_params=params(),
        cost_estimate=pl.CostEstimate(
            flops=64 * count * width * HD, bytes_accessed=1, transcendentals=0
        ),
        name="norm_backward",
    )(queries, normed_grad, mask, gain, own, before)


def late_kernel(mine_ref, mate_ref, other_ref, *refs):
    for side, state_ref, parts in ((0, mate_ref, refs[0:2] + refs[4:6]), (1, other_ref, refs[2:4] + refs[6:8])):
        own, got, keep, send = parts
        half = keep.shape[0]

        def times(state, block):
            return lax.dot_general(state, block, (((side,), (0,)), ((), ())), preferred_element_type=f32)

        for slot in range(2 * half):
            out = keep if slot < half else send
            for h in range(mine_ref.shape[0]):
                rows = slice(h * HD, (h + 1) * HD)
                total = times(mine_ref[h].astype(bf16), own[slot, rows, :])
                total += times(state_ref[h].astype(bf16), got[slot, rows, :])
                out[slot % half, rows, :] = total.astype(bf16)


def late_terms(mine, mate, other, value_keep, value_got, key_keep, key_got):
    slots, rows, width = value_keep.shape
    vmem = pl.BlockSpec(memory_space=pltpu.VMEM)
    shape = jax.ShapeDtypeStruct((slots // 2, rows, width), bf16)
    return pl.pallas_call(
        late_kernel,
        in_specs=[vmem] * 7,
        out_specs=[vmem] * 4,
        out_shape=[shape] * 4,
        compiler_params=params(),
        cost_estimate=COST,
        name="late_terms",
    )(mine, mate, other, value_keep, value_got, key_keep, key_got)


def key_value_kernel(key_ref, value_ref, grad_ref, key_grad_ref, value_grad_ref):
    state_grad = grad_ref[0].astype(bf16)
    key_grad_ref[...] = dot(value_ref[...], state_grad).astype(bf16)
    value_grad_ref[...] = dot_t(key_ref[...], state_grad).astype(bf16)


def key_value_grads(keys, values, state_grad_t):
    count, width = keys.shape
    column = pl.BlockSpec((count, HD), lambda h: (0, h))
    out = jax.ShapeDtypeStruct((count, width), bf16)
    return pl.pallas_call(
        key_value_kernel,
        grid=(width // HD,),
        in_specs=[column, column, pl.BlockSpec((1, HD, HD), lambda h: (h, 0, 0))],
        out_specs=[column, column],
        out_shape=[out, out],
        compiler_params=params(),
        cost_estimate=COST,
        name="key_value_grads",
    )(keys, values, state_grad_t)


def input_kernel(order, place_ref, query_ref, key_ref, value_ref, weight_ref, keep_ref, send_ref, held_ref):
    total = dot_t(query_ref[...], weight_ref[0])
    total += dot_t(key_ref[...], weight_ref[1])
    total += dot_t(value_ref[...], weight_ref[2])
    held_ref[...] = total.astype(bf16).reshape(held_ref.shape)
    half = len(order) // 2
    for index in range(half):
        keep_ref[index] = held_ref[place_ref[1] ^ order[index]]
        send_ref[index] = held_ref[place_ref[1] ^ order[half + index]]


def input_terms(grads, weight, info, order, chunk, chunks, tile=512):
    count, width = grads[0].shape
    half = len(order) // 2
    rows = count // len(order)
    columns = D // chunks
    first = chunk * columns // tile
    full = pl.BlockSpec((count, width), lambda i, b: (0, 0))
    out = pl.BlockSpec((half, rows, tile), lambda i, b: (0, 0, i))
    shape = jax.ShapeDtypeStruct((half, rows, columns), bf16)
    return pl.pallas_call(
        functools.partial(input_kernel, order),
        grid_spec=pltpu.PrefetchScalarGridSpec(
            num_scalar_prefetch=1,
            grid=(columns // tile,),
            in_specs=[full, full, full, pl.BlockSpec((3, tile, width), lambda i, b: (0, first + i, 0))],
            out_specs=[out, out],
            scratch_shapes=[pltpu.VMEM((len(order), rows, tile), bf16)],
        ),
        out_shape=[shape, shape],
        compiler_params=params(20),
        cost_estimate=COST,
        name="input_terms",
    )(info, *grads, weight)


def finish_kernel(query_keep_ref, query_got_ref, late_keep_ref, late_got_ref, out_ref):
    width = query_keep_ref.shape[0]
    out_ref[0] = (query_keep_ref[...].astype(f32) + query_got_ref[...].astype(f32)).T
    for index in range(2):
        rows = slice(index * width, (index + 1) * width)
        out_ref[1 + index] = (late_keep_ref[rows, :].astype(f32) + late_got_ref[rows, :].astype(f32)).T


def finish(query_keep, query_got, late_keep, late_got):
    rows, width = query_keep.shape
    return pl.pallas_call(
        finish_kernel,
        out_shape=jax.ShapeDtypeStruct((3, width, rows), f32),
        compiler_params=params(),
        cost_estimate=COST,
        name="finish",
    )(query_keep, query_got, late_keep, late_got)


def after(value, *others):
    return lax.optimization_barrier((value,) + others)[0]


def per_device(layer_input, output_grad, loss_mask, proj_weight, out_weight, norm_gain):
    count = layer_input.shape[0]
    seq_bits = lax.axis_size("seq").bit_length() - 1
    head_bits = lax.axis_size("head").bit_length() - 1
    stages = list(range(seq_bits))
    order, swapped = slot_order(stages), slot_order([1, 0] + stages[2:])
    half = len(order) // 2
    head_order = slot_order(list(range(head_bits)))
    info = jnp.stack([lax.axis_index("seq"), lax.axis_index("head")]).astype(jnp.int32)
    layer_input, output_grad, loss_mask, proj_weight, norm_gain = after(
        (layer_input, output_grad, loss_mask, proj_weight, norm_gain), info
    )
    weights = jnp.transpose(proj_weight, (1, 0, 2))
    mask = loss_mask.reshape(1, count)

    def project(rows, index):
        return jnp.dot(rows, weights[index], preferred_element_type=f32).astype(bf16)

    def terms(left, right, *parts):
        outputs = [(0, 0, left.shape[0], slots) for slots in parts]
        return gradient_terms([left], right, info, outputs)

    keys, values, own_state, sent, keys_t, values_t, layer_input = block_states(layer_input, weights)

    got = exchange(sent, "seq", 0)
    (value_send,) = terms(values_t, after(layer_input, own_state), order[half:])
    queries = project(after(layer_input, value_send), 0)
    got = after(got, queries)
    before, total, sent = prefix_step(info, 0, [own_state, got], False)
    value_got = exchange(after(value_send, total), "seq", 0)
    for bit in stages[1:]:
        got = exchange(sent, "seq", bit)
        if bit == 1:
            normed_grad = dot_t(after(output_grad, total), out_weight)
            (key_send,) = terms(keys_t, after(layer_input, normed_grad), swapped[half:])
            got = after(got, key_send)
        elif bit == 2:
            (mark,) = small(mark_kernel, after(info, total), [], [((8, 128), f32)], "mark")
            key_got = exchange(after(key_send, mark), "seq", 1)
            got = after(got, mark)
        before, *sums_on = prefix_step(info, bit, [total, got, before], bit == stages[-1])
        if sums_on:
            total, sent = sums_on

    normed_t, query_grad, query_grad_t, own_grad, sent = middle(
        queries, normed_grad, mask, norm_gain[None, :], own_state, before
    )

    got = exchange(sent, "seq", 0)
    out_keep, out_send = terms(normed_t, after(output_grad, own_grad), order[:half], order[half:])
    got = after(got, out_keep, value_got)
    total, mine, mate, sent = suffix_first(info, own_grad, got)
    out_got = exchange(after(out_send, total), "seq", 0)

    got = exchange(sent, "seq", 1)
    query_keep, query_send = terms(query_grad_t, after(layer_input, total), order[:half], order[half:])
    got = after(got, query_keep, key_got)
    mine, mate, other, *sums_on = suffix_step(info, 1, [total, mine, mate, got], False)
    total, sent = sums_on
    query_got = exchange(after(query_send, total), "seq", 0)

    for bit in stages[2:]:
        got = exchange(sent, "seq", bit)
        if bit == 2:
            (value_keep,) = terms(values_t, after(layer_input, total), order[:half])
            (key_keep,) = terms(keys_t, after(layer_input, value_keep), swapped[:half])
            got = after(got, key_keep)
        mine, mate, other, *sums_on = suffix_step(
            info, bit, [total, mine, mate, other, got], bit == stages[-1]
        )
        if sums_on:
            total, sent = sums_on

    value_keep, value_send, key_keep, key_send = late_terms(
        mine, mate, other, value_keep, value_got, key_keep, key_got
    )
    value_got = exchange(value_send, "seq", 1)
    key_got = exchange(key_send, "seq", 0)

    key_grad, value_grad = key_value_grads(keys, values, after(mine, value_keep))
    grads = (query_grad, key_grad, value_grad)
    input_keep, input_send = input_terms(grads, weights, info, head_order, 0, 1)

    def stage(keep, got, token, bit, axis="seq"):
        keep, send = sums([(keep, after(got, token))])
        return keep, exchange(send, axis, bit)

    def rest(keep, got, bits_left):
        for bit in bits_left:
            keep, got = stage(keep, got, keep, bit)
        return keep[0], got[0]

    value_got, key_got = after((value_got, key_got), input_keep)
    late_keep, late_send = sums([(value_keep, value_got), (key_keep, key_got)], merge=True)
    late_got = exchange(late_send, "seq", 2)
    out_keep, out_got = stage(out_keep, out_got, late_keep, 1)
    input_got = exchange(after(input_send, out_keep), "head", 0)
    for bit in range(1, head_bits):
        input_keep, input_got = stage(input_keep, input_got, out_keep, bit, "head")
    out_keep, out_got = stage(out_keep, out_got, (input_keep, late_got), 2)
    query_keep, query_got = stage(query_keep, query_got, out_keep, 1)
    query_keep, query_send = sums([(query_keep, after(query_got, query_keep))])
    out_got, input_got = after((out_got, input_got), query_keep)
    query_got = after(exchange(query_send, "seq", 2), out_got, input_got)

    out_pair = rest(out_keep, out_got, stages[3:])
    late_pair = rest(late_keep, late_got, stages[3:])
    query_pair = rest(query_keep, query_got, stages[3:])
    input_grad = (input_keep[0].astype(f32) + input_got[0].astype(f32)).astype(bf16)
    out_weight_grad = out_pair[0].astype(f32) + out_pair[1].astype(f32)
    proj_weight_grad = finish(*query_pair, *late_pair)
    return (input_grad, jnp.transpose(proj_weight_grad, (1, 0, 2)), out_weight_grad)


def solution(mesh):
    in_specs = (
        P("seq", None),
        P("seq", None),
        P("seq"),
        P(None, None, "head"),
        P("head", None),
        P("head"),
    )
    out_specs = (P(("seq", "head"), None), P("seq", None, "head"), P("head", "seq"))
    return jax.shard_map(
        per_device, mesh=mesh, in_specs=in_specs, out_specs=out_specs, check_vma=False
    )
```

```python
import functools

import jax
import jax.numpy as jnp
from jax import lax
from jax.experimental import pallas as pl
from jax.experimental.pallas import tpu as pltpu
from jax.sharding import PartitionSpec as P

D = 2048
HD = 128
BLOCK = 1024
epsilon = 1e-06
f32 = jnp.float32
bf16 = jnp.bfloat16
MIB = 1024 * 1024
COST = pl.CostEstimate(flops=1000000, bytes_accessed=1, transcendentals=0)


def params(mib=16):
    return pltpu.CompilerParams(vmem_limit_bytes=mib * MIB)


def dot(a, b):
    return lax.dot_general(a, b, (((1,), (0,)), ((), ())), preferred_element_type=f32)


def dot_t(a, b):
    return lax.dot_general(a, b, (((1,), (1,)), ((), ())), preferred_element_type=f32)


def exchange(arr, axis, bit):
    count = lax.axis_size(axis)
    return lax.ppermute(arr, axis, [(i, i ^ (1 << bit)) for i in range(count)])


def slot_order(stage_bits):
    order = [0]
    for bit in reversed(stage_bits):
        order = order + [slot | (1 << bit) for slot in order]
    return order


def states_kernel(parts, rows_ref, weight_ref, key_ref, value_ref, state_ref, sent_ref, key_t_ref, value_t_ref, copy_ref, held_ref, sems):
    heads = state_ref.shape[0]
    step = copy_ref.shape[0] // parts
    value_copy = pltpu.make_async_copy(weight_ref.at[2], held_ref.at[0], sems.at[0])
    key_copy = pltpu.make_async_copy(weight_ref.at[1], held_ref.at[1], sems.at[1])
    row_copies = []
    for part in range(parts):
        chunk = pl.ds(part * step, step)
        row_copies.append(pltpu.make_async_copy(rows_ref.at[chunk], copy_ref.at[chunk], sems.at[2 + part]))
    value_copy.start()
    for copy in row_copies:
        copy.start()
    key_copy.start()
    value_copy.wait()
    for part in range(parts):
        row_copies[part].wait()
        chunk = slice(part * step, (part + 1) * step)
        value_ref[chunk, :] = dot(copy_ref[chunk, :], held_ref[0]).astype(bf16)
    for h in range(heads):
        columns = slice(h * HD, (h + 1) * HD)
        value_t_ref[columns, :] = value_ref[:, columns].T
    key_copy.wait()
    key_ref[...] = dot(copy_ref[...], held_ref[1]).astype(bf16)
    for h in range(heads):
        columns = slice(h * HD, (h + 1) * HD)
        key_t = key_ref[:, columns].T
        key_t_ref[columns, :] = key_t
        state = dot(key_t, value_ref[:, columns])
        state_ref[h] = state
        sent_ref[h] = state.astype(bf16)


def block_states(rows, weights, parts=4):
    count, depth = rows.shape
    width = weights.shape[2]
    heads = width // HD
    hbm = pl.BlockSpec(memory_space=pltpu.HBM)
    vmem = pl.BlockSpec(memory_space=pltpu.VMEM)
    return pl.pallas_call(
        functools.partial(states_kernel, parts),
        in_specs=[hbm, hbm],
        out_specs=[vmem] * 7,
        out_shape=[
            jax.ShapeDtypeStruct((count, width), bf16),
            jax.ShapeDtypeStruct((count, width), bf16),
            jax.ShapeDtypeStruct((heads, HD, HD), f32),
            jax.ShapeDtypeStruct((heads, HD, HD), bf16),
            jax.ShapeDtypeStruct((width, count), bf16),
            jax.ShapeDtypeStruct((width, count), bf16),
            jax.ShapeDtypeStruct((count, depth), bf16),
        ],
        scratch_shapes=[pltpu.VMEM((2, depth, width), bf16), pltpu.SemaphoreType.DMA((2 + parts,))],
        compiler_params=params(44),
        cost_estimate=COST,
        name="block_states",
    )(rows, weights)


def terms_kernel(number, outputs, position_ref, *refs):
    lefts, right, outs = refs[:number], refs[number], refs[number + 1 :]
    width = outs[0].shape[2]
    jobs = {}
    for out, (left, low, high, slots) in zip(outs, outputs):
        for index, slot in enumerate(slots):
            jobs.setdefault((left, slot), []).append((low, high, out, index))
    for (left, slot), parts in jobs.items():
        start = pl.multiple_of((position_ref[0] ^ slot) * width, width)
        product = dot(lefts[left][...], right[:, pl.ds(start, width)]).astype(bf16)
        for low, high, out, index in parts:
            out[index] = product[low:high]


def gradient_terms(lefts, right, info, outputs):
    count = right.shape[0]
    width = right.shape[1] // lax.axis_size("seq")
    if width % 128:
        blocked = right.reshape(count, -1, width)
        results = []
        for left, low, high, slots in outputs:
            picked = jnp.take(blocked, info[0] ^ jnp.array(slots, jnp.int32), axis=1)
            part = jnp.einsum("at,tnb->nab", lefts[left][low:high], picked, preferred_element_type=f32)
            results.append(part.astype(bf16))
        return results
    shapes = [(len(slots), high - low, width) for _, low, high, slots in outputs]
    size = sum(n * r * w for n, r, w in shapes)
    vmem = pl.BlockSpec(memory_space=pltpu.VMEM)
    return pl.pallas_call(
        functools.partial(terms_kernel, len(lefts), outputs),
        in_specs=[pl.BlockSpec(memory_space=pltpu.SMEM)] + [vmem] * (len(lefts) + 1),
        out_specs=[vmem] * len(outputs),
        out_shape=[jax.ShapeDtypeStruct(shape, bf16) for shape in shapes],
        compiler_params=params(),
        cost_estimate=COST,
        name="gradient_terms",
    )(info, *lefts, right)


def sums_kernel(groups, merge, *refs):
    ins, outs = refs[: 2 * groups], refs[2 * groups :]
    low = 0
    for index in range(groups):
        keep, got = ins[2 * index], ins[2 * index + 1]
        half, rows = keep.shape[0] // 2, keep.shape[1]
        if merge:
            kept, sent = (out.at[:, low : low + rows, :] for out in outs)
            low += rows
        else:
            kept, sent = outs[2 * index], outs[2 * index + 1]
        for slot in range(half):
            kept[slot] = (keep[slot].astype(f32) + got[slot].astype(f32)).astype(bf16)
            other = half + slot
            sent[slot] = (keep[other].astype(f32) + got[other].astype(f32)).astype(bf16)


def sums(pairs, merge=False):
    slots, rows, width = pairs[0][0].shape
    total = sum(keep.shape[1] for keep, _ in pairs) if merge else rows
    shape = jax.ShapeDtypeStruct((slots // 2, total, width), bf16)
    vmem = pl.BlockSpec(memory_space=pltpu.VMEM)
    outs = 2 if merge else 2 * len(pairs)
    size = sum(keep.size for keep, _ in pairs)
    return pl.pallas_call(
        functools.partial(sums_kernel, len(pairs), merge),
        in_specs=[vmem] * (2 * len(pairs)),
        out_specs=[vmem] * outs,
        out_shape=[shape] * outs,
        compiler_params=params(),
        cost_estimate=COST,
        name="sums",
    )(*[array for pair in pairs for array in pair])


def flag(info_ref, bit):
    return ((info_ref[0] >> bit) & 1).astype(f32)


def small(kernel, info, arrays, shapes, name):
    vmem = pl.BlockSpec(memory_space=pltpu.VMEM)
    return pl.pallas_call(
        kernel,
        in_specs=[pl.BlockSpec(memory_space=pltpu.SMEM)] + [vmem] * len(arrays),
        out_specs=[vmem] * len(shapes),
        out_shape=[jax.ShapeDtypeStruct(shape, kind) for shape, kind in shapes],
        compiler_params=params(),
        cost_estimate=COST,
        name=name,
    )(info, *arrays)


def mark_kernel(info_ref, out_ref):
    out_ref[...] = jnp.full(out_ref.shape, flag(info_ref, 0))


def prefix_kernel(bit, info_ref, total_ref, got_ref, *refs):
    got = got_ref[...].astype(f32)
    before = got * flag(info_ref, bit)
    if bit:
        before += refs[0][...]
        refs = refs[1:]
    refs[0][...] = before
    if len(refs) > 1:
        total = total_ref[...] + got
        refs[1][...] = total
        refs[2][...] = total.astype(bf16)


def prefix_step(info, bit, arrays, last):
    shape = arrays[0].shape
    shapes = [(shape, f32)] if last else [(shape, f32), (shape, f32), (shape, bf16)]
    return small(functools.partial(prefix_kernel, bit), info, arrays, shapes, "prefix_step")


def suffix_first_kernel(info_ref, own_ref, got_ref, total_ref, mine_ref, mate_ref, sent_ref):
    upper = flag(info_ref, 0)
    own, got = own_ref[...], got_ref[...].astype(f32)
    total = own + got
    mine = own + got * (1.0 - upper)
    total_ref[...] = total
    mine_ref[...] = mine
    mate_ref[...] = got + own * upper
    sent_ref[0] = total.astype(bf16)
    sent_ref[1] = mine.astype(bf16)


def suffix_first(info, own, got):
    shape = own.shape
    shapes = [(shape, f32), (shape, f32), (shape, f32), ((2,) + shape, bf16)]
    return small(suffix_first_kernel, info, [own, got], shapes, "suffix_first")


def suffix_kernel(bit, inputs, info_ref, *refs):
    arrays, outs = refs[:inputs], refs[inputs:]
    upper = flag(info_ref, bit)
    total = arrays[0][...]
    if bit == 1:
        got = arrays[3][0].astype(f32)
        other = arrays[3][1].astype(f32) + total * upper
        later = got * (1.0 - upper)
    else:
        got = arrays[4][...].astype(f32)
        later = got * (1.0 - upper)
        other = arrays[3][...] + later
    outs[0][...] = arrays[1][...] + later
    outs[1][...] = arrays[2][...] + later
    outs[2][...] = other
    if len(outs) > 3:
        outs[3][...] = total + got
        outs[4][...] = (total + got).astype(bf16)


def suffix_step(info, bit, arrays, last):
    shape = arrays[0].shape
    shapes = [(shape, f32)] * 3 if last else [(shape, f32)] * 4 + [(shape, bf16)]
    return small(functools.partial(suffix_kernel, bit, len(arrays)), info, arrays, shapes, "suffix_step")


def middle_kernel(query_ref, grad_ref, mask_ref, gain_ref, own_ref, before_ref, normed_t_ref, query_grad_ref, query_grad_t_ref, block_grad_ref, sent_ref, held_ref):
    mask_row = mask_ref[...].astype(f32)

    @pl.when(pl.program_id(0) == 0)
    def _():
        held_ref[...] = jnp.broadcast_to(mask_row, held_ref.shape[::-1]).T

    query = query_ref[...]
    state = (before_ref[0] + own_ref[0]).astype(bf16)
    mask = held_ref[...]
    gain = gain_ref[...].astype(f32)
    attended = dot(query, state)
    scale = lax.rsqrt(jnp.mean(attended * attended, -1, keepdims=True) + epsilon)
    unit = attended * scale
    normed_t_ref[...] = (unit * gain * mask).astype(bf16).T
    scaled = grad_ref[...] * mask * gain
    inner = jnp.mean(scaled * attended, -1, keepdims=True)
    attended_grad = (scale * scaled - attended * (scale * scale * scale) * inner).astype(bf16)
    attended_grad_t = attended_grad.T
    block_grad = dot(attended_grad_t, query)
    block_grad_ref[0] = block_grad
    sent_ref[0] = block_grad.astype(bf16)
    query_grad_ref[...] = dot_t(attended_grad, state).astype(bf16)
    query_grad_t_ref[...] = dot(state, attended_grad_t).astype(bf16)


def middle(queries, normed_grad, mask, gain, own, before):
    count, width = queries.shape
    heads = width // HD
    column = pl.BlockSpec((count, HD), lambda h: (0, h))
    row = pl.BlockSpec((HD, count), lambda h: (h, 0))
    square = pl.BlockSpec((1, HD, HD), lambda h: (h, 0, 0))
    return pl.pallas_call(
        middle_kernel,
        grid=(heads,),
        in_specs=[
            column,
            column,
            pl.BlockSpec((1, count), lambda h: (0, 0)),
            pl.BlockSpec((1, HD), lambda h: (0, h)),
            square,
            square,
        ],
        out_specs=[row, column, row, square, square],
        out_shape=[
            jax.ShapeDtypeStruct((width, count), bf16),
            jax.ShapeDtypeStruct((count, width), bf16),
            jax.ShapeDtypeStruct((width, count), bf16),
            jax.ShapeDtypeStruct((heads, HD, HD), f32),
            jax.ShapeDtypeStruct((heads, HD, HD), bf16),
        ],
        scratch_shapes=[pltpu.VMEM((count, HD), f32)],
        compiler_params=params(),
        cost_estimate=pl.CostEstimate(
            flops=64 * count * width * HD, bytes_accessed=1, transcendentals=0
        ),
        name="norm_backward",
    )(queries, normed_grad, mask, gain, own, before)


def late_kernel(mine_ref, mate_ref, other_ref, *refs):
    for side, state_ref, parts in ((0, mate_ref, refs[0:2] + refs[4:6]), (1, other_ref, refs[2:4] + refs[6:8])):
        own, got, keep, send = parts
        half = keep.shape[0]

        def times(state, block):
            return lax.dot_general(state, block, (((side,), (0,)), ((), ())), preferred_element_type=f32)

        for slot in range(2 * half):
            out = keep if slot < half else send
            for h in range(mine_ref.shape[0]):
                rows = slice(h * HD, (h + 1) * HD)
                total = times(mine_ref[h].astype(bf16), own[slot, rows, :])
                total += times(state_ref[h].astype(bf16), got[slot, rows, :])
                out[slot % half, rows, :] = total.astype(bf16)


def late_terms(mine, mate, other, value_keep, value_got, key_keep, key_got):
    slots, rows, width = value_keep.shape
    vmem = pl.BlockSpec(memory_space=pltpu.VMEM)
    shape = jax.ShapeDtypeStruct((slots // 2, rows, width), bf16)
    return pl.pallas_call(
        late_kernel,
        in_specs=[vmem] * 7,
        out_specs=[vmem] * 4,
        out_shape=[shape] * 4,
        compiler_params=params(),
        cost_estimate=COST,
        name="late_terms",
    )(mine, mate, other, value_keep, value_got, key_keep, key_got)


def key_value_kernel(key_ref, value_ref, grad_ref, key_grad_ref, value_grad_ref):
    state_grad = grad_ref[0].astype(bf16)
    key_grad_ref[...] = dot(value_ref[...], state_grad).astype(bf16)
    value_grad_ref[...] = dot_t(key_ref[...], state_grad).astype(bf16)


def key_value_grads(keys, values, state_grad_t):
    count, width = keys.shape
    column = pl.BlockSpec((count, HD), lambda h: (0, h))
    out = jax.ShapeDtypeStruct((count, width), bf16)
    return pl.pallas_call(
        key_value_kernel,
        grid=(width // HD,),
        in_specs=[column, column, pl.BlockSpec((1, HD, HD), lambda h: (h, 0, 0))],
        out_specs=[column, column],
        out_shape=[out, out],
        compiler_params=params(),
        cost_estimate=COST,
        name="key_value_grads",
    )(keys, values, state_grad_t)


def input_kernel(order, place_ref, query_ref, key_ref, value_ref, weight_ref, keep_ref, send_ref, held_ref):
    total = dot_t(query_ref[...], weight_ref[0])
    total += dot_t(key_ref[...], weight_ref[1])
    total += dot_t(value_ref[...], weight_ref[2])
    held_ref[...] = total.astype(bf16).reshape(held_ref.shape)
    half = len(order) // 2
    for index in range(half):
        keep_ref[index] = held_ref[place_ref[1] ^ order[index]]
        send_ref[index] = held_ref[place_ref[1] ^ order[half + index]]


def input_terms(grads, weight, info, order, chunk, chunks, tile=512):
    count, width = grads[0].shape
    half = len(order) // 2
    rows = count // len(order)
    columns = D // chunks
    first = chunk * columns // tile
    full = pl.BlockSpec((count, width), lambda i, b: (0, 0))
    out = pl.BlockSpec((half, rows, tile), lambda i, b: (0, 0, i))
    shape = jax.ShapeDtypeStruct((half, rows, columns), bf16)
    return pl.pallas_call(
        functools.partial(input_kernel, order),
        grid_spec=pltpu.PrefetchScalarGridSpec(
            num_scalar_prefetch=1,
            grid=(columns // tile,),
            in_specs=[full, full, full, pl.BlockSpec((3, tile, width), lambda i, b: (0, first + i, 0))],
            out_specs=[out, out],
            scratch_shapes=[pltpu.VMEM((len(order), rows, tile), bf16)],
        ),
        out_shape=[shape, shape],
        compiler_params=params(20),
        cost_estimate=COST,
        name="input_terms",
    )(info, *grads, weight)


def finish_kernel(query_keep_ref, query_got_ref, late_keep_ref, late_got_ref, out_ref):
    width = query_keep_ref.shape[0]
    out_ref[0] = (query_keep_ref[...].astype(f32) + query_got_ref[...].astype(f32)).T
    for index in range(2):
        rows = slice(index * width, (index + 1) * width)
        out_ref[1 + index] = (late_keep_ref[rows, :].astype(f32) + late_got_ref[rows, :].astype(f32)).T


def finish(query_keep, query_got, late_keep, late_got):
    rows, width = query_keep.shape
    return pl.pallas_call(
        finish_kernel,
        out_shape=jax.ShapeDtypeStruct((3, width, rows), f32),
        compiler_params=params(),
        cost_estimate=COST,
        name="finish",
    )(query_keep, query_got, late_keep, late_got)


def after(value, *others):
    return lax.optimization_barrier((value,) + others)[0]


def per_device(layer_input, output_grad, loss_mask, proj_weight, out_weight, norm_gain):
    count = layer_input.shape[0]
    seq_bits = lax.axis_size("seq").bit_length() - 1
    head_bits = lax.axis_size("head").bit_length() - 1
    stages = list(range(seq_bits))
    order, swapped = slot_order(stages), slot_order([1, 0] + stages[2:])
    half = len(order) // 2
    head_order = slot_order(list(range(head_bits)))
    info = jnp.stack([lax.axis_index("seq"), lax.axis_index("head")]).astype(jnp.int32)
    layer_input, output_grad, loss_mask, proj_weight, norm_gain = after(
        (layer_input, output_grad, loss_mask, proj_weight, norm_gain), info
    )
    weights = jnp.transpose(proj_weight, (1, 0, 2))
    mask = loss_mask.reshape(1, count)

    def project(rows, index):
        return jnp.dot(rows, weights[index], preferred_element_type=f32).astype(bf16)

    def terms(left, right, *parts):
        outputs = [(0, 0, left.shape[0], slots) for slots in parts]
        return gradient_terms([left], right, info, outputs)

    keys, values, own_state, sent, keys_t, values_t, layer_input = block_states(layer_input, weights)

    got = exchange(sent, "seq", 0)
    (value_send,) = terms(values_t, after(layer_input, own_state), order[half:])
    queries = project(after(layer_input, value_send), 0)
    got = after(got, queries)
    before, total, sent = prefix_step(info, 0, [own_state, got], False)
    value_got = exchange(after(value_send, total), "seq", 0)
    for bit in stages[1:]:
        got = exchange(sent, "seq", bit)
        if bit == 1:
            normed_grad = dot_t(after(output_grad, total), out_weight)
            (key_send,) = terms(keys_t, after(layer_input, normed_grad), swapped[half:])
            got = after(got, key_send)
        elif bit == 2:
            (mark,) = small(mark_kernel, after(info, total), [], [((8, 128), f32)], "mark")
            key_got = exchange(after(key_send, mark), "seq", 1)
            got = after(got, mark)
        before, *sums_on = prefix_step(info, bit, [total, got, before], bit == stages[-1])
        if sums_on:
            total, sent = sums_on

    normed_t, query_grad, query_grad_t, own_grad, sent = middle(
        queries, normed_grad, mask, norm_gain[None, :], own_state, before
    )

    got = exchange(sent, "seq", 0)
    out_keep, out_send = terms(normed_t, after(output_grad, own_grad), order[:half], order[half:])
    got = after(got, out_keep, value_got)
    total, mine, mate, sent = suffix_first(info, own_grad, got)
    out_got = exchange(after(out_send, total), "seq", 0)

    got = exchange(sent, "seq", 1)
    query_keep, query_send = terms(query_grad_t, after(layer_input, total), order[:half], order[half:])
    got = after(got, query_keep, key_got)
    mine, mate, other, *sums_on = suffix_step(info, 1, [total, mine, mate, got], False)
    total, sent = sums_on
    query_got = exchange(after(query_send, total), "seq", 0)

    for bit in stages[2:]:
        got = exchange(sent, "seq", bit)
        if bit == 2:
            (value_keep,) = terms(values_t, after(layer_input, total), order[:half])
            (key_keep,) = terms(keys_t, after(layer_input, value_keep), swapped[:half])
            got = after(got, key_keep)
        mine, mate, other, *sums_on = suffix_step(
            info, bit, [total, mine, mate, other, got], bit == stages[-1]
        )
        if sums_on:
            total, sent = sums_on

    value_keep, value_send, key_keep, key_send = late_terms(
        mine, mate, other, value_keep, value_got, key_keep, key_got
    )
    value_got = exchange(value_send, "seq", 1)
    key_got = exchange(key_send, "seq", 0)

    key_grad, value_grad = key_value_grads(keys, values, after(mine, value_keep))
    grads = (query_grad, key_grad, value_grad)
    input_keep, input_send = input_terms(grads, weights, info, head_order, 0, 1)

    def stage(keep, got, token, bit, axis="seq"):
        keep, send = sums([(keep, after(got, token))])
        return keep, exchange(send, axis, bit)

    def rest(keep, got, bits_left):
        for bit in bits_left:
            keep, got = stage(keep, got, keep, bit)
        return keep[0], got[0]

    value_got, key_got = after((value_got, key_got), input_keep)
    late_keep, late_send = sums([(value_keep, value_got), (key_keep, key_got)], merge=True)
    late_got = exchange(late_send, "seq", 2)
    out_keep, out_got = stage(out_keep, out_got, late_keep, 1)
    input_got = exchange(after(input_send, out_keep), "head", 0)
    for bit in range(1, head_bits):
        input_keep, input_got = stage(input_keep, input_got, out_keep, bit, "head")
    out_keep, out_got = stage(out_keep, out_got, (input_keep, late_got), 2)
    query_keep, query_got = stage(query_keep, query_got, out_keep, 1)
    query_keep, query_send = sums([(query_keep, after(query_got, query_keep))])
    out_got, input_got = after((out_got, input_got), query_keep)
    query_got = after(exchange(query_send, "seq", 2), out_got, input_got)

    out_pair = rest(out_keep, out_got, stages[3:])
    late_pair = rest(late_keep, late_got, stages[3:])
    query_pair = rest(query_keep, query_got, stages[3:])
    input_grad = (input_keep[0].astype(f32) + input_got[0].astype(f32)).astype(bf16)
    out_weight_grad = out_pair[0].astype(f32) + out_pair[1].astype(f32)
    proj_weight_grad = finish(*query_pair, *late_pair)
    return (input_grad, jnp.transpose(proj_weight_grad, (1, 0, 2)), out_weight_grad)


def solution(mesh):
    in_specs = (
        P("seq", None),
        P("seq", None),
        P("seq"),
        P(None, None, "head"),
        P("head", None),
        P("head"),
    )
    out_specs = (P(("seq", "head"), None), P("seq", None, "head"), P("head", "seq"))
    return jax.shard_map(
        per_device, mesh=mesh, in_specs=in_specs, out_specs=out_specs, check_vma=False
    )
```
